32 devices in a mesh: dp: 16 (over z, x, core), mp: 2 (over y).
Axes of the slice: x: 2, y: 2, z: 4, core: 2. Of those that a mesh axis runs over, the one named last changes fastest.
Arguments:
- patches: bfloat16 [40960, 512], P(('dp', 'mp')), may hold values from -6 to 6
- cotangent: bfloat16 [40960, 512], P(('dp', 'mp')), may hold values from -6 to 6
- key_count: int32 [80], P('dp'), may hold values from 64 to 512, as said below
- w_qkv: float32 [3, 512, 512], P(None, None, 'mp')
- w_proj: float32 [512, 512], P('mp'), may hold values from -1 to 1
- w_up: float32 [512, 2048], P(None, 'mp')
- w_down: float32 [2048, 512], P('mp'), may hold values from -0.125 to 0.125
- qv_bias: float32 [2, 512], P(None, 'mp'), may hold values from -3 to 3
- up_bias: float32 [2048], P('mp'), may hold values from -3 to 3
- vec_params: float32 [6, 512], replicated
- first_qkv: float32 [3, 512, 512], P(None, None, 'mp'), may hold values from -0.00028163442 to 0.00028163442
- second_qkv: float32 [3, 512, 512], P(None, None, 'mp'), may hold values from 1.6815404e-08 to 6.6627074e-08
- first_proj: float32 [512, 512], P('mp'), may hold values from -0.00028163442 to 0.00028163442
- second_proj: float32 [512, 512], P('mp'), may hold values from 1.6815404e-08 to 6.6627074e-08
- first_up: float32 [512, 2048], P(None, 'mp'), may hold values from -0.00028163442 to 0.00028163442
- second_up: float32 [512, 2048], P(None, 'mp'), may hold values from 1.6815404e-08 to 6.6627074e-08
- first_down: float32 [2048, 512], P('mp'), may hold values from -0.00028163442 to 0.00028163442
- second_down: float32 [2048, 512], P('mp'), may hold values from 1.6815404e-08 to 6.6627074e-08
- first_qv_bias: float32 [2, 512], P(None, 'mp'), may hold values from -0.00056326884 to 0.00056326884
- second_qv_bias: float32 [2, 512], P(None, 'mp'), may hold values from 6.6627074e-08 to 2.665083e-07
- first_up_bias: float32 [2048], P('mp'), may hold values from -0.00056326884 to 0.00056326884
- second_up_bias: float32 [2048], P('mp'), may hold values from 9.518153e-09 to 3.8072614e-08
- first_vec: float32 [6, 512], replicated, may hold values from -0.00056326884 to 0.00056326884
- second_vec: float32 [6, 512], replicated, may hold values from 6.6627074e-08 to 2.665083e-07
Outputs:
- activations: bfloat16 [40960, 512], P(('dp', 'mp'))
- input_grad: float32 [40960, 512], P(('dp', 'mp'))
- grad_norm: float32 [], replicated
- qkv_new: float32 [3, 512, 512], P(None, None, 'mp')
- qkv_first: float32 [3, 512, 512], P(None, None, 'mp')
- qkv_second: float32 [3, 512, 512], P(None, None, 'mp')
- proj_new: float32 [512, 512], P('mp')
- proj_first: float32 [512, 512], P('mp')
- proj_second: float32 [512, 512], P('mp')
- up_new: float32 [512, 2048], P(None, 'mp')
- up_first: float32 [512, 2048], P(None, 'mp')
- up_second: float32 [512, 2048], P(None, 'mp')
- down_new: float32 [2048, 512], P('mp')
- down_first: float32 [2048, 512], P('mp')
- down_second: float32 [2048, 512], P('mp')
- qv_bias_new: float32 [2, 512], P(None, 'mp')
- qv_bias_first: float32 [2, 512], P(None, 'mp')
- qv_bias_second: float32 [2, 512], P(None, 'mp')
- up_bias_new: float32 [2048], P('mp')
- up_bias_first: float32 [2048], P('mp')
- up_bias_second: float32 [2048], P('mp')
- vec_new: float32 [6, 512], replicated
- vec_first: float32 [6, 512], replicated
- vec_second: float32 [6, 512], replicated
The draws below stay inside these ranges and needn't reach their ends.
Inputs may be any that keep to these rules, and one draw needn't show every extreme that they name: `key_count`: each group's count is 512 (a full field) or between 64 and 512 // 4 (a small field padded); group 0 is full.
All inputs are finite; a program needn't handle non-finite values.
Results may differ from the reference program's by a relative error of at most 0.025.
Values may be sent and summed in bfloat16 or wider, within the bound.
A program may use at most 256 MiB of HBM per device.

```python
import math
import jax
import jax.numpy as jnp
from jax import lax

D = 512
HEADS = 16
HD = 32
FF = 2048
L = 512
ADAM_STEP = 10
SEQS = 80
TOKENS = 40960
NPARAM = 3151872


def draw_key_count(key, part):
    kind_key, size_key = jax.random.split(key)
    full_field = jax.random.randint(kind_key, (SEQS,), 0, 2)
    full_field = full_field.at[0].set(1)
    reduced = jax.random.randint(size_key, (SEQS,), L // 8, L // 4 + 1)
    return jnp.where(full_field == 1, L, reduced).astype(jnp.int32)


def draw_w_qkv(key, part):
    values = jax.random.normal(key, (3, D, D), jnp.float32)
    column = jnp.arange(D, dtype=jnp.float32) / D
    slab = jnp.arange(3)[:, None, None]
    ramped = jnp.where(slab == 2, 0.5 + column[None, None, :], 1.0)
    return values * ramped * D ** (-0.5)


def draw_w_up(key, part):
    values = jax.random.normal(key, (D, FF), jnp.float32)
    column = jnp.arange(FF, dtype=jnp.float32) / FF
    return values * (0.5 + column[None, :]) * D ** (-0.5)


def draw_vec_params(key, part):
    values = jax.random.normal(key, (6, D), jnp.float32)
    row_index = jnp.arange(6)[:, None]
    gain_rows = (row_index == 0) | (row_index == 2)
    return jnp.where(gain_rows, 1.0 + 0.15 * values, 0.3 * values)


def shard_levels(rng, extent, cuts, least, high):
    level, own = 1.0, jax.random.fold_in(rng, 6)
    for dim, shards_of in cuts:
        heights = jnp.exp(jax.random.uniform(jax.random.fold_in(own, dim), (shards_of,), jnp.float32, least / len(cuts), high / len(cuts)))
        level = level * jnp.repeat(heights, extent[dim] // shards_of).reshape([-1 if axis == dim else 1 for axis in range(len(extent))])
    return level


def scatter_about(rng, dims, deviation, limit, pieces=(), held_as=jnp.bfloat16):
    gain = shard_levels(rng, dims, pieces, -0.22, 0.18) if pieces else 1.0
    drawn = jax.random.normal(rng, dims, jnp.float32) * deviation * gain
    return jnp.minimum(jnp.maximum(drawn, -limit), limit).astype(held_as)


def setup_inputs(seed: int = 0) -> dict:
    streams_of = jax.random.split(jax.random.key(seed), 25)
    return {
        "patches": scatter_about(streams_of[0], (TOKENS, D), 1.0, 6.0, ((0, 32),)),
        "cotangent": scatter_about(streams_of[1], (TOKENS, D), 1.0, 6.0, ((0, 32),)),
        "key_count": draw_key_count(jax.random.fold_in(streams_of[24], 71), 0),
        "w_qkv": draw_w_qkv(jax.random.fold_in(streams_of[24], 71), 0),
        "w_proj": scatter_about(streams_of[4], (D, D), (D // 16) ** -0.5, 1.0, ((0, 2),), jnp.float32),
        "w_up": draw_w_up(jax.random.fold_in(streams_of[24], 71), 0),
        "w_down": scatter_about(streams_of[6], (FF, D), FF ** -0.5, 0.125, ((0, 2),), jnp.float32),
        "qv_bias": scatter_about(streams_of[7], (2, D), 0.5, 3.0, ((1, 2),), jnp.float32),
        "up_bias": scatter_about(streams_of[8], (FF,), 0.5, 3.0, ((0, 2),), jnp.float32),
        "vec_params": draw_vec_params(jax.random.fold_in(streams_of[24], 71), 0),
        "first_qkv": scatter_about(streams_of[10], (3, D, D), (0.11 * NPARAM ** -0.5), 0.00028163442, ((2, 2),), jnp.float32),
        "second_qkv": jnp.clip(jnp.exp(math.log(6.662707363602749e-08) - 1.37681562 * jax.random.uniform(streams_of[11], (3, D, D), jnp.float32) ** shard_levels(streams_of[11], (3, D, D), ((2, 2),), -0.2, 0.2)), 1.6815404180192672e-08, 6.662707363602749e-08),
        "first_proj": scatter_about(streams_of[12], (D, D), (0.11 * NPARAM ** -0.5), 0.00028163442, ((0, 2),), jnp.float32),
        "second_proj": jnp.clip(jnp.exp(math.log(6.662707363602749e-08) - 1.37681562 * jax.random.uniform(streams_of[13], (D, D), jnp.float32) ** shard_levels(streams_of[13], (D, D), ((0, 2),), -0.2, 0.2)), 1.6815404180192672e-08, 6.662707363602749e-08),
        "first_up": scatter_about(streams_of[14], (D, FF), (0.11 * NPARAM ** -0.5), 0.00028163442, ((1, 2),), jnp.float32),
        "second_up": jnp.clip(jnp.exp(math.log(6.662707363602749e-08) - 1.37681562 * jax.random.uniform(streams_of[15], (D, FF), jnp.float32) ** shard_levels(streams_of[15], (D, FF), ((1, 2),), -0.2, 0.2)), 1.6815404180192672e-08, 6.662707363602749e-08),
        "first_down": scatter_about(streams_of[16], (FF, D), (0.11 * NPARAM ** -0.5), 0.00028163442, ((0, 2),), jnp.float32),
        "second_down": jnp.clip(jnp.exp(math.log(6.662707363602749e-08) - 1.37681562 * jax.random.uniform(streams_of[17], (FF, D), jnp.float32) ** shard_levels(streams_of[17], (FF, D), ((0, 2),), -0.2, 0.2)), 1.6815404180192672e-08, 6.662707363602749e-08),
        "first_qv_bias": scatter_about(streams_of[18], (2, D), (0.22 * NPARAM ** -0.5), 0.00056326884, ((1, 2),), jnp.float32),
        "second_qv_bias": jnp.clip(jnp.exp(math.log(2.6650829454410996e-07) - 1.3862944 * jax.random.uniform(streams_of[19], (2, D), jnp.float32) ** shard_levels(streams_of[19], (2, D), ((1, 2),), -0.2, 0.2)), 6.662707363602749e-08, 2.6650829454410996e-07),
        "first_up_bias": scatter_about(streams_of[20], (FF,), (0.22 * NPARAM ** -0.5), 0.00056326884, ((0, 2),), jnp.float32),
        "second_up_bias": jnp.clip(jnp.exp(math.log(3.807261350630142e-08) - 1.3862944 * jax.random.uniform(streams_of[21], (FF,), jnp.float32) ** shard_levels(streams_of[21], (FF,), ((0, 2),), -0.2, 0.2)), 9.518153376575356e-09, 3.807261350630142e-08),
        "first_vec": scatter_about(streams_of[22], (6, D), (0.22 * NPARAM ** -0.5), 0.00056326884, (), jnp.float32),
        "second_vec": jnp.clip(jnp.exp(jax.random.uniform(streams_of[23], (6, D), jnp.float32, math.log(6.662707363602749e-08), math.log(2.6650829454410996e-07))), 6.662707363602749e-08, 2.6650829454410996e-07),
    }


NORM_EPS = 1e-06
BETA_FIRST = 0.9
BETA_SECOND = 0.95
ADAM_EPS = 1e-08
DECAY_RATE = 0.05
MATRIX_RATE = 0.1
VECTOR_RATE = 0.8
CLIP_NORM = 1.0
MASK_FILL = -1e+30

@jax.custom_vjp
def low(v):
    return lax.optimization_barrier(v.astype(jnp.bfloat16)).astype(jnp.float32)

@jax.custom_vjp
def low_back(v):
    return v

def low_keep(v):
    return (low(v), None)

def low_pass(kept, grad):
    return (grad,)

def back_keep(v):
    return (v, None)

def back_low(kept, grad):
    return (low(grad),)
low.defvjp(low_keep, low_pass)
low_back.defvjp(back_keep, back_low)

def layer_norm(values, norm_gain, norm_shift):
    row_mean = lax.optimization_barrier(jnp.mean(values, axis=-1, keepdims=True))
    centred = values - row_mean
    inverse = lax.rsqrt(lax.optimization_barrier(jnp.mean(centred * centred, axis=-1, keepdims=True)) + NORM_EPS)
    return centred * inverse * norm_gain + norm_shift

def product(left, right):
    return jnp.dot(left, right, precision=lax.Precision.HIGHEST)

def attend(group):
    queries, key_rows, value_rows, count_one = group
    query_heads = queries.reshape(L, HEADS, HD)
    key_heads = key_rows.reshape(L, HEADS, HD)
    value_heads = value_rows.reshape(L, HEADS, HD)
    raw_scores = low_back(jnp.einsum('qhd,khd->hqk', query_heads, key_heads, precision=lax.Precision.HIGHEST))
    visible = lax.iota(jnp.int32, L) < count_one
    scores = jnp.where(visible[None, None, :], raw_scores * HD ** (-0.5), MASK_FILL)
    probs = low(jax.nn.softmax(scores, axis=-1))
    mixed = jnp.einsum('hqk,khd->qhd', probs, value_heads, precision=lax.Precision.HIGHEST).reshape(L, D)
    return low(low_back(mixed))

def forward(patch_rows, w_qkv, w_proj, w_up, w_down, qv_bias, up_bias, vec_params, key_count):
    norm_one = low(layer_norm(patch_rows, vec_params[0], vec_params[1]))
    qkv_low = low(w_qkv)
    queries = low(low_back(product(norm_one, qkv_low[0]) + qv_bias[0]))
    key_rows = low(low_back(product(norm_one, qkv_low[1])))
    value_rows = low(low_back(product(norm_one, qkv_low[2]) + qv_bias[1]))
    seq_total = patch_rows.shape[0] // L
    mixed = lax.map(jax.checkpoint(attend), (queries.reshape(seq_total, L, D), key_rows.reshape(seq_total, L, D), value_rows.reshape(seq_total, L, D), key_count))
    branch = low_back(product(mixed.reshape(-1, D), low(w_proj)) + vec_params[4])
    resid = patch_rows + branch
    norm_two = low(layer_norm(resid, vec_params[2], vec_params[3]))
    up_pre = low_back(product(norm_two, low(w_up)) + up_bias)
    hidden = low(jax.nn.gelu(up_pre, approximate=False))
    down_out = low_back(product(hidden, low(w_down)) + vec_params[5])
    return resid + down_out

def adam_update(weight, gradient, moment_one, moment_two, step_rate, decay_rate):
    first_new = BETA_FIRST * moment_one + (1.0 - BETA_FIRST) * gradient
    second_new = BETA_SECOND * moment_two + (1.0 - BETA_SECOND) * gradient * gradient
    first_hat = first_new / (1.0 - BETA_FIRST ** ADAM_STEP)
    second_hat = second_new / (1.0 - BETA_SECOND ** ADAM_STEP)
    weight_new = weight - step_rate * (first_hat / (jnp.sqrt(second_hat) + ADAM_EPS) + decay_rate * weight)
    return (weight_new, first_new, second_new)

def reference(patches, cotangent, key_count, w_qkv, w_proj, w_up, w_down, qv_bias, up_bias, vec_params, first_qkv, second_qkv, first_proj, second_proj, first_up, second_up, first_down, second_down, first_qv_bias, second_qv_bias, first_up_bias, second_up_bias, first_vec, second_vec):

    def run(patch_rows, *weights):
        return forward(patch_rows, *weights, key_count)
    block_out, pull_back = jax.vjp(run, patches.astype(jnp.float32), w_qkv, w_proj, w_up, w_down, qv_bias, up_bias, vec_params)
    grads = pull_back(cotangent.astype(jnp.float32))
    input_grad = grads[0]
    total = jnp.float32(0.0)
    for gradient in grads[1:]:
        total = total + jnp.sum(gradient * gradient)
    grad_norm = jnp.sqrt(total)
    factor = jnp.minimum(1.0, CLIP_NORM / (grad_norm + 1e-06))
    qkv_new, qkv_first, qkv_second = adam_update(w_qkv, grads[1] * factor, first_qkv, second_qkv, MATRIX_RATE, DECAY_RATE)
    proj_new, proj_first, proj_second = adam_update(w_proj, grads[2] * factor, first_proj, second_proj, MATRIX_RATE, DECAY_RATE)
    up_new, up_first, up_second = adam_update(w_up, grads[3] * factor, first_up, second_up, MATRIX_RATE, DECAY_RATE)
    down_new, down_first, down_second = adam_update(w_down, grads[4] * factor, first_down, second_down, MATRIX_RATE, DECAY_RATE)
    qvb_new, qvb_first, qvb_second = adam_update(qv_bias, grads[5] * factor, first_qv_bias, second_qv_bias, VECTOR_RATE, 0.0)
    upb_new, upb_first, upb_second = adam_update(up_bias, grads[6] * factor, first_up_bias, second_up_bias, VECTOR_RATE, 0.0)
    vec_new, vec_first, vec_second = adam_update(vec_params, grads[7] * factor, first_vec, second_vec, VECTOR_RATE, 0.0)
    return (block_out.astype(jnp.bfloat16), input_grad, grad_norm, qkv_new, qkv_first, qkv_second, proj_new, proj_first, proj_second, up_new, up_first, up_second, down_new, down_first, down_second, qvb_new, qvb_first, qvb_second, upb_new, upb_first, upb_second, vec_new, vec_first, vec_second)
```

```python
import jax
import jax.numpy as jnp
from jax import lax
from jax.experimental import pallas as pl
from jax.experimental.pallas import tpu as pltpu
from jax.sharding import PartitionSpec as P

HD = 32
ADAM_STEP = 10


NORM_EPS = 1e-06
BETA_FIRST = 0.9
BETA_SECOND = 0.95
ADAM_EPS = 1e-08
DECAY_RATE = 0.05
MATRIX_RATE = 0.1
VECTOR_RATE = 0.8
CLIP_NORM = 1.0
MASK_FILL = -1e30
LOG2E = 1.4426950408889634
BF = jnp.bfloat16
F32 = jnp.float32
MESH = pl.DeviceIdType.MESH
SEQ = 512
HALF = 256
VMEM_LIMIT = 58 * 1024 * 1024


def mm_nn(left, right):
    return lax.dot_general(left, right, (((1,), (0,)), ((), ())), preferred_element_type=F32)


def mm_nt(left, right):
    return lax.dot_general(left, right, (((1,), (1,)), ((), ())), preferred_element_type=F32)


def mm_tn(left, right):
    return lax.dot_general(left, right, (((0,), (0,)), ((), ())), preferred_element_type=F32)


def partners(dp):
    core = dp + 1 - 2 * lax.rem(dp, 2)
    x_side = dp + 2 - 4 * lax.rem(lax.div(dp, 2), 2)
    z_near = dp + 4 - 8 * lax.rem(lax.div(dp, 4), 2)
    z_far = dp + 8 - 16 * lax.rem(lax.div(dp, 8), 2)
    return core, x_side, z_near, z_far


def greet(targets):
    barrier = pltpu.get_barrier_semaphore()
    for target in targets:
        pl.semaphore_signal(barrier, inc=1, device_id=target, device_id_type=MESH)
    pl.semaphore_wait(barrier, len(targets))


def full_spec(shape):
    return pl.BlockSpec(shape, lambda *_: (0,) * len(shape))


def sds(shape, dtype):
    return jax.ShapeDtypeStruct(shape, dtype)


def row_block(index, mp):
    return pl.multiple_of(lax.rem(index + 4 * (1 - mp), 5) * HALF, HALF)


def ext_cols(index):
    return pl.multiple_of(jnp.where(index == 0, 0, HALF + HALF * index), HALF)


def norm_forward(values, norm_gain, norm_shift):
    row_mean = jnp.mean(values, axis=-1, keepdims=True)
    centred = values - row_mean
    inverse = lax.rsqrt(jnp.mean(centred * centred, axis=-1, keepdims=True) + NORM_EPS)
    normed = centred * inverse
    return (normed * norm_gain + norm_shift, normed, inverse)


def norm_backward(grad_rows, normed, inverse, norm_gain):
    scaled = grad_rows * norm_gain
    centre_term = jnp.mean(scaled, axis=-1, keepdims=True)
    slope_term = jnp.mean(scaled * normed, axis=-1, keepdims=True)
    return inverse * (scaled - centre_term - normed * slope_term)


def exact_gelu(values):
    return jax.nn.gelu(values, approximate=False)


def key_mask(key_count, length):
    position = lax.broadcasted_iota(jnp.int32, (1, 1, 1, length), 3)
    return position < key_count[:, None, None, None]


def masked_scores(queries, key_rows, key_count):
    raw_scores = jnp.einsum(
        "sqhe,skhe->shqk", queries, key_rows, preferred_element_type=jnp.float32
    )
    scaled = raw_scores * queries.shape[-1] ** (-0.5)
    return jnp.where(key_mask(key_count, key_rows.shape[1]), scaled, MASK_FILL)


def attend_backward(queries, key_rows, value_rows, key_count, log_total, attended_grad):
    scores = masked_scores(queries, key_rows, key_count)
    probs = jnp.exp(scores - log_total)
    probs_low = probs.astype(jnp.bfloat16)
    probs_grad = jnp.einsum(
        "sqhe,skhe->shqk", attended_grad, value_rows, preferred_element_type=jnp.float32
    )
    score_grad = probs * (probs_grad - jnp.sum(probs_grad * probs, axis=-1, keepdims=True))
    visible = key_mask(key_count, key_rows.shape[1])
    raw_grad = jnp.where(visible, score_grad * queries.shape[-1] ** (-0.5), 0.0).astype(
        jnp.bfloat16
    )
    query_grad = jnp.einsum(
        "shqk,skhe->sqhe", raw_grad, key_rows, preferred_element_type=jnp.float32
    )
    key_grad = jnp.einsum("shqk,sqhe->skhe", raw_grad, queries, preferred_element_type=jnp.float32)
    value_grad = jnp.einsum(
        "shqk,sqhe->skhe", probs_low, attended_grad, preferred_element_type=jnp.float32
    )
    return jnp.stack([query_grad, key_grad, value_grad])


def own_slice(values, own_start, own_rows):
    return lax.dynamic_slice_in_dim(values, own_start, own_rows, 0)


def contract_rows(left, right):
    return lax.dot_general(
        left, right, (((0,), (0,)), ((), ())), preferred_element_type=jnp.float32
    )


def contract_cols(left, right):
    return lax.dot_general(
        left, right, (((1,), (1,)), ((), ())), preferred_element_type=jnp.float32
    )


def adam_update(weight, gradient, moment_one, moment_two, step_rate, decay_rate):
    first_new = BETA_FIRST * moment_one + (1.0 - BETA_FIRST) * gradient
    second_new = BETA_SECOND * moment_two + (1.0 - BETA_SECOND) * gradient * gradient
    first_hat = first_new / (1.0 - BETA_FIRST**ADAM_STEP)
    second_hat = second_new / (1.0 - BETA_SECOND**ADAM_STEP)
    weight_new = weight - step_rate * (
        first_hat / (jnp.sqrt(second_hat) + ADAM_EPS) + decay_rate * weight
    )
    return (weight_new, first_new, second_new)


def local(
    patches,
    cotangent,
    key_count,
    w_qkv,
    w_proj,
    w_up,
    w_down,
    qv_bias,
    up_bias,
    vec_params,
    first_qkv,
    second_qkv,
    first_proj,
    second_proj,
    first_up,
    second_up,
    first_down,
    second_down,
    first_qv_bias,
    second_qv_bias,
    first_up_bias,
    second_up_bias,
    first_vec,
    second_vec,
):
    own_rows = patches.shape[0]
    seq_count = key_count.shape[0]
    own_start = lax.axis_index("mp") * own_rows
    local_width = w_proj.shape[0]
    local_heads = local_width // HD
    own_grad = cotangent.astype(jnp.float32)
    qkv_low = w_qkv.astype(jnp.bfloat16)
    proj_low = w_proj.astype(jnp.bfloat16)
    up_low = w_up.astype(jnp.bfloat16)
    down_low = w_down.astype(jnp.bfloat16)
    gain_one, shift_one = (vec_params[0], vec_params[1])
    gain_two, shift_two = (vec_params[2], vec_params[3])
    proj_shift, down_shift = (vec_params[4], vec_params[5])
    qkv_shift = jnp.stack([qv_bias[0], jnp.zeros_like(qv_bias[0]), qv_bias[1]])[:, None, :]
    gathered, grad_all = (
        lax.all_gather(patches, "mp", axis=0, tiled=True),
        lax.all_gather(cotangent, "mp", axis=0, tiled=True),
    )
    whole_rows = gathered.astype(jnp.float32)
    normed_all, unit_one, inverse_one = norm_forward(whole_rows, gain_one, shift_one)
    norm_one = normed_all.astype(jnp.bfloat16)
    projected = (
        jnp.einsum("td,cde->cte", norm_one, qkv_low, preferred_element_type=jnp.float32) + qkv_shift
    )
    shaped = projected.astype(jnp.bfloat16).reshape(3, seq_count, -1, local_heads, HD)
    queries, key_rows, value_rows = (shaped[0], shaped[1], shaped[2])
    scores = masked_scores(queries, key_rows, key_count)
    top_score = jnp.max(scores, axis=-1, keepdims=True)
    log_total = top_score + jnp.log(jnp.sum(jnp.exp(scores - top_score), axis=-1, keepdims=True))
    probs_low = jnp.exp(scores - log_total).astype(jnp.bfloat16)
    attended = jnp.einsum(
        "shqk,skhe->sqhe", probs_low, value_rows, preferred_element_type=jnp.float32
    )
    attended_low = attended.astype(jnp.bfloat16).reshape(-1, local_width)
    proj_part = jnp.dot(attended_low, proj_low, preferred_element_type=jnp.float32)
    resid_all = whole_rows + lax.psum(proj_part, "mp") + proj_shift
    mid_all, unit_two, inverse_two = norm_forward(resid_all, gain_two, shift_two)
    norm_two = mid_all.astype(jnp.bfloat16)
    up_pre = jnp.dot(norm_two, up_low, preferred_element_type=jnp.float32) + up_bias
    hidden_full, gelu_pull = jax.vjp(exact_gelu, up_pre)
    hidden_low = hidden_full.astype(jnp.bfloat16)
    down_part = jnp.dot(hidden_low, down_low, preferred_element_type=jnp.float32)
    out_all = (
        resid_all + lax.psum(down_part.astype(jnp.bfloat16), "mp").astype(jnp.float32) + down_shift
    )
    block_out = own_slice(out_all, own_start, own_rows)
    activations = block_out.astype(jnp.bfloat16)
    down_grad = contract_rows(hidden_low, grad_all)
    hidden_grad = contract_cols(grad_all, down_low)
    up_grad_rows = gelu_pull(hidden_grad)[0].astype(jnp.bfloat16)
    up_grad = contract_rows(norm_two, up_grad_rows)
    up_bias_grad = jnp.sum(up_grad_rows.astype(jnp.float32), axis=0)
    mid_part = contract_cols(up_grad_rows, up_low)
    mid_all_grad = lax.psum(mid_part.astype(jnp.bfloat16), "mp").astype(jnp.float32)
    resid_all_grad = grad_all.astype(jnp.float32) + norm_backward(
        mid_all_grad, unit_two, inverse_two, gain_two
    )
    branch_low = resid_all_grad.astype(jnp.bfloat16)
    own_branch = own_slice(branch_low, own_start, own_rows)
    mid_grad = own_slice(mid_all_grad, own_start, own_rows)
    mid_unit = own_slice(unit_two, own_start, own_rows)
    proj_grad = contract_rows(attended_low, branch_low)
    attended_grad = (
        contract_cols(branch_low, proj_low)
        .astype(jnp.bfloat16)
        .reshape(seq_count, -1, local_heads, HD)
    )
    qkv_grads = attend_backward(queries, key_rows, value_rows, key_count, log_total, attended_grad)
    qkv_grad_rows = qkv_grads.reshape(3, -1, local_width).astype(jnp.bfloat16)
    qkv_grad = jnp.einsum(
        "td,cte->cde", norm_one, qkv_grad_rows, preferred_element_type=jnp.float32
    )
    qkv_grad_sums = jnp.sum(qkv_grad_rows.astype(jnp.float32), axis=1)
    qv_bias_grad = jnp.stack([qkv_grad_sums[0], qkv_grad_sums[2]])
    first_part = jnp.einsum(
        "cte,cde->td", qkv_grad_rows, qkv_low, preferred_element_type=jnp.float32
    )
    first_all = lax.psum(first_part.astype(jnp.bfloat16), "mp").astype(jnp.float32)
    input_all = resid_all_grad + norm_backward(first_all, unit_one, inverse_one, gain_one)
    input_grad = own_slice(input_all, own_start, own_rows)
    own_first_grad = own_slice(first_all, own_start, own_rows)
    own_unit_one = own_slice(unit_one, own_start, own_rows)
    vec_grad = jnp.stack(
        [
            jnp.sum(own_first_grad * own_unit_one, axis=0),
            jnp.sum(own_first_grad, axis=0),
            jnp.sum(mid_grad * mid_unit, axis=0),
            jnp.sum(mid_grad, axis=0),
            jnp.sum(own_branch.astype(jnp.float32), axis=0),
            jnp.sum(own_grad, axis=0),
        ]
    )
    summed = (
        lax.psum(qkv_grad.astype(jnp.bfloat16), "dp").astype(jnp.float32),
        lax.psum(proj_grad.astype(jnp.bfloat16), "dp").astype(jnp.float32),
        lax.psum(up_grad.astype(jnp.bfloat16), "dp").astype(jnp.float32),
        lax.psum(down_grad.astype(jnp.bfloat16), "dp").astype(jnp.float32),
        lax.psum(qv_bias_grad.astype(jnp.bfloat16), "dp").astype(jnp.float32),
        lax.psum(up_bias_grad.astype(jnp.bfloat16), "dp").astype(jnp.float32),
        lax.psum(vec_grad.astype(jnp.bfloat16), "dp").astype(jnp.float32),
    )
    split_square = jnp.float32(0.0)
    for gradient in summed[:6]:
        split_square = split_square + jnp.sum(gradient * gradient)
    vec_total, split_total = lax.psum((summed[6], split_square), "mp")
    grad_norm = jnp.sqrt(split_total + jnp.sum(vec_total * vec_total))
    factor = jnp.minimum(1.0, CLIP_NORM / (grad_norm + 1e-06))
    qkv_new, qkv_first, qkv_second = adam_update(
        w_qkv, summed[0] * factor, first_qkv, second_qkv, MATRIX_RATE, DECAY_RATE
    )
    proj_new, proj_first, proj_second = adam_update(
        w_proj, summed[1] * factor, first_proj, second_proj, MATRIX_RATE, DECAY_RATE
    )
    up_new, up_first, up_second = adam_update(
        w_up, summed[2] * factor, first_up, second_up, MATRIX_RATE, DECAY_RATE
    )
    down_new, down_first, down_second = adam_update(
        w_down, summed[3] * factor, first_down, second_down, MATRIX_RATE, DECAY_RATE
    )
    qvb_new, qvb_first, qvb_second = adam_update(
        qv_bias, summed[4] * factor, first_qv_bias, second_qv_bias, VECTOR_RATE, 0.0
    )
    upb_new, upb_first, upb_second = adam_update(
        up_bias, summed[5] * factor, first_up_bias, second_up_bias, VECTOR_RATE, 0.0
    )
    vec_new, vec_first, vec_second = adam_update(
        vec_params, vec_total * factor, first_vec, second_vec, VECTOR_RATE, 0.0
    )
    return (
        activations,
        input_grad,
        grad_norm,
        qkv_new,
        qkv_first,
        qkv_second,
        proj_new,
        proj_first,
        proj_second,
        up_new,
        up_first,
        up_second,
        down_new,
        down_first,
        down_second,
        qvb_new,
        qvb_first,
        qvb_second,
        upb_new,
        upb_first,
        upb_second,
        vec_new,
        vec_first,
        vec_second,
    )


def gather_kernel(
    qkv_ref, proj_ref, up_ref, down_ref, small_ref, rows_ref,
    wt_ref, wp_ref, wu_ref, wd_ref, sm_ref, other_ref,
    send_sem, recv_sem,
):
    dp, mp = lax.axis_index("dp"), lax.axis_index("mp")
    peer = 1 - mp
    core, x_side, _, _ = partners(dp)
    quarter = lax.rem(dp, 4)
    x_quarter = lax.rem(quarter + 2, 4)
    greet([{"mp": peer}, {"dp": core}, {"dp": x_side}])

    full = [wt_ref, wp_ref, wu_ref, wd_ref]

    def piece(ref, side, part):
        rows = ref.shape[-2] // 4
        where = pl.ds(pl.multiple_of(part * rows, rows), rows)
        return ref.at[side, :, where, :] if len(ref.shape) == 4 else ref.at[side, where, :]

    def send(src, dst, index, target):
        copy = pltpu.make_async_remote_copy(
            src_ref=src, dst_ref=dst, send_sem=send_sem.at[index], recv_sem=recv_sem.at[index],
            device_id=target, device_id_type=MESH,
        )
        copy.start()
        return copy

    copies = []
    own = pl.multiple_of((1 - mp) * 4 * HALF, HALF)
    copies.append(send(rows_ref.at[pl.ds(own, HALF), :], other_ref, 0, {"mp": peer}))
    sm_ref[mp] = small_ref[...]
    copies.append(send(sm_ref.at[mp], sm_ref.at[mp], 1, {"mp": peer}))
    first = []
    for index in range(4):
        if index == 0:
            for part in range(3):
                wt_ref[mp, part] = qkv_ref[part].T.astype(BF)
        else:
            full[index][mp] = (None, proj_ref, up_ref, down_ref)[index][...].astype(BF)
        src = piece(full[index], mp, quarter)
        first.append(send(src, src, 2 + index, {"mp": peer}))
    second, third = [], []
    for index in range(4):
        first[index].wait_recv()
        src = piece(full[index], peer, quarter)
        second.append(send(src, src, 6 + index, {"dp": x_side}))
        third.append(send(src, src, 10 + index, {"dp": core}))
    for index in range(4):
        second[index].wait_recv()
        src = piece(full[index], peer, x_quarter)
        third.append(send(src, src, 14 + index, {"dp": core}))
    for copy in copies + third:
        copy.wait_recv()
    for copy in copies + first + second + third:
        copy.wait_send()


def gather_weights(w_qkv, w_proj, w_up, w_down, small, patches):
    vmem = pl.BlockSpec(memory_space=pltpu.VMEM)
    return pl.pallas_call(
        gather_kernel,
        out_shape=[
            sds((2, 3, 256, 512), BF), sds((2, 256, 512), BF), sds((2, 512, 1024), BF),
            sds((2, 1024, 512), BF), sds((2, 8, 1024), F32), sds((HALF, 512), BF),
        ],
        in_specs=[vmem] * 6,
        out_specs=[vmem] * 6,
        scratch_shapes=[pltpu.SemaphoreType.DMA((18,)), pltpu.SemaphoreType.DMA((18,))],
        compiler_params=pltpu.CompilerParams(
            collective_id=0, has_side_effects=True, vmem_limit_bytes=VMEM_LIMIT
        ),
        name="gather_weights",
    )(w_qkv, w_proj, w_up, w_down, small, patches)


def layer_norm_rows(rows, gain, shift):
    centred = rows - jnp.mean(rows, axis=-1, keepdims=True)
    inverse = lax.rsqrt(jnp.mean(centred * centred, axis=-1, keepdims=True) + NORM_EPS)
    unit = centred * inverse
    return unit * gain + shift, unit, inverse


def layer_norm_back(grad, unit, inverse, gain):
    scaled = grad * gain
    centre = jnp.mean(scaled, axis=-1, keepdims=True)
    slope = jnp.mean(scaled * unit, axis=-1, keepdims=True)
    return inverse * (scaled - centre - unit * slope)


def head_rows(block, sub):
    return pl.ds(pl.multiple_of(block * 128 + sub * HD, HD), HD)


def head_cols(block):
    return pl.ds(pl.multiple_of(block * 128, 128), 128)


def key_bias(shape, mp, count, shared):
    slot = lax.broadcasted_iota(jnp.int32, shape, 0)
    if shared:
        slot = lax.rem(slot + HALF * mp, SEQ)
    return jnp.where(slot < count, 0.0, MASK_FILL).astype(BF)


def widen(rows, sub):
    zeros = jnp.zeros_like(rows)
    row = lax.broadcasted_iota(jnp.int32, rows.shape, 0)
    ones = jnp.where(row == 0, 1.0, 0.0).astype(BF)
    parts = [zeros] * 4
    parts[sub] = rows
    parts[(sub + 1) % 4] = ones
    return jnp.concatenate(parts, axis=0)


def widen_plain(rows, sub):
    parts = [jnp.zeros_like(rows)] * 4
    parts[sub] = rows
    return jnp.concatenate(parts, axis=0)


def score_tile(key_block, bias, query_rows, sub):
    lane = lax.broadcasted_iota(jnp.int32, key_block.shape, 1)
    keys = jnp.where(lane // HD == (sub + 1) % 4, bias, key_block)
    return mm_nn(keys, widen(query_rows, sub))


def attend_kernel(
    count_ref, x_ref, other_ref, wt_ref, vec_ref, small_ref,
    nt_ref, qt_ref, kt_ref, k_ref, v_ref, ot_ref, lse_ref,
    vt_ref, bias_ref, s_ref,
):
    group = pl.program_id(0)
    mp = lax.axis_index("mp")
    gain, shift = vec_ref[0:1, :], vec_ref[1:2, :]

    def as_column(row):
        return jnp.broadcast_to(row, (8, row.shape[1])).T[:, 0:1]

    def project(norm, base):
        width = norm.shape[0]
        at = slice(base, base + width)
        nt_ref[:, at] = norm.T
        for side in range(2):
            own = slice(side * 256, side * 256 + 256)
            q_bias, v_bias = small_ref[side, 1:2, 0:256], small_ref[side, 2:3, 0:256]
            scale = LOG2E * HD ** (-0.5)
            qt_ref[own, at] = ((mm_nt(wt_ref[side, 0], norm) + as_column(q_bias)) * scale).astype(BF)
            kt_ref[own, at] = mm_nt(wt_ref[side, 1], norm).astype(BF)
            vt_ref[own, at] = (mm_nt(wt_ref[side, 2], norm) + as_column(v_bias)).astype(BF)
            k_ref[at, own] = mm_nt(norm, wt_ref[side, 1]).astype(BF)
            v_ref[at, own] = (mm_nt(norm, wt_ref[side, 2]) + v_bias).astype(BF)

    def norm_of(ref, start):
        rows = ref[pl.ds(start, HALF), :].astype(F32)
        return layer_norm_rows(rows, gain, shift)[0].astype(BF)

    def attend(queries):
        bias = bias_ref[...]

        def scores(block, sub):
            return score_tile(
                k_ref[:, head_cols(block)], bias, qt_ref[head_rows(block, sub), :queries], sub
            )

        s_ref[0, :, :queries] = scores(0, 0)

        def body(block, carry):
            for sub in range(4):
                following = (block, sub + 1) if sub < 3 else (lax.rem(block + 1, 4), 0)
                s_ref[(sub + 1) % 2, :, :queries] = scores(*following)
                tile = s_ref[sub % 2, :, :queries]
                top = jnp.max(tile, axis=0, keepdims=True)
                weights = jnp.exp2(tile - top)
                rows = head_rows(block, sub)
                values = jnp.concatenate([vt_ref[rows, :], jnp.ones((16, SEQ), BF)], axis=0)
                mixed = mm_nn(values, weights.astype(BF))
                total = mixed[HD : HD + 1]
                ot_ref[rows, :queries] = (mixed[:HD] * (1.0 / total)).astype(BF)
                lse_ref[0, block, sub : sub + 1, :queries] = top + jnp.log2(total)
            return carry

        lax.fori_loop(0, 4, body, 0)

    @pl.when(group == 0)
    def _():
        bias_ref[...] = key_bias(bias_ref.shape, mp, count_ref[2], True)
        project(norm_of(x_ref, row_block(0, mp)), 0)
        project(norm_of(other_ref, 0), HALF)
        attend(HALF)

    @pl.when(group > 0)
    def _():
        bias_ref[...] = key_bias(bias_ref.shape, mp, count_ref[3 * mp + group - 1], False)
        for part in range(2):
            project(norm_of(x_ref, row_block(2 * group - 1 + part, mp)), part * HALF)
        attend(SEQ)


def attend_forward(key_count, patches, other, wt, vec_params, small):
    tall = pl.BlockSpec((512, SEQ), lambda g: (0, g))
    wide = pl.BlockSpec((SEQ, 512), lambda g: (g, 0))
    ext = 3 * SEQ
    return pl.pallas_call(
        attend_kernel,
        grid=(3,),
        out_shape=[
            sds((512, ext), BF), sds((512, ext), BF), sds((512, ext), BF), sds((ext, 512), BF),
            sds((ext, 512), BF), sds((512, ext), BF), sds((3, 4, 8, SEQ), F32),
        ],
        in_specs=[
            pl.BlockSpec(memory_space=pltpu.SMEM), full_spec(patches.shape), full_spec(other.shape),
            full_spec(wt.shape), full_spec(vec_params.shape), full_spec(small.shape),
        ],
        out_specs=[
            tall, tall, tall, wide, wide, tall,
            pl.BlockSpec((1, 4, 8, SEQ), lambda g: (g, 0, 0, 0)),
        ],
        scratch_shapes=[
            pltpu.VMEM((512, SEQ), BF), pltpu.VMEM((SEQ, 128), BF), pltpu.VMEM((2, SEQ, SEQ), F32)
        ],
        compiler_params=pltpu.CompilerParams(vmem_limit_bytes=VMEM_LIMIT),
        name="attend_forward",
    )(key_count, patches, other, wt, vec_params, small)


def mlp_kernel(
    x_ref, dy_ref, ot_ref, wp_ref, wu_ref, wd_ref, vec_ref, small_ref,
    act_ref, dres_ref, dot_ref, gd_ref, gu_ref, gp_ref, vsum_ref, bsum_ref,
    res_ref, n2_ref, out_ref, dn_ref, hid_ref, dup_ref, dyc_ref, br_ref,
):
    step = pl.program_id(0)
    mp = lax.axis_index("mp")
    gain, shift = vec_ref[2:3, :], vec_ref[3:4, :]
    w_proj = wp_ref[...].reshape(512, 512)

    def rows(index):
        return pl.ds(pl.multiple_of(index * HALF, HALF), HALF)

    @pl.when(step == 0)
    def _():
        def body(index, carry):
            x_rows = x_ref[pl.ds(row_block(index, mp), HALF), :].astype(F32)
            mixed = ot_ref[:, pl.ds(ext_cols(index), HALF)]
            resid = x_rows + mm_tn(mixed, w_proj) + vec_ref[4:5, :]
            res_ref[rows(index), :] = resid
            n2_ref[rows(index), :] = layer_norm_rows(resid, gain, shift)[0].astype(BF)
            out_ref[rows(index), :] = resid + vec_ref[5:6, :]
            dn_ref[rows(index), :] = jnp.zeros((HALF, 512), F32)
            dyc_ref[rows(index), :] = dy_ref[pl.ds(row_block(index, mp), HALF), :]
            return carry

        lax.fori_loop(0, 5, body, 0)

    w_up, w_down = wu_ref[0], wd_ref[0]
    up_bias = small_ref[step // 2, 0:1, pl.ds(pl.multiple_of(lax.rem(step, 2) * 512, 512), 512)]

    def body(index, total):
        at = rows(index)
        up_pre = mm_nn(n2_ref[at, :], w_up) + up_bias
        cumulative = 0.5 * (1.0 + lax.erf(up_pre * (0.5**0.5)))
        density = jnp.exp(-0.5 * up_pre * up_pre) * 0.3989422804014327
        hidden = (up_pre * cumulative).astype(BF)
        hid_ref[at, :] = hidden
        out_ref[at, :] += mm_nn(hidden, w_down)
        slope = cumulative + up_pre * density
        dup = (mm_nt(dyc_ref[at, :], w_down) * slope).astype(BF)
        dup_ref[at, :] = dup
        dn_ref[at, :] += mm_nt(dup, w_up)
        return total + jnp.sum(dup.astype(F32).reshape(HALF // 8, 8, 512), axis=0)

    total = lax.fori_loop(0, 5, body, jnp.zeros((8, 512), F32))
    bsum_ref[0] = total
    gd_ref[0] = mm_tn(hid_ref[...], dyc_ref[...]).astype(BF)
    gu_ref[0] = mm_tn(n2_ref[...], dup_ref[...]).astype(BF)

    @pl.when(step == 3)
    def _():
        vsum_ref[...] = jnp.zeros_like(vsum_ref)

        def body(index, carry):
            at = rows(index)
            act_ref[pl.ds(row_block(index, mp), HALF), :] = out_ref[at, :].astype(BF)
            _, unit, inverse = layer_norm_rows(res_ref[at, :], gain, shift)
            dn = dn_ref[at, :]
            dy = dyc_ref[at, :].astype(F32)
            dres = dy + layer_norm_back(dn, unit, inverse, gain)
            dres_ref[at, :] = dres
            branch = dres.astype(BF)
            br_ref[at, :] = branch
            dot_ref[:, pl.ds(ext_cols(index), HALF)] = mm_nt(w_proj, branch).astype(BF)
            sums = [dn * unit, dn, branch.astype(F32), dy]
            for place, value in enumerate(sums):
                vsum_ref[place] += jnp.sum(value.reshape(HALF // 8, 8, 512), axis=0)
            return carry

        lax.fori_loop(0, 5, body, 0)
        mixed = jnp.concatenate([ot_ref[:, 0:HALF], ot_ref[:, SEQ:]], axis=1)
        gp_ref[...] = mm_nn(mixed, br_ref[...]).astype(BF).reshape(2, 256, 512)


def mlp(patches, cotangent, ot, wp, wu, wd, vec_params, small):
    rows = patches.shape[0]
    ext = 3 * SEQ
    up_spec = pl.BlockSpec((1, 512, 512), lambda f: (f // 2, 0, f % 2))
    down_spec = pl.BlockSpec((1, 512, 512), lambda f: (f // 2, f % 2, 0))
    return pl.pallas_call(
        mlp_kernel,
        grid=(4,),
        out_shape=[
            sds((rows, 512), BF), sds((rows, 512), F32), sds((512, ext), BF), sds((2, 1024, 512), BF),
            sds((2, 512, 1024), BF), sds((2, 256, 512), BF), sds((4, 8, 512), F32), sds((4, 8, 512), F32),
        ],
        in_specs=[
            full_spec((rows, 512)), full_spec((rows, 512)), full_spec((512, ext)), full_spec(wp.shape),
            up_spec, down_spec, full_spec(vec_params.shape), full_spec(small.shape),
        ],
        out_specs=[
            full_spec((rows, 512)), full_spec((rows, 512)), full_spec((512, ext)), down_spec, up_spec,
            full_spec((2, 256, 512)), full_spec((4, 8, 512)), pl.BlockSpec((1, 8, 512), lambda f: (f, 0, 0)),
        ],
        scratch_shapes=[
            pltpu.VMEM((rows, 512), F32), pltpu.VMEM((rows, 512), BF), pltpu.VMEM((rows, 512), F32),
            pltpu.VMEM((rows, 512), F32), pltpu.VMEM((rows, 512), BF), pltpu.VMEM((rows, 512), BF),
            pltpu.VMEM((rows, 512), BF), pltpu.VMEM((rows, 512), BF),
        ],
        compiler_params=pltpu.CompilerParams(vmem_limit_bytes=VMEM_LIMIT),
        name="mlp",
    )(patches, cotangent, ot, wp, wu, wd, vec_params, small)


def attend_back_kernel(
    count_ref, qt_ref, kt_ref, dot_ref, ot_ref, k_ref, v_ref, lse_ref, nt_ref, wt_ref,
    g_ref, dn_ref, far_ref, bsum_ref,
    grads_ref, acc_ref, bias_ref, s_ref, dp_ref,
):
    step = pl.program_id(0)
    mp = lax.axis_index("mp")

    @pl.when(step == 0)
    def _():
        acc_ref[...] = jnp.zeros_like(acc_ref)
        grads_ref[0:128, HALF:SEQ] = jnp.zeros((128, HALF), BF)
        bias_ref[0] = key_bias((SEQ, 128), mp, count_ref[2], True)
        for group in (1, 2):
            bias_ref[group] = key_bias((SEQ, 128), mp, count_ref[3 * mp + group - 1], False)

    def heads(group, queries):
        base = pl.multiple_of(group * SEQ, SEQ)
        keys_at, queries_at = pl.ds(base, SEQ), pl.ds(base, queries)
        bias = bias_ref[group]

        def tiles(sub):
            own = slice(sub * HD, sub * HD + HD)
            s_ref[sub % 2, :, :queries] = score_tile(
                k_ref[keys_at, :], bias, qt_ref[own, queries_at], sub
            )
            dp_ref[sub % 2, :, :queries] = mm_nn(
                v_ref[keys_at, :], widen_plain(dot_ref[own, queries_at], sub)
            )

        tiles(0)
        for sub in range(4):
            if sub < 3:
                tiles(sub + 1)
            own = slice(sub * HD, sub * HD + HD)
            q_rows, do_rows = qt_ref[own, queries_at], dot_ref[own, queries_at]
            delta = jnp.sum(
                do_rows.astype(F32) * ot_ref[own, queries_at].astype(F32), axis=0, keepdims=True
            )
            probs = jnp.exp2(s_ref[sub % 2, :, :queries] - lse_ref[group, 0, sub : sub + 1, :queries])
            draw = (probs * (dp_ref[sub % 2, :, :queries] - delta)).astype(BF)
            dq = mm_nn(kt_ref[own, keys_at], draw) * (HD ** (-0.5))
            grads_ref[own, queries_at] = dq.astype(BF)
            dk = mm_nt(q_rows, draw) * (1.0 / LOG2E)
            grads_ref[128 + sub * HD : 160 + sub * HD, keys_at] = dk.astype(BF)
            dv = mm_nt(do_rows, probs.astype(BF))
            grads_ref[256 + sub * HD : 288 + sub * HD, keys_at] = dv.astype(BF)

    heads(0, HALF)

    def body(group, carry):
        heads(group, SEQ)
        return carry

    lax.fori_loop(1, 3, body, 0)
    grads = grads_ref[...]
    for part in range(3):
        g_ref[0, part] = mm_nt(nt_ref[...], grads[part * 128 : part * 128 + 128]).astype(BF)
    bsum_ref[0] = mm_nt(jnp.ones((8, grads.shape[1]), BF), grads)
    acc_ref[...] += mm_tn(grads, wt_ref[0].reshape(384, 512))

    @pl.when(step == 3)
    def _():
        dn_ref[0:HALF] = acc_ref[0:HALF]
        dn_ref[HALF:] = acc_ref[SEQ:]
        far_ref[...] = acc_ref[HALF:SEQ].astype(BF)


def attend_back(key_count, qt, kt, dot, ot, k, v, lse, nt, wt):
    ext = 3 * SEQ
    tall = pl.BlockSpec((128, ext), lambda b: (b, 0))
    wide = pl.BlockSpec((ext, 128), lambda b: (0, b))
    return pl.pallas_call(
        attend_back_kernel,
        grid=(4,),
        out_shape=[
            sds((2, 3, 512, 256), BF), sds((ext - HALF, 512), F32), sds((HALF, 512), BF),
            sds((4, 8, 384), F32),
        ],
        in_specs=[
            pl.BlockSpec(memory_space=pltpu.SMEM), tall, tall, tall, tall, wide, wide,
            pl.BlockSpec((3, 1, 8, SEQ), lambda b: (0, b, 0, 0)), full_spec((512, ext)),
            pl.BlockSpec((1, 3, 128, 512), lambda b: (b // 2, 0, b % 2, 0)),
        ],
        out_specs=[
            pl.BlockSpec((1, 3, 512, 128), lambda b: (b // 2, 0, 0, b % 2)),
            full_spec((ext - HALF, 512)), full_spec((HALF, 512)),
            pl.BlockSpec((1, 8, 384), lambda b: (b, 0, 0)),
        ],
        scratch_shapes=[
            pltpu.VMEM((384, ext), BF), pltpu.VMEM((ext, 512), F32), pltpu.VMEM((3, SEQ, 128), BF),
            pltpu.VMEM((2, SEQ, SEQ), F32), pltpu.VMEM((2, SEQ, SEQ), F32),
        ],
        compiler_params=pltpu.CompilerParams(vmem_limit_bytes=VMEM_LIMIT),
        name="attend_back",
    )(key_count, qt, kt, dot, ot, k, v, lse, nt, wt)


def input_grad_kernel(x_ref, dn_ref, far_ref, dres_ref, vec_ref, grad_ref, vsum_ref):
    mp = lax.axis_index("mp")
    gain, shift = vec_ref[0:1, :], vec_ref[1:2, :]
    vsum_ref[...] = jnp.zeros_like(vsum_ref)

    def block(index, dn):
        at = pl.ds(pl.multiple_of(index * HALF, HALF), HALF)
        place = pl.ds(row_block(index, mp), HALF)
        _, unit, inverse = layer_norm_rows(x_ref[place, :].astype(F32), gain, shift)
        grad_ref[place, :] = dres_ref[at, :] + layer_norm_back(dn, unit, inverse, gain)
        vsum_ref[0] += jnp.sum((dn * unit).reshape(HALF // 8, 8, 512), axis=0)
        vsum_ref[1] += jnp.sum(dn.reshape(HALF // 8, 8, 512), axis=0)

    block(0, dn_ref[0:HALF] + far_ref[...].astype(F32))

    def body(index, carry):
        block(index, dn_ref[pl.ds(pl.multiple_of(index * HALF, HALF), HALF), :])
        return carry

    lax.fori_loop(1, 5, body, 0)


def finish_input(patches, dn, far, dres, vec_params):
    return pl.pallas_call(
        input_grad_kernel,
        out_shape=[sds(patches.shape, F32), sds((2, 8, 512), F32)],
        compiler_params=pltpu.CompilerParams(vmem_limit_bytes=VMEM_LIMIT),
        name="finish_input",
    )(patches, dn, far, dres, vec_params)


def reduce_kernel(
    down_ref, up_ref, proj_ref, qkv_ref, one_ref, two_ref, up_sum_ref, qkv_sum_ref,
    down_out, up_out, proj_out, qkv_out, small_out, norm_ref,
    *scratch,
):
    sends, scratch = scratch[-2:], scratch[:-2]
    send_sem, recv_sem = sends
    dp, mp = lax.axis_index("dp"), lax.axis_index("mp")
    core, x_side, z_near, z_far = partners(dp)
    targets = [{"dp": core}, {"mp": 1 - mp}, {"dp": x_side}, {"dp": z_near}, {"dp": z_far}]
    bits = [lax.rem(dp, 2), None] + [lax.rem(lax.div(dp, size), 2) for size in (2, 4, 8)]
    greet(targets)

    def send(src, dst, index, stage):
        copy = pltpu.make_async_remote_copy(
            src_ref=src, dst_ref=dst, send_sem=send_sem.at[index], recv_sem=recv_sem.at[index],
            device_id=targets[stage], device_id_type=MESH,
        )
        copy.start()
        return copy

    started = []
    arrays = []
    for index, (grad, out) in enumerate(
        [(down_ref, down_out), (up_ref, up_out), (proj_ref, proj_out), (qkv_ref, qkv_out)]
    ):
        fore, own, *landing = scratch[7 * index : 7 * index + 7]
        arrays.append((grad, out, fore, own, landing, 9 * index))
    small_bufs = scratch[28]
    square_bufs = scratch[29]

    def rows(start, size):
        return pl.ds(pl.multiple_of(start, 16), size)

    def share(total, upto):
        start, size = 0, total
        for stage in (0, 2, 3, 4):
            if stage > upto:
                break
            size //= 2
            start = start + bits[stage] * size
        return start, size

    live = {}

    def begin(entry, stage):
        grad, out, fore, own, landing, base = entry
        total = grad.shape[1]
        if stage == 0:
            size = total // 2
            away = (1 - bits[0]) * size
            live[base] = send(grad.at[:, rows(away, size), :], landing[0], base, 0)
        elif stage == 1:
            live[base] = send(fore, landing[1], base + 1, 1)
        elif stage <= 4:
            start, size = share(total, stage)
            outer, outer_size = share(total, stage - 1)
            away = (1 - bits[stage]) * size
            offset = outer - share(total, 0)[0]
            live[base] = send(own.at[rows(offset + away, size), :], landing[stage], base + stage, stage)
        else:
            level = (None, 4, 3, 2, 0)[stage - 4]
            start, size = share(total, level)
            where = out.at[rows(start, size), :]
            live[base] = send(where, where, base + stage, level)
        started.append(live[base])

    def end(entry, stage):
        grad, out, fore, own, landing, base = entry
        total = grad.shape[1]
        live[base].wait_recv()
        first = share(total, 0)[0]
        if stage == 0:
            size = total // 2
            at = rows(first, size)
            fore[...] = grad[1 - mp, at, :] + landing[0][1 - mp]
            own[...] = grad[mp, at, :] + landing[0][mp]
        elif stage == 1:
            own[...] += landing[1][...]
        elif stage <= 4:
            start, size = share(total, stage)
            at = rows(start - first, size)
            value = own[at, :] + landing[stage][...]
            if stage < 4:
                own[at, :] = value
            else:
                out[rows(start, size), :] = value
                wide = value.astype(F32)
                square = jnp.sum((wide * wide).reshape(-1, 8, wide.shape[1]), axis=0)
                folded = square[:, 0:128]
                for lane in range(1, wide.shape[1] // 128):
                    folded = folded + square[:, lane * 128 : lane * 128 + 128]
                squares.append(folded)

    squares = []
    small_live = []
    square_live = []

    def small_begin(stage):
        small_live.append(send(small_bufs.at[0, stage], small_bufs.at[1, stage], 36 + stage, stage))

    def small_end(stage):
        small_live[stage].wait_recv()
        value = small_bufs[0, stage] + small_bufs[1, stage]
        if stage < 4:
            small_bufs[0, stage + 1] = value
        else:
            small_out[...] = value

    order = (4, 3, 2, 0, 1)

    def square_begin(place):
        square_live.append(
            send(square_bufs.at[0, place], square_bufs.at[1, place], 41 + place, order[place])
        )

    def square_end(place):
        square_live[place].wait_recv()
        value = square_bufs[0, place] + square_bufs[1, place]
        if place < 4:
            square_bufs[0, place + 1] = value
        else:
            total = jnp.sum(small_out[...] * small_out[...]) + jnp.sum(value)
            norm_ref[...] = jnp.sqrt(jnp.full((8, 128), total, F32))

    def small_row(place, value):
        small_bufs[0, 0, place : place + 1, :] = value

    small_bufs[0, 0] = jnp.zeros((16, 512), F32)
    for block in range(4):
        lanes = slice(block * 128, block * 128 + 128)
        small_bufs[0, 0, 0:1, lanes] = qkv_sum_ref[block, 0:1, 0:128]
        small_bufs[0, 0, 1:2, lanes] = qkv_sum_ref[block, 0:1, 256:384]
        small_row(2 + block, jnp.sum(up_sum_ref[block], axis=0, keepdims=True))
        small_row(8 + block, jnp.sum(two_ref[block], axis=0, keepdims=True))
    for place in range(2):
        small_row(6 + place, jnp.sum(one_ref[place], axis=0, keepdims=True))
    small_begin(0)
    for tick in range(4 + 9):
        for index, entry in enumerate(arrays):
            stage = tick - index
            if stage < 0 or stage > 9:
                continue
            if stage > 0:
                end(entry, stage - 1)
            if stage < 9:
                begin(entry, stage)
            if stage == 5 and index == 3:
                square_bufs[0, 0] = squares[0] + squares[1] + squares[2] + squares[3]
                square_begin(0)
            if stage > 5 and index == 3:
                square_end(stage - 6)
                square_begin(stage - 5)
        if 1 <= tick <= 5:
            small_end(tick - 1)
            if tick < 5:
                small_begin(tick)
    square_end(4)
    for copy in started + small_live + square_live:
        copy.wait_send()


def reduce_gradients(down, up, proj, qkv, *sums):
    vmem = pl.BlockSpec(memory_space=pltpu.VMEM)
    scratch = []
    for array in (down, up, proj, qkv):
        _, rows, width = array.shape
        scratch += [pltpu.VMEM((rows // 2, width), BF), pltpu.VMEM((rows // 2, width), BF)]
        scratch += [pltpu.VMEM((2, rows // 2, width), BF), pltpu.VMEM((rows // 2, width), BF)]
        scratch += [pltpu.VMEM((rows // size, width), BF) for size in (4, 8, 16)]
    scratch += [pltpu.VMEM((2, 5, 16, 512), F32), pltpu.VMEM((2, 5, 8, 128), F32)]
    scratch += [pltpu.SemaphoreType.DMA((46,)), pltpu.SemaphoreType.DMA((46,))]
    return pl.pallas_call(
        reduce_kernel,
        out_shape=[sds(array.shape[1:], BF) for array in (down, up, proj, qkv)]
        + [sds((16, 512), F32), sds((8, 128), F32)],
        in_specs=[vmem] * 8,
        out_specs=[vmem] * 6,
        scratch_shapes=scratch,
        compiler_params=pltpu.CompilerParams(
            collective_id=1, has_side_effects=True, vmem_limit_bytes=VMEM_LIMIT
        ),
        name="reduce_gradients",
    )(down, up, proj, qkv, *sums)


def adam_kernel(norm_ref, *refs):
    factor = jnp.minimum(1.0, CLIP_NORM / (norm_ref[0:1, 0:1] + 1e-06))
    for index in range(4):
        weight_ref, one_ref, two_ref, grad_ref = refs[4 * index : 4 * index + 4]
        outs = refs[16 + 3 * index : 19 + 3 * index]
        results = adam_update(
            weight_ref[...], grad_ref[...].astype(F32) * factor, one_ref[...], two_ref[...],
            MATRIX_RATE, DECAY_RATE,
        )
        for out, value in zip(outs, results):
            out[...] = value


def adam_matrices(norm, groups):
    steps = 8
    in_specs, out_specs, out_shape, args = [full_spec((8, 128))], [], [], [norm]
    for group in groups:
        rows, width = group[0].shape
        spec = pl.BlockSpec((rows // steps, width), lambda i: (i, 0))
        in_specs += [spec] * 4
        out_specs += [spec] * 3
        out_shape += [sds((rows, width), F32)] * 3
        args += list(group)
    outs = pl.pallas_call(
        adam_kernel,
        grid=(steps,),
        out_shape=out_shape,
        in_specs=in_specs,
        out_specs=out_specs,
        compiler_params=pltpu.CompilerParams(vmem_limit_bytes=VMEM_LIMIT),
        name="adam_matrices",
    )(*args)
    return [outs[3 * index : 3 * index + 3] for index in range(len(groups))]


IN_SPECS = (
            P(("dp", "mp"), None),
            P(("dp", "mp"), None),
            P("dp"),
            P(None, None, "mp"),
            P("mp", None),
            P(None, "mp"),
            P("mp", None),
            P(None, "mp"),
            P("mp"),
            P(),
            P(None, None, "mp"),
            P(None, None, "mp"),
            P("mp", None),
            P("mp", None),
            P(None, "mp"),
            P(None, "mp"),
            P("mp", None),
            P("mp", None),
            P(None, "mp"),
            P(None, "mp"),
            P("mp"),
            P("mp"),
            P(),
            P(),
        )
OUT_SPECS = (
            P(("dp", "mp"), None),
            P(("dp", "mp"), None),
            P(),
            P(None, None, "mp"),
            P(None, None, "mp"),
            P(None, None, "mp"),
            P("mp", None),
            P("mp", None),
            P("mp", None),
            P(None, "mp"),
            P(None, "mp"),
            P(None, "mp"),
            P("mp", None),
            P("mp", None),
            P("mp", None),
            P(None, "mp"),
            P(None, "mp"),
            P(None, "mp"),
            P("mp"),
            P("mp"),
            P("mp"),
            P(),
            P(),
            P(),
        )


def paired(
    patches, cotangent, key_count, w_qkv, w_proj, w_up, w_down, qv_bias, up_bias, vec_params,
    first_qkv, second_qkv, first_proj, second_proj, first_up, second_up, first_down, second_down,
    first_qv_bias, second_qv_bias, first_up_bias, second_up_bias, first_vec, second_vec,
):
    mp = lax.axis_index("mp")
    small = jnp.concatenate(
        [up_bias[None, :], jnp.pad(qv_bias, ((0, 0), (0, 768))), jnp.zeros((5, 1024), F32)], axis=0
    )
    wt, wp, wu, wd, small_all, other = gather_weights(w_qkv, w_proj, w_up, w_down, small, patches)
    nt, qt, kt, k, v, ot, lse = attend_forward(key_count, patches, other, wt, vec_params, small_all)
    activations, dres, dot, g_down, g_up, g_proj, vsum_two, up_sums = mlp(
        patches, cotangent, ot, wp, wu, wd, vec_params, small_all
    )
    g_qkv, dn, far, qkv_sums = attend_back(key_count, qt, kt, dot, ot, k, v, lse, nt, wt)
    arrived = lax.ppermute(far, "mp", [(0, 1), (1, 0)])
    input_grad, vsum_one = finish_input(patches, dn, arrived, dres, vec_params)
    down, up, proj, qkv, small_total, norm = reduce_gradients(
        g_down, g_up, g_proj, g_qkv.reshape(2, 1536, 256), vsum_one, vsum_two, up_sums, qkv_sums
    )
    flat = lambda array: array.reshape(-1, array.shape[-1])
    groups = [
        (flat(w_qkv), flat(first_qkv), flat(second_qkv), qkv),
        (w_proj, first_proj, second_proj, proj),
        (w_up, first_up, second_up, up),
        (w_down, first_down, second_down, down),
    ]
    new_qkv, new_proj, new_up, new_down = adam_matrices(norm, groups)
    grad_norm = norm[0, 0]
    factor = jnp.minimum(1.0, CLIP_NORM / (grad_norm + 1e-06))
    qv_total = lax.dynamic_slice_in_dim(small_total[0:2], mp * 256, 256, 1)
    up_total = lax.dynamic_slice_in_dim(small_total[2:6].reshape(-1), mp * 1024, 1024, 0)
    new_qvb = adam_update(qv_bias, qv_total * factor, first_qv_bias, second_qv_bias, VECTOR_RATE, 0.0)
    new_upb = adam_update(up_bias, up_total * factor, first_up_bias, second_up_bias, VECTOR_RATE, 0.0)
    new_vec = adam_update(
        vec_params, small_total[6:12] * factor, first_vec, second_vec, VECTOR_RATE, 0.0
    )
    return (
        activations, input_grad, grad_norm, *[array.reshape(w_qkv.shape) for array in new_qkv],
        *new_proj, *new_up, *new_down, *new_qvb, *new_upb, *new_vec,
    )


def fits_pairs(mesh, args):
    if dict(mesh.shape) != {"dp": 16, "mp": 2}:
        return False
    return args[0].shape == (40960, 512) and args[2].shape == (80,)


def solution(mesh):
    def run(*args):
        body = paired if fits_pairs(mesh, args) else local
        return jax.shard_map(body, mesh=mesh, in_specs=IN_SPECS, out_specs=OUT_SPECS, check_vma=False)(*args)

    return run
```

```python
import jax
import jax.numpy as jnp
from jax import lax
from jax.experimental import pallas as pl
from jax.experimental.pallas import tpu as pltpu
from jax.sharding import PartitionSpec as P

HD = 32
ADAM_STEP = 10


NORM_EPS = 1e-06
BETA_FIRST = 0.9
BETA_SECOND = 0.95
ADAM_EPS = 1e-08
DECAY_RATE = 0.05
MATRIX_RATE = 0.1
VECTOR_RATE = 0.8
CLIP_NORM = 1.0
MASK_FILL = -1e30
LOG2E = 1.4426950408889634
BF = jnp.bfloat16
F32 = jnp.float32
MESH = pl.DeviceIdType.MESH
SEQ = 512
HALF = 256
VMEM_LIMIT = 58 * 1024 * 1024


def mm_nn(left, right):
    return lax.dot_general(left, right, (((1,), (0,)), ((), ())), preferred_element_type=F32)


def mm_nt(left, right):
    return lax.dot_general(left, right, (((1,), (1,)), ((), ())), preferred_element_type=F32)


def mm_tn(left, right):
    return lax.dot_general(left, right, (((0,), (0,)), ((), ())), preferred_element_type=F32)


def partners(dp):
    core = dp + 1 - 2 * lax.rem(dp, 2)
    x_side = dp + 2 - 4 * lax.rem(lax.div(dp, 2), 2)
    z_near = dp + 4 - 8 * lax.rem(lax.div(dp, 4), 2)
    z_far = dp + 8 - 16 * lax.rem(lax.div(dp, 8), 2)
    return core, x_side, z_near, z_far


def greet(targets):
    barrier = pltpu.get_barrier_semaphore()
    for target in targets:
        pl.semaphore_signal(barrier, inc=1, device_id=target, device_id_type=MESH)
    pl.semaphore_wait(barrier, len(targets))


def full_spec(shape):
    return pl.BlockSpec(shape, lambda *_: (0,) * len(shape))


def sds(shape, dtype):
    return jax.ShapeDtypeStruct(shape, dtype)


def row_block(index, mp):
    return pl.multiple_of(lax.rem(index + 4 * (1 - mp), 5) * HALF, HALF)


def ext_cols(index):
    return pl.multiple_of(jnp.where(index == 0, 0, HALF + HALF * index), HALF)


def norm_forward(values, norm_gain, norm_shift):
    row_mean = jnp.mean(values, axis=-1, keepdims=True)
    centred = values - row_mean
    inverse = lax.rsqrt(jnp.mean(centred * centred, axis=-1, keepdims=True) + NORM_EPS)
    normed = centred * inverse
    return (normed * norm_gain + norm_shift, normed, inverse)


def norm_backward(grad_rows, normed, inverse, norm_gain):
    scaled = grad_rows * norm_gain
    centre_term = jnp.mean(scaled, axis=-1, keepdims=True)
    slope_term = jnp.mean(scaled * normed, axis=-1, keepdims=True)
    return inverse * (scaled - centre_term - normed * slope_term)


def exact_gelu(values):
    return jax.nn.gelu(values, approximate=False)


def key_mask(key_count, length):
    position = lax.broadcasted_iota(jnp.int32, (1, 1, 1, length), 3)
    return position < key_count[:, None, None, None]


def masked_scores(queries, key_rows, key_count):
    raw_scores = jnp.einsum(
        "sqhe,skhe->shqk", queries, key_rows, preferred_element_type=jnp.float32
    )
    scaled = raw_scores * queries.shape[-1] ** (-0.5)
    return jnp.where(key_mask(key_count, key_rows.shape[1]), scaled, MASK_FILL)


def attend_backward(queries, key_rows, value_rows, key_count, log_total, attended_grad):
    scores = masked_scores(queries, key_rows, key_count)
    probs = jnp.exp(scores - log_total)
    probs_low = probs.astype(jnp.bfloat16)
    probs_grad = jnp.einsum(
        "sqhe,skhe->shqk", attended_grad, value_rows, preferred_element_type=jnp.float32
    )
    score_grad = probs * (probs_grad - jnp.sum(probs_grad * probs, axis=-1, keepdims=True))
    visible = key_mask(key_count, key_rows.shape[1])
    raw_grad = jnp.where(visible, score_grad * queries.shape[-1] ** (-0.5), 0.0).astype(
        jnp.bfloat16
    )
    query_grad = jnp.einsum(
        "shqk,skhe->sqhe", raw_grad, key_rows, preferred_element_type=jnp.float32
    )
    key_grad = jnp.einsum("shqk,sqhe->skhe", raw_grad, queries, preferred_element_type=jnp.float32)
    value_grad = jnp.einsum(
        "shqk,sqhe->skhe", probs_low, attended_grad, preferred_element_type=jnp.float32
    )
    return jnp.stack([query_grad, key_grad, value_grad])


def own_slice(values, own_start, own_rows):
    return lax.dynamic_slice_in_dim(values, own_start, own_rows, 0)


def contract_rows(left, right):
    return lax.dot_general(
        left, right, (((0,), (0,)), ((), ())), preferred_element_type=jnp.float32
    )


def contract_cols(left, right):
    return lax.dot_general(
        left, right, (((1,), (1,)), ((), ())), preferred_element_type=jnp.float32
    )


def adam_update(weight, gradient, moment_one, moment_two, step_rate, decay_rate):
    first_new = BETA_FIRST * moment_one + (1.0 - BETA_FIRST) * gradient
    second_new = BETA_SECOND * moment_two + (1.0 - BETA_SECOND) * gradient * gradient
    first_hat = first_new / (1.0 - BETA_FIRST**ADAM_STEP)
    second_hat = second_new / (1.0 - BETA_SECOND**ADAM_STEP)
    weight_new = weight - step_rate * (
        first_hat / (jnp.sqrt(second_hat) + ADAM_EPS) + decay_rate * weight
    )
    return (weight_new, first_new, second_new)


def local(
    patches,
    cotangent,
    key_count,
    w_qkv,
    w_proj,
    w_up,
    w_down,
    qv_bias,
    up_bias,
    vec_params,
    first_qkv,
    second_qkv,
    first_proj,
    second_proj,
    first_up,
    second_up,
    first_down,
    second_down,
    first_qv_bias,
    second_qv_bias,
    first_up_bias,
    second_up_bias,
    first_vec,
    second_vec,
):
    own_rows = patches.shape[0]
    seq_count = key_count.shape[0]
    own_start = lax.axis_index("mp") * own_rows
    local_width = w_proj.shape[0]
    local_heads = local_width // HD
    own_grad = cotangent.astype(jnp.float32)
    qkv_low = w_qkv.astype(jnp.bfloat16)
    proj_low = w_proj.astype(jnp.bfloat16)
    up_low = w_up.astype(jnp.bfloat16)
    down_low = w_down.astype(jnp.bfloat16)
    gain_one, shift_one = (vec_params[0], vec_params[1])
    gain_two, shift_two = (vec_params[2], vec_params[3])
    proj_shift, down_shift = (vec_params[4], vec_params[5])
    qkv_shift = jnp.stack([qv_bias[0], jnp.zeros_like(qv_bias[0]), qv_bias[1]])[:, None, :]
    gathered, grad_all = (
        lax.all_gather(patches, "mp", axis=0, tiled=True),
        lax.all_gather(cotangent, "mp", axis=0, tiled=True),
    )
    whole_rows = gathered.astype(jnp.float32)
    normed_all, unit_one, inverse_one = norm_forward(whole_rows, gain_one, shift_one)
    norm_one = normed_all.astype(jnp.bfloat16)
    projected = (
        jnp.einsum("td,cde->cte", norm_one, qkv_low, preferred_element_type=jnp.float32) + qkv_shift
    )
    shaped = projected.astype(jnp.bfloat16).reshape(3, seq_count, -1, local_heads, HD)
    queries, key_rows, value_rows = (shaped[0], shaped[1], shaped[2])
    scores = masked_scores(queries, key_rows, key_count)
    top_score = jnp.max(scores, axis=-1, keepdims=True)
    log_total = top_score + jnp.log(jnp.sum(jnp.exp(scores - top_score), axis=-1, keepdims=True))
    probs_low = jnp.exp(scores - log_total).astype(jnp.bfloat16)
    attended = jnp.einsum(
        "shqk,skhe->sqhe", probs_low, value_rows, preferred_element_type=jnp.float32
    )
    attended_low = attended.astype(jnp.bfloat16).reshape(-1, local_width)
    proj_part = jnp.dot(attended_low, proj_low, preferred_element_type=jnp.float32)
    resid_all = whole_rows + lax.psum(proj_part, "mp") + proj_shift
    mid_all, unit_two, inverse_two = norm_forward(resid_all, gain_two, shift_two)
    norm_two = mid_all.astype(jnp.bfloat16)
    up_pre = jnp.dot(norm_two, up_low, preferred_element_type=jnp.float32) + up_bias
    hidden_full, gelu_pull = jax.vjp(exact_gelu, up_pre)
    hidden_low = hidden_full.astype(jnp.bfloat16)
    down_part = jnp.dot(hidden_low, down_low, preferred_element_type=jnp.float32)
    out_all = (
        resid_all + lax.psum(down_part.astype(jnp.bfloat16), "mp").astype(jnp.float32) + down_shift
    )
    block_out = own_slice(out_all, own_start, own_rows)
    activations = block_out.astype(jnp.bfloat16)
    down_grad = contract_rows(hidden_low, grad_all)
    hidden_grad = contract_cols(grad_all, down_low)
    up_grad_rows = gelu_pull(hidden_grad)[0].astype(jnp.bfloat16)
    up_grad = contract_rows(norm_two, up_grad_rows)
    up_bias_grad = jnp.sum(up_grad_rows.astype(jnp.float32), axis=0)
    mid_part = contract_cols(up_grad_rows, up_low)
    mid_all_grad = lax.psum(mid_part.astype(jnp.bfloat16), "mp").astype(jnp.float32)
    resid_all_grad = grad_all.astype(jnp.float32) + norm_backward(
        mid_all_grad, unit_two, inverse_two, gain_two
    )
    branch_low = resid_all_grad.astype(jnp.bfloat16)
    own_branch = own_slice(branch_low, own_start, own_rows)
    mid_grad = own_slice(mid_all_grad, own_start, own_rows)
    mid_unit = own_slice(unit_two, own_start, own_rows)
    proj_grad = contract_rows(attended_low, branch_low)
    attended_grad = (
        contract_cols(branch_low, proj_low)
        .astype(jnp.bfloat16)
        .reshape(seq_count, -1, local_heads, HD)
    )
    qkv_grads = attend_backward(queries, key_rows, value_rows, key_count, log_total, attended_grad)
    qkv_grad_rows = qkv_grads.reshape(3, -1, local_width).astype(jnp.bfloat16)
    qkv_grad = jnp.einsum(
        "td,cte->cde", norm_one, qkv_grad_rows, preferred_element_type=jnp.float32
    )
    qkv_grad_sums = jnp.sum(qkv_grad_rows.astype(jnp.float32), axis=1)
    qv_bias_grad = jnp.stack([qkv_grad_sums[0], qkv_grad_sums[2]])
    first_part = jnp.einsum(
        "cte,cde->td", qkv_grad_rows, qkv_low, preferred_element_type=jnp.float32
    )
    first_all = lax.psum(first_part.astype(jnp.bfloat16), "mp").astype(jnp.float32)
    input_all = resid_all_grad + norm_backward(first_all, unit_one, inverse_one, gain_one)
    input_grad = own_slice(input_all, own_start, own_rows)
    own_first_grad = own_slice(first_all, own_start, own_rows)
    own_unit_one = own_slice(unit_one, own_start, own_rows)
    vec_grad = jnp.stack(
        [
            jnp.sum(own_first_grad * own_unit_one, axis=0),
            jnp.sum(own_first_grad, axis=0),
            jnp.sum(mid_grad * mid_unit, axis=0),
            jnp.sum(mid_grad, axis=0),
            jnp.sum(own_branch.astype(jnp.float32), axis=0),
            jnp.sum(own_grad, axis=0),
        ]
    )
    summed = (
        lax.psum(qkv_grad.astype(jnp.bfloat16), "dp").astype(jnp.float32),
        lax.psum(proj_grad.astype(jnp.bfloat16), "dp").astype(jnp.float32),
        lax.psum(up_grad.astype(jnp.bfloat16), "dp").astype(jnp.float32),
        lax.psum(down_grad.astype(jnp.bfloat16), "dp").astype(jnp.float32),
        lax.psum(qv_bias_grad.astype(jnp.bfloat16), "dp").astype(jnp.float32),
        lax.psum(up_bias_grad.astype(jnp.bfloat16), "dp").astype(jnp.float32),
        lax.psum(vec_grad.astype(jnp.bfloat16), "dp").astype(jnp.float32),
    )
    split_square = jnp.float32(0.0)
    for gradient in summed[:6]:
        split_square = split_square + jnp.sum(gradient * gradient)
    vec_total, split_total = lax.psum((summed[6], split_square), "mp")
    grad_norm = jnp.sqrt(split_total + jnp.sum(vec_total * vec_total))
    factor = jnp.minimum(1.0, CLIP_NORM / (grad_norm + 1e-06))
    qkv_new, qkv_first, qkv_second = adam_update(
        w_qkv, summed[0] * factor, first_qkv, second_qkv, MATRIX_RATE, DECAY_RATE
    )
    proj_new, proj_first, proj_second = adam_update(
        w_proj, summed[1] * factor, first_proj, second_proj, MATRIX_RATE, DECAY_RATE
    )
    up_new, up_first, up_second = adam_update(
        w_up, summed[2] * factor, first_up, second_up, MATRIX_RATE, DECAY_RATE
    )
    down_new, down_first, down_second = adam_update(
        w_down, summed[3] * factor, first_down, second_down, MATRIX_RATE, DECAY_RATE
    )
    qvb_new, qvb_first, qvb_second = adam_update(
        qv_bias, summed[4] * factor, first_qv_bias, second_qv_bias, VECTOR_RATE, 0.0
    )
    upb_new, upb_first, upb_second = adam_update(
        up_bias, summed[5] * factor, first_up_bias, second_up_bias, VECTOR_RATE, 0.0
    )
    vec_new, vec_first, vec_second = adam_update(
        vec_params, vec_total * factor, first_vec, second_vec, VECTOR_RATE, 0.0
    )
    return (
        activations,
        input_grad,
        grad_norm,
        qkv_new,
        qkv_first,
        qkv_second,
        proj_new,
        proj_first,
        proj_second,
        up_new,
        up_first,
        up_second,
        down_new,
        down_first,
        down_second,
        qvb_new,
        qvb_first,
        qvb_second,
        upb_new,
        upb_first,
        upb_second,
        vec_new,
        vec_first,
        vec_second,
    )


def layer_norm_rows(rows, gain, shift):
    centred = rows - jnp.mean(rows, axis=-1, keepdims=True)
    inverse = lax.rsqrt(jnp.mean(centred * centred, axis=-1, keepdims=True) + NORM_EPS)
    unit = centred * inverse
    return unit * gain + shift, unit, inverse


def layer_norm_back(grad, unit, inverse, gain):
    scaled = grad * gain
    centre = jnp.mean(scaled, axis=-1, keepdims=True)
    slope = jnp.mean(scaled * unit, axis=-1, keepdims=True)
    return inverse * (scaled - centre - unit * slope)


def head_rows(block, sub):
    return pl.ds(pl.multiple_of(block * 128 + sub * HD, HD), HD)


def head_cols(block):
    return pl.ds(pl.multiple_of(block * 128, 128), 128)


def key_bias(shape, mp, count, shared):
    slot = lax.broadcasted_iota(jnp.int32, shape, 0)
    if shared:
        slot = lax.rem(slot + HALF * mp, SEQ)
    return jnp.where(slot < count, 0.0, MASK_FILL).astype(BF)


def widen(rows, sub):
    zeros = jnp.zeros_like(rows)
    row = lax.broadcasted_iota(jnp.int32, rows.shape, 0)
    ones = jnp.where(row == 0, 1.0, 0.0).astype(BF)
    parts = [zeros] * 4
    parts[sub] = rows
    parts[(sub + 1) % 4] = ones
    return jnp.concatenate(parts, axis=0)


def widen_plain(rows, sub):
    parts = [jnp.zeros_like(rows)] * 4
    parts[sub] = rows
    return jnp.concatenate(parts, axis=0)


def score_tile(key_block, bias, query_rows, sub):
    lane = lax.broadcasted_iota(jnp.int32, key_block.shape, 1)
    keys = jnp.where(lane // HD == (sub + 1) % 4, bias, key_block)
    return mm_nn(keys, widen(query_rows, sub))


def forward_kernel(
    count_ref, qkv_ref, proj_ref, up_ref, down_ref, small_ref, x_ref, vec_ref,
    wt_out, wp_out, wu_out, wd_out, sm_out,
    nt_out, qt_out, kt_out, k_out, v_out, ot_out, lse_out,
    wt_ref, own_proj, own_up, own_down, sm_ref, other_ref,
    norm_ref, nt_ref, qt_ref, kt_ref, vt_ref, k_ref, v_ref, ot_ref, lse_ref, bias_ref, s_ref,
    send_sem, recv_sem, local_sem,
):
    dp, mp = lax.axis_index("dp"), lax.axis_index("mp")
    peer = 1 - mp
    core, x_side, _, _ = partners(dp)
    quarter = lax.rem(dp, 4)
    x_quarter = lax.rem(quarter + 2, 4)
    gain, shift = vec_ref[0:1, :], vec_ref[1:2, :]
    greet([{"mp": peer}, {"dp": core}, {"dp": x_side}])

    remote, local = [], []

    class Transfer:
        def __init__(self, src, dst, target):
            self.index = len(remote)
            self.views = (src, dst, target)
            remote.append(self)
            self.make().start()

        def make(self):
            src, dst, target = self.views
            return pltpu.make_async_remote_copy(
                src_ref=src(), dst_ref=dst(), send_sem=send_sem.at[self.index],
                recv_sem=recv_sem.at[self.index], device_id=target, device_id_type=MESH,
            )

        def wait_recv(self):
            self.make().wait_recv()

        def wait_send(self):
            self.make().wait_send()

    def send(src, dst, target):
        return Transfer(src, dst, target)

    def keep(src, dst):
        copy = pltpu.make_async_copy(src, dst, local_sem.at[len(local)])
        copy.start()
        local.append(copy)

    def span(start, size):
        return pl.ds(pl.multiple_of(start, 16), size)

    pieces = []
    for part in range(3):
        pieces.append((wt_ref.at[mp, part], lambda side, part=part: wt_ref.at[side, part], 64, 0))
    pieces.append((own_proj, lambda side: wp_out.at[side], 64, 0))
    for shard, out, rows in ((own_up, wu_out, 128), (own_down, wd_out, 256)):
        for part in range(2):
            pieces.append((shard, lambda side, out=out: out.at[side], rows // 2, part * rows * 2))

    def place(ref, index, part):
        rows, base = pieces[index][2], pieces[index][3]
        return ref.at[span(base + part * rows, rows), :]

    first, second, third = {}, {}, {}

    def to_peer(index):
        first[index] = send(
            lambda: place(pieces[index][0], index, quarter),
            lambda: place(pieces[index][1](mp), index, quarter), {"mp": peer},
        )

    def to_sides(index):
        first[index].wait_recv()
        at = lambda: place(pieces[index][1](peer), index, quarter)
        second[index] = send(at, at, {"dp": x_side})
        third[index] = [send(at, at, {"dp": core})]

    def to_core(index):
        second[index].wait_recv()
        at = lambda: place(pieces[index][1](peer), index, x_quarter)
        third[index].append(send(at, at, {"dp": core}))

    def arrive(index):
        for copy in third[index]:
            copy.wait_recv()

    own_half = pl.multiple_of((1 - mp) * 4 * HALF, HALF)
    for part in range(3):
        wt_ref[mp, part] = qkv_ref[part].T.astype(BF)
        to_peer(part)
    sm_ref[mp] = small_ref[...]
    small_copy = send(lambda: sm_ref.at[mp], lambda: sm_ref.at[mp], {"mp": peer})
    own_proj[...] = proj_ref[...].astype(BF)
    own_up[...] = up_ref[...].astype(BF)
    own_down[...] = down_ref[...].astype(BF)
    keep(wt_ref.at[mp], wt_out.at[mp])
    keep(own_proj, wp_out.at[mp])
    keep(own_up, wu_out.at[mp])
    keep(own_down, wd_out.at[mp])

    def as_column(row):
        return jnp.broadcast_to(row, (8, row.shape[1])).T[:, 0:1]

    def normalise(group, part, rows):
        base = group * SEQ + part * HALF
        norm = layer_norm_rows(rows.astype(F32), gain, shift)[0].astype(BF)
        norm_ref[span(base, HALF), :] = norm
        nt_ref[:, pl.ds(pl.multiple_of(base, HALF), HALF)] = norm.T

    def project(side, group):
        base = pl.multiple_of(group * SEQ, SEQ)
        at = pl.ds(base, SEQ)
        own = pl.ds(pl.multiple_of(side * 256, 256), 256)
        norm = norm_ref[at, :]
        q_bias, v_bias = sm_ref[side, 1:2, 0:256], sm_ref[side, 2:3, 0:256]
        scale = LOG2E * HD ** (-0.5)
        qt_ref[own, at] = ((mm_nt(wt_ref[side, 0], norm) + as_column(q_bias)) * scale).astype(BF)
        kt_ref[own, at] = mm_nt(wt_ref[side, 1], norm).astype(BF)
        vt_ref[own, :] = (mm_nt(wt_ref[side, 2], norm) + as_column(v_bias)).astype(BF)
        k_ref[at, own] = mm_nt(norm, wt_ref[side, 1]).astype(BF)
        v_ref[at, own] = (mm_nt(norm, wt_ref[side, 2]) + v_bias).astype(BF)

    def attend(side, group, queries, between):
        base = pl.multiple_of(group * SEQ, SEQ)
        keys_at, queries_at = pl.ds(base, SEQ), pl.ds(base, queries)
        bias = bias_ref[group]

        def scores(block, sub):
            return score_tile(
                k_ref[keys_at, head_cols(block)], bias, qt_ref[head_rows(block, sub), queries_at], sub
            )

        s_ref[0, :, :queries] = scores(2 * side, 0)

        def body(step, carry):
            block = 2 * side + step
            for sub in range(4):
                following = (block, sub + 1) if sub < 3 else (2 * side + 1, 0)
                s_ref[(sub + 1) % 2, :, :queries] = scores(*following)
                tile = s_ref[sub % 2, :, :queries]
                top = jnp.max(tile, axis=0, keepdims=True)
                weights = jnp.exp2(tile - top)
                rows = head_rows(block, sub)
                values = jnp.concatenate([vt_ref[rows, :], jnp.ones((16, SEQ), BF)], axis=0)
                mixed = mm_nn(values, weights.astype(BF))
                total = mixed[HD : HD + 1]
                ot_ref[rows, queries_at] = (mixed[:HD] * (1.0 / total)).astype(BF)
                lse_ref[group, block, sub : sub + 1, :queries] = top + jnp.log2(total)

            @pl.when(step == 0)
            def _():
                between()

            return carry

        lax.fori_loop(0, 2, body, 0)

    def nothing():
        pass

    def unit(side, group, queries, early=nothing, between=nothing):
        project(side, group)
        early()
        attend(side, group, queries, between)
        at = pl.ds(pl.multiple_of(group * SEQ, SEQ), SEQ)
        own = pl.ds(pl.multiple_of(side * 256, 256), 256)
        keep(qt_ref.at[own, at], qt_out.at[own, at])
        keep(kt_ref.at[own, at], kt_out.at[own, at])
        keep(ot_ref.at[own, at], ot_out.at[own, at])
        keep(k_ref.at[at, own], k_out.at[at, own])
        keep(v_ref.at[at, own], v_out.at[at, own])

    def in_turn(*calls):
        def run():
            for call, *indices in calls:
                for index in indices:
                    call(index)

        return run

    for group in (1, 2):
        bias_ref[group] = key_bias((SEQ, 128), mp, count_ref[3 * mp + group - 1], False)
        for part in range(2):
            normalise(group, part, x_ref[pl.ds(row_block(2 * group - 1 + part, mp), HALF), :])
        if group == 1:
            to_peer(3)
            to_peer(4)
    bias_ref[0] = key_bias((SEQ, 128), mp, count_ref[2], True)
    normalise(0, 0, x_ref[pl.ds(row_block(0, mp), HALF), :])
    for index in range(3):
        to_sides(index)
    to_peer(5)
    unit(mp, 1, SEQ)
    in_turn((to_sides, 3, 4), (to_peer, 6))()
    unit(mp, 2, SEQ, between=in_turn((to_core, 0, 1, 2), (to_sides, 5), (to_peer, 7)))
    small_copy.wait_recv()
    keep(sm_ref, sm_out)
    for index in range(3):
        arrive(index)
    keep(wt_ref.at[peer], wt_out.at[peer])
    rows_copy = send(lambda: x_ref.at[pl.ds(own_half, HALF), :], lambda: other_ref, {"mp": peer})
    unit(peer, 1, SEQ, early=in_turn((to_sides, 6)), between=in_turn((to_core, 3, 4)))
    in_turn((to_sides, 7))()
    unit(peer, 2, SEQ, early=in_turn((to_core, 5)), between=in_turn((to_core, 6)))
    rows_copy.wait_recv()
    normalise(0, 1, other_ref[...])
    keep(nt_ref, nt_out)
    unit(mp, 0, HALF, between=in_turn((to_core, 7)))
    unit(peer, 0, HALF)
    keep(lse_ref, lse_out)
    for index in range(3, 8):
        arrive(index)
    for copy in remote:
        copy.wait_send()
    for copy in local:
        copy.wait()


def forward(key_count, w_qkv, w_proj, w_up, w_down, small, patches, vec_params):
    ext = 3 * SEQ
    vmem, hbm = pl.BlockSpec(memory_space=pltpu.VMEM), pl.BlockSpec(memory_space=pl.ANY)
    return pl.pallas_call(
        forward_kernel,
        out_shape=[
            sds((2, 3, 256, 512), BF), sds((2, 256, 512), BF), sds((2, 512, 1024), BF),
            sds((2, 1024, 512), BF), sds((2, 8, 1024), F32),
            sds((512, ext), BF), sds((512, ext), BF), sds((512, ext), BF), sds((ext, 512), BF),
            sds((ext, 512), BF), sds((512, ext), BF), sds((3, 4, 8, SEQ), F32),
        ],
        in_specs=[pl.BlockSpec(memory_space=pltpu.SMEM)] + [vmem] * 7,
        out_specs=[hbm] * 12,
        scratch_shapes=[
            pltpu.VMEM((2, 3, 256, 512), BF), pltpu.VMEM((256, 512), BF), pltpu.VMEM((512, 1024), BF),
            pltpu.VMEM((1024, 512), BF), pltpu.VMEM((2, 8, 1024), F32), pltpu.VMEM((HALF, 512), BF),
            pltpu.VMEM((ext, 512), BF), pltpu.VMEM((512, ext), BF), pltpu.VMEM((512, ext), BF),
            pltpu.VMEM((512, ext), BF), pltpu.VMEM((512, SEQ), BF), pltpu.VMEM((ext, 512), BF),
            pltpu.VMEM((ext, 512), BF), pltpu.VMEM((512, ext), BF), pltpu.VMEM((3, 4, 8, SEQ), F32),
            pltpu.VMEM((3, SEQ, 128), BF), pltpu.VMEM((2, SEQ, SEQ), F32),
            pltpu.SemaphoreType.DMA((34,)), pltpu.SemaphoreType.DMA((34,)), pltpu.SemaphoreType.DMA((40,)),
        ],
        compiler_params=pltpu.CompilerParams(
            collective_id=0, has_side_effects=True, vmem_limit_bytes=VMEM_LIMIT
        ),
        name="forward",
    )(key_count, w_qkv, w_proj, w_up, w_down, small, patches, vec_params)


def mlp_kernel(
    x_ref, dy_ref, ot_ref, wp_ref, wu_ref, wd_ref, vec_ref, small_ref,
    act_ref, dres_ref, dot_ref, gd_ref, gu_ref, gp_ref, vsum_ref, bsum_ref,
    res_ref, n2_ref, out_ref, dn_ref, hid_ref, dup_ref, dyc_ref, br_ref,
):
    step = pl.program_id(0)
    mp = lax.axis_index("mp")
    gain, shift = vec_ref[2:3, :], vec_ref[3:4, :]
    w_proj = wp_ref[...].reshape(512, 512)

    def rows(index):
        return pl.ds(pl.multiple_of(index * HALF, HALF), HALF)

    @pl.when(step == 0)
    def _():
        def body(index, carry):
            x_rows = x_ref[pl.ds(row_block(index, mp), HALF), :].astype(F32)
            mixed = ot_ref[:, pl.ds(ext_cols(index), HALF)]
            resid = x_rows + mm_tn(mixed, w_proj) + vec_ref[4:5, :]
            res_ref[rows(index), :] = resid
            n2_ref[rows(index), :] = layer_norm_rows(resid, gain, shift)[0].astype(BF)
            out_ref[rows(index), :] = resid + vec_ref[5:6, :]
            dn_ref[rows(index), :] = jnp.zeros((HALF, 512), F32)
            dyc_ref[rows(index), :] = dy_ref[pl.ds(row_block(index, mp), HALF), :]
            return carry

        lax.fori_loop(0, 5, body, 0)

    w_up, w_down = wu_ref[0], wd_ref[0]
    up_bias = small_ref[step // 2, 0:1, pl.ds(pl.multiple_of(lax.rem(step, 2) * 512, 512), 512)]

    def body(index, total):
        at = rows(index)
        up_pre = mm_nn(n2_ref[at, :], w_up) + up_bias
        cumulative = 0.5 * (1.0 + lax.erf(up_pre * (0.5**0.5)))
        density = jnp.exp(-0.5 * up_pre * up_pre) * 0.3989422804014327
        hidden = (up_pre * cumulative).astype(BF)
        hid_ref[at, :] = hidden
        out_ref[at, :] += mm_nn(hidden, w_down)
        slope = cumulative + up_pre * density
        dup = (mm_nt(dyc_ref[at, :], w_down) * slope).astype(BF)
        dup_ref[at, :] = dup
        dn_ref[at, :] += mm_nt(dup, w_up)
        return total + jnp.sum(dup.astype(F32).reshape(HALF // 8, 8, 512), axis=0)

    total = lax.fori_loop(0, 5, body, jnp.zeros((8, 512), F32))
    bsum_ref[0] = total
    gd_ref[0] = mm_tn(hid_ref[...], dyc_ref[...]).astype(BF)
    gu_ref[0] = mm_tn(n2_ref[...], dup_ref[...]).astype(BF)

    @pl.when(step == 3)
    def _():
        vsum_ref[...] = jnp.zeros_like(vsum_ref)

        def body(index, carry):
            at = rows(index)
            act_ref[pl.ds(row_block(index, mp), HALF), :] = out_ref[at, :].astype(BF)
            _, unit, inverse = layer_norm_rows(res_ref[at, :], gain, shift)
            dn = dn_ref[at, :]
            dy = dyc_ref[at, :].astype(F32)
            dres = dy + layer_norm_back(dn, unit, inverse, gain)
            dres_ref[at, :] = dres
            branch = dres.astype(BF)
            br_ref[at, :] = branch
            dot_ref[:, pl.ds(ext_cols(index), HALF)] = mm_nt(w_proj, branch).astype(BF)
            sums = [dn * unit, dn, branch.astype(F32), dy]
            for place, value in enumerate(sums):
                vsum_ref[place] += jnp.sum(value.reshape(HALF // 8, 8, 512), axis=0)
            return carry

        lax.fori_loop(0, 5, body, 0)
        mixed = jnp.concatenate([ot_ref[:, 0:HALF], ot_ref[:, SEQ:]], axis=1)
        gp_ref[...] = mm_nn(mixed, br_ref[...]).astype(BF).reshape(2, 256, 512)


def mlp(patches, cotangent, ot, wp, wu, wd, vec_params, small):
    rows = patches.shape[0]
    ext = 3 * SEQ
    up_spec = pl.BlockSpec((1, 512, 512), lambda f: (f // 2, 0, f % 2))
    down_spec = pl.BlockSpec((1, 512, 512), lambda f: (f // 2, f % 2, 0))
    return pl.pallas_call(
        mlp_kernel,
        grid=(4,),
        out_shape=[
            sds((rows, 512), BF), sds((rows, 512), F32), sds((512, ext), BF), sds((2, 1024, 512), BF),
            sds((2, 512, 1024), BF), sds((2, 256, 512), BF), sds((4, 8, 512), F32), sds((4, 8, 512), F32),
        ],
        in_specs=[
            full_spec((rows, 512)), full_spec((rows, 512)), full_spec((512, ext)), full_spec(wp.shape),
            up_spec, down_spec, full_spec(vec_params.shape), full_spec(small.shape),
        ],
        out_specs=[
            full_spec((rows, 512)), full_spec((rows, 512)), full_spec((512, ext)), down_spec, up_spec,
            full_spec((2, 256, 512)), full_spec((4, 8, 512)), pl.BlockSpec((1, 8, 512), lambda f: (f, 0, 0)),
        ],
        scratch_shapes=[
            pltpu.VMEM((rows, 512), F32), pltpu.VMEM((rows, 512), BF), pltpu.VMEM((rows, 512), F32),
            pltpu.VMEM((rows, 512), F32), pltpu.VMEM((rows, 512), BF), pltpu.VMEM((rows, 512), BF),
            pltpu.VMEM((rows, 512), BF), pltpu.VMEM((rows, 512), BF),
        ],
        compiler_params=pltpu.CompilerParams(vmem_limit_bytes=VMEM_LIMIT),
        name="mlp",
    )(patches, cotangent, ot, wp, wu, wd, vec_params, small)


SCHEDULE = (
    (
        ("F", 0, 0), ("F", 1, 0), ("F", 2, 0), ("F", 3, 0), ("F", 4, 0), ("O", 0, 0), ("O", 1, 0),
        ("O", 2, 0), ("O", 3, 0), ("O", 4, 0),
    ),
    (
        ("F", 0, 1),
    ),
    (
    ),
    (
        ("F", 1, 1),
    ),
    (
        ("O", 0, 1),
    ),
    (
    ),
    (
        ("F", 2, 1),
    ),
    (
    ),
    (
        ("F", 5, 0), ("O", 0, 2), ("O", 1, 1),
    ),
    (
        ("F", 3, 1),
    ),
    (
    ),
    (
        ("F", 4, 1), ("O", 0, 3), ("O", 2, 1),
    ),
    (
        ("F", 6, 0), ("O", 1, 2),
    ),
    (
        ("F", 5, 1), ("O", 0, 4), ("O", 2, 2),
    ),
    (
        ("O", 3, 1),
    ),
    (
        ("F", 6, 1), ("O", 1, 3),
    ),
    (
        ("O", 0, 5), ("O", 2, 3), ("O", 4, 1), ("O", 5, 0),
    ),
    (
        ("O", 1, 4),
    ),
    (
        ("O", 3, 2), ("O", 5, 1),
    ),
    (
        ("O", 0, 6), ("O", 4, 2),
    ),
    (
        ("O", 1, 5), ("O", 6, 0),
    ),
    (
    ),
    (
        ("O", 2, 4),
    ),
    (
        ("O", 0, 7), ("O", 3, 3), ("O", 6, 1),
    ),
    (
    ),
    (
        ("O", 0, 8), ("O", 1, 6), ("O", 4, 3), ("O", 5, 2),
    ),
    (
        ("O", 2, 5), ("O", 6, 2), ("O", 3, 4), ("O", 4, 4), ("small", 0), ("O", 5, 3), ("O", 1, 7),
        ("O", 2, 6), ("small", 1), ("O", 6, 3), ("O", 1, 8), ("small", 2), ("O", 3, 5), ("O", 4, 5),
        ("small", 3), ("O", 5, 4), ("O", 2, 7), ("O", 6, 4), "square", ("small", 4), ("O", 2, 8), ("O", 3, 6),
        ("O", 4, 6), ("square", 0), ("O", 5, 5), ("square", 1), ("O", 6, 5), ("O", 3, 7), ("square", 2),
        ("O", 5, 6), ("O", 6, 6), ("O", 4, 7), ("O", 3, 8), ("square", 3), ("O", 4, 8), ("square", 4),
        ("O", 5, 7), ("O", 5, 8), ("O", 6, 7), ("O", 6, 8),
    ),
)


class Transfers:
    def __init__(self, send_sem, recv_sem):
        self.sems = (send_sem, recv_sem)
        self.all = {}

    def make(self, key):
        index, src, dst, target = self.all[key]
        return pltpu.make_async_remote_copy(
            src_ref=src(), dst_ref=dst(), send_sem=self.sems[0].at[index], recv_sem=self.sems[1].at[index],
            device_id=target, device_id_type=MESH,
        )

    def plan(self, key, src, dst, target):
        self.all[key] = (len(self.all), src, dst, target)

    def start(self, key, *views):
        if views:
            self.plan(key, *views)
        self.make(key).start()

    def arrive(self, key):
        self.make(key).wait_recv()

    def finish(self):
        for key in self.all:
            self.make(key).wait_send()


class Loads:
    def __init__(self, sem):
        self.sem = sem
        self.all = {}

    def make(self, key):
        index, src, dst = self.all[key]
        return pltpu.make_async_copy(src(), dst(), self.sem.at[index])

    def plan(self, key, src, dst):
        self.all[key] = (len(self.all), src, dst)

    def start(self, key, *views):
        if views:
            self.plan(key, *views)
        self.make(key).start()

    def wait(self, key):
        self.make(key).wait()


def cut(ref, start, size):
    rows = pl.ds(pl.multiple_of(start, 16), size)
    return ref.at[:, rows, :] if len(ref.shape) == 3 else ref.at[rows, :]


PIECES = ((512, 512), (512, 512), (512, 512), (512, 512), (256, 512), (3, 512, 128), (3, 512, 128))


def piece_rows(index, size):
    return (*PIECES[index][:-2], PIECES[index][-2] // size, PIECES[index][-1])


def backward_kernel(
    count_ref, qt_in, kt_in, dot_in, ot_in, k_in, v_in, lse_ref, nt_in, wt_in,
    gd_in, gu_in, gp_in, x_in, dres_in, vec_ref, two_ref, up_sum_ref,
    grad_out, down_out, up_out, proj_out, qkv_out, small_out, norm_out,
    qt_ref, kt_ref, dot_ref, ot_ref, k_ref, v_ref, nt_ref, wt_ref, x_ref, dres_ref,
    shared_ref, grads_ref, acc_ref, bias_ref, s_ref, dp_ref, g_ref, bsum_ref,
    far_send, far_recv, small_bufs, square_bufs, *rest,
):
    buffers, (send_sem, recv_sem, local_sem) = rest[:-3], rest[-3:]
    dp, mp = lax.axis_index("dp"), lax.axis_index("mp")
    peer = 1 - mp
    core, x_side, z_near, z_far = partners(dp)
    targets = [{"dp": core}, {"mp": peer}, {"dp": x_side}, {"dp": z_near}, {"dp": z_far}]
    bits = [lax.rem(dp, 2), None] + [lax.rem(lax.div(dp, size), 2) for size in (2, 4, 8)]
    sent, loads = Transfers(send_sem, recv_sem), Loads(local_sem)

    def block_at(place):
        return 2 * jnp.where(place < 2, peer, mp) + lax.rem(place, 2)

    def source(index, side):
        if index < 4:
            lanes = slice(index // 2 * 512, index // 2 * 512 + 512)
            return gu_in.at[side, :, lanes] if index % 2 else gd_in.at[side, lanes, :]
        if index == 4:
            return gp_in.at[side]
        return g_ref.at[index - 5 + (0 if side is peer else 2)]

    def result(index):
        if index < 4:
            lanes = slice(index // 2 * 512, index // 2 * 512 + 512)
            return up_out.at[:, lanes] if index % 2 else down_out.at[lanes, :]
        if index == 4:
            return proj_out
        return qkv_out.at[:, :, slice((index - 5) * 128, (index - 5) * 128 + 128)]

    def piece_buffers(index):
        return buffers[9 * index : 9 * index + 9]

    def share(total, upto):
        start, size = 0, total
        for stage in (0, 2, 3, 4):
            if stage <= upto:
                size //= 2
                start = start + bits[stage] * size
        return start, size

    for place in range(4):
        block = block_at(place)
        rows = pl.ds(pl.multiple_of(block * 128, 128), 128)
        for name, src, dst in (
            ("qt", qt_in, qt_ref), ("kt", kt_in, kt_ref), ("dot", dot_in, dot_ref), ("ot", ot_in, ot_ref)
        ):
            loads.start(
                (name, place), lambda src=src, rows=rows: src.at[rows, :],
                lambda dst=dst, place=place: dst.at[place],
            )
        for name, src, dst in (("k", k_in, k_ref), ("v", v_in, v_ref)):
            loads.start(
                (name, place), lambda src=src, rows=rows: src.at[:, rows],
                lambda dst=dst, place=place: dst.at[place],
            )
        if place == 0:
            loads.start("wt", lambda: wt_in, lambda: wt_ref)
    loads.start("nt", lambda: nt_in, lambda: nt_ref)
    for index in range(5):
        total = PIECES[index][-2]
        for side, slot in ((peer, 0), (mp, 2)):
            loads.start(
                ("kept", index, slot),
                lambda index=index, side=side, total=total: cut(
                    source(index, side), bits[0] * (total // 2), total // 2
                ),
                lambda index=index, slot=slot: piece_buffers(index)[slot],
            )
    loads.start("x", lambda: x_in, lambda: x_ref)
    loads.start("dres", lambda: dres_in, lambda: dres_ref)
    greet(targets)

    def plan_piece(index):
        total = PIECES[index][-2]
        half = total // 2
        kept = bits[0] * half
        fore, fore_core, own, own_core, own_peer, own_x, own_near, own_far, out = piece_buffers(index)
        away = (1 - bits[0]) * half
        sent.plan(("F", index, 0), lambda: cut(source(index, peer), away, half), lambda: fore_core, targets[0])
        sent.plan(("F", index, 1), lambda: fore, lambda: own_peer, targets[1])
        sent.plan(("O", index, 0), lambda: cut(source(index, mp), away, half), lambda: own_core, targets[0])
        for stage, landing in ((1, own_x), (2, own_near), (3, own_far)):
            level = stage + 1
            outer, outer_size = share(total, level - 1)
            size = outer_size // 2
            start = outer - kept + (1 - bits[level]) * size
            sent.plan(
                ("O", index, stage), lambda start=start, size=size: cut(own, start, size),
                lambda landing=landing: landing, targets[level],
            )
        for stage, level in ((4, 4), (5, 3), (6, 2), (7, 0)):
            start, size = share(total, level)
            where = lambda start=start, size=size: cut(out, start, size)
            sent.plan(("O", index, stage), where, where, targets[level])
        loads.plan(("out", index), lambda: out, lambda: result(index))

    def event(kind, index, stage):
        total = PIECES[index][-2]
        half = total // 2
        kept = bits[0] * half
        fore, fore_core, own, own_core, own_peer, own_x, own_near, own_far, out = piece_buffers(index)
        if stage > 0:
            sent.arrive((kind, index, stage - 1))
        if kind == "F" and stage == 1:
            if index < 5:
                loads.wait(("kept", index, 0))
                fore[...] += fore_core[...]
            else:
                fore[...] = cut(source(index, peer), kept, half)[...] + fore_core[...]
        elif stage == 1:
            sent.arrive(("F", index, 1))
            if index < 5:
                loads.wait(("kept", index, 2))
                base = own[...]
            else:
                base = cut(source(index, mp), kept, half)[...]
            own[...] = (base.astype(F32) + own_core[...].astype(F32) + own_peer[...].astype(F32)).astype(BF)
        elif 2 <= stage <= 4:
            start, size = share(total, stage)
            landing = (own_x, own_near, own_far)[stage - 2]
            value = cut(own, start - kept, size)[...] + landing[...]
            if stage < 4:
                cut(own, start - kept, size)[...] = value
            else:
                cut(out, start, size)[...] = value
                wide = value.astype(F32)
                square = jnp.sum((wide * wide).reshape(-1, 8, wide.shape[-1]), axis=0)
                folded = square[:, 0:128]
                for lane in range(1, square.shape[1] // 128):
                    folded = folded + square[:, lane * 128 : lane * 128 + 128]
                square_bufs[0, 0] += folded
        if stage == 8:
            loads.start(("out", index))
        else:
            sent.start((kind, index, stage))

    for index in range(7):
        plan_piece(index)

    def run(events):
        for item in events:
            event(*item)

    square_bufs[0, 0] = jnp.zeros((8, 128), F32)
    bias_ref[0] = key_bias((SEQ, 128), mp, count_ref[2], True)
    for group in (1, 2):
        bias_ref[group] = key_bias((SEQ, 128), mp, count_ref[3 * mp + group - 1], False)
    run(SCHEDULE[0])

    def heads(place, group, queries, out, out_base, between):
        block = block_at(place)
        base = pl.multiple_of(group * SEQ, SEQ)
        keys_at, queries_at = pl.ds(base, SEQ), pl.ds(base, queries)
        out_keys = pl.ds(out_base, SEQ)
        out_queries = pl.ds(out_base, queries)
        bias = bias_ref[group]

        def tiles(sub):
            own = slice(sub * HD, sub * HD + HD)
            s_ref[sub % 2, :, :queries] = score_tile(
                k_ref[place, keys_at, :], bias, qt_ref[place, own, queries_at], sub
            )
            dp_ref[sub % 2, :, :queries] = mm_nn(
                v_ref[place, keys_at, :], widen_plain(dot_ref[place, own, queries_at], sub)
            )

        tiles(0)
        for sub in range(4):
            if sub < 3:
                tiles(sub + 1)
            own = slice(sub * HD, sub * HD + HD)
            q_rows, do_rows = qt_ref[place, own, queries_at], dot_ref[place, own, queries_at]
            delta = jnp.sum(
                do_rows.astype(F32) * ot_ref[place, own, queries_at].astype(F32), axis=0, keepdims=True
            )
            probs = jnp.exp2(
                s_ref[sub % 2, :, :queries] - lse_ref[group, block, sub : sub + 1, :queries]
            )
            draw = (probs * (dp_ref[sub % 2, :, :queries] - delta)).astype(BF)
            dq = mm_nn(kt_ref[place, own, keys_at], draw) * (HD ** (-0.5))
            out[own, out_queries] = dq.astype(BF)
            dk = mm_nt(q_rows, draw) * (1.0 / LOG2E)
            out[128 + sub * HD : 160 + sub * HD, out_keys] = dk.astype(BF)
            dv = mm_nt(do_rows, probs.astype(BF))
            out[256 + sub * HD : 288 + sub * HD, out_keys] = dv.astype(BF)
            if sub == 1:
                between()

    def weights_of(place):
        block = block_at(place)
        side, part = lax.div(block, 2), lax.rem(block, 2)
        return wt_ref[side, :, pl.ds(pl.multiple_of(part * 128, 128), 128), :].reshape(384, 512)

    acc_ref[...] = jnp.zeros_like(acc_ref)
    for place in range(4):
        for name in ("qt", "kt", "dot", "ot", "k", "v"):
            loads.wait((name, place))
        if place == 0:
            loads.wait("wt")
        shared_ref[place, 0:128, HALF:SEQ] = jnp.zeros((128, HALF), BF)

    def shared_step(place, carry):
        heads(place, 0, HALF, shared_ref.at[place], 0, lambda: None)
        acc_ref[0:SEQ] += mm_tn(shared_ref[place], weights_of(place))
        for turn in range(4):

            @pl.when(place == turn)
            def _():
                run(SCHEDULE[1 + turn])

        return carry

    lax.fori_loop(0, 4, shared_step, 0)
    far_send[...] = acc_ref[HALF:SEQ].astype(BF)
    sent.start("far", lambda: far_send, lambda: far_recv, targets[1])
    loads.wait("nt")

    def main_step(step, carry):
        place, group = lax.div(step, 2), 1 + lax.rem(step, 2)

        def pump(first):
            for turn in range(8):

                @pl.when(step == turn)
                def _():
                    run(SCHEDULE[first + 2 * turn])

        out_base = pl.multiple_of((group - 1) * SEQ, SEQ)
        heads(place, group, SEQ, grads_ref, out_base, lambda: pump(5))

        @pl.when(group == 2)
        def _():
            for part in range(3):
                rows = slice(part * 128, part * 128 + 128)
                total = mm_nt(nt_ref[:, 0:SEQ], shared_ref[place, rows, :])
                total += mm_nt(nt_ref[:, SEQ:], grads_ref[rows, :])
                g_ref[place, part] = total.astype(BF)
            ones = jnp.ones((8, 2 * SEQ), BF)
            bsum_ref[place] = mm_nt(ones[:, :SEQ], shared_ref[place]) + mm_nt(ones, grads_ref[...])
            acc_ref[SEQ:] += mm_tn(grads_ref[...], weights_of(place))

        pump(6)
        return carry

    lax.fori_loop(0, 8, main_step, 0)

    gain, shift = vec_ref[0:1, :], vec_ref[1:2, :]
    loads.wait("x")
    loads.wait("dres")
    run(SCHEDULE[21])

    def finish_rows(index, dn, sums):
        at = pl.ds(pl.multiple_of(index * HALF, HALF), HALF)
        place = pl.ds(row_block(index, mp), HALF)
        _, unit, inverse = layer_norm_rows(x_ref[place, :].astype(F32), gain, shift)
        grad_out[place, :] = dres_ref[at, :] + layer_norm_back(dn, unit, inverse, gain)
        folded = [jnp.sum(value.reshape(HALF // 8, 8, 512), axis=0) for value in (dn * unit, dn)]
        return sums[0] + folded[0], sums[1] + folded[1]

    def finish_step(index, sums):
        sums = finish_rows(
            index, acc_ref[pl.ds(pl.multiple_of(HALF * index + HALF, HALF), HALF), :], sums
        )
        for turn in range(1, 5):

            @pl.when(index == turn)
            def _():
                run(SCHEDULE[21 + turn])

        return sums

    zero = jnp.zeros((8, 512), F32)
    sums = lax.fori_loop(1, 5, finish_step, (zero, zero))
    sent.arrive("far")
    sums = finish_rows(0, acc_ref[0:HALF] + far_recv[...].astype(F32), sums)

    def small_row(place, value):
        small_bufs[0, 0, place : place + 1, :] = value

    small_bufs[0, 0] = jnp.zeros((16, 512), F32)
    for place in range(4):
        lanes = pl.ds(pl.multiple_of(block_at(place) * 128, 128), 128)
        small_bufs[0, 0, 0:1, lanes] = bsum_ref[place, 0:1, 0:128]
        small_bufs[0, 0, 1:2, lanes] = bsum_ref[place, 0:1, 256:384]
        small_row(2 + place, jnp.sum(up_sum_ref[place], axis=0, keepdims=True))
        small_row(8 + place, jnp.sum(two_ref[place], axis=0, keepdims=True))
    for place in range(2):
        small_row(6 + place, jnp.sum(sums[place], axis=0, keepdims=True))

    def small_start(stage):
        sent.start(
            ("small", stage), lambda: small_bufs.at[0, stage], lambda: small_bufs.at[1, stage], targets[stage]
        )

    def small_end(stage):
        sent.arrive(("small", stage))
        value = small_bufs[0, stage] + small_bufs[1, stage]
        if stage < 4:
            small_bufs[0, stage + 1] = value
            small_start(stage + 1)
        else:
            small_out[...] = value

    order = (4, 3, 2, 0, 1)

    def square_start(place):
        sent.start(
            ("square", place), lambda: square_bufs.at[0, place], lambda: square_bufs.at[1, place],
            targets[order[place]],
        )

    def square_end(place):
        sent.arrive(("square", place))
        value = square_bufs[0, place] + square_bufs[1, place]
        if place < 4:
            square_bufs[0, place + 1] = value
            square_start(place + 1)
        else:
            total = jnp.sum(small_out[...] * small_out[...]) + jnp.sum(value)
            norm_out[...] = jnp.sqrt(jnp.full((8, 128), total, F32))

    small_start(0)
    for item in SCHEDULE[26]:
        if item == "square":
            square_start(0)
        elif item[0] == "small":
            small_end(item[1])
        elif item[0] == "square":
            square_end(item[1])
        else:
            event(*item)
    sent.finish()
    for index in range(7):
        loads.wait(("out", index))


def backward(key_count, qt, kt, dot, ot, k, v, lse, nt, wt, gd, gu, gp, patches, dres, vec_params, two, ups):
    ext, rows = 3 * SEQ, patches.shape[0]
    vmem, hbm = pl.BlockSpec(memory_space=pltpu.VMEM), pl.BlockSpec(memory_space=pl.ANY)
    buffers = []
    for index in range(7):
        for size in (2, 2, 2, 2, 2, 4, 8, 16, 1):
            buffers.append(pltpu.VMEM(piece_rows(index, size), BF))
    return pl.pallas_call(
        backward_kernel,
        out_shape=[
            sds((rows, 512), F32), sds((1024, 512), BF), sds((512, 1024), BF), sds((256, 512), BF),
            sds((3, 512, 256), BF), sds((16, 512), F32), sds((8, 128), F32),
        ],
        in_specs=[pl.BlockSpec(memory_space=pltpu.SMEM)] + [hbm] * 6 + [vmem] + [hbm] * 7 + [vmem] * 3,
        out_specs=[vmem] + [hbm] * 4 + [vmem] * 2,
        scratch_shapes=[
            *[pltpu.VMEM((4, 128, ext), BF)] * 4, *[pltpu.VMEM((4, ext, 128), BF)] * 2,
            pltpu.VMEM((512, ext), BF), pltpu.VMEM((2, 3, 256, 512), BF), pltpu.VMEM((rows, 512), BF),
            pltpu.VMEM((rows, 512), F32), pltpu.VMEM((4, 384, SEQ), BF), pltpu.VMEM((384, 2 * SEQ), BF),
            pltpu.VMEM((ext, 512), F32), pltpu.VMEM((3, SEQ, 128), BF), pltpu.VMEM((2, SEQ, SEQ), F32),
            pltpu.VMEM((2, SEQ, SEQ), F32), pltpu.VMEM((4, 3, 512, 128), BF), pltpu.VMEM((4, 8, 384), F32),
            pltpu.VMEM((HALF, 512), BF), pltpu.VMEM((HALF, 512), BF), pltpu.VMEM((2, 5, 16, 512), F32),
            pltpu.VMEM((2, 5, 8, 128), F32), *buffers, pltpu.SemaphoreType.DMA((81,)),
            pltpu.SemaphoreType.DMA((81,)), pltpu.SemaphoreType.DMA((48,)),
        ],
        compiler_params=pltpu.CompilerParams(
            collective_id=1, has_side_effects=True, vmem_limit_bytes=VMEM_LIMIT
        ),
        name="backward",
    )(key_count, qt, kt, dot, ot, k, v, lse, nt, wt, gd, gu, gp, patches, dres, vec_params, two, ups)


def adam_kernel(norm_ref, *refs):
    factor = jnp.minimum(1.0, CLIP_NORM / (norm_ref[0:1, 0:1] + 1e-06))
    for index in range(4):
        weight_ref, one_ref, two_ref, grad_ref = refs[4 * index : 4 * index + 4]
        outs = refs[16 + 3 * index : 19 + 3 * index]
        results = adam_update(
            weight_ref[...], grad_ref[...].astype(F32) * factor, one_ref[...], two_ref[...],
            MATRIX_RATE, DECAY_RATE,
        )
        for out, value in zip(outs, results):
            out[...] = value


def adam_matrices(norm, groups):
    steps = 8
    in_specs, out_specs, out_shape, args = [full_spec((8, 128))], [], [], [norm]
    for group in groups:
        rows, width = group[0].shape
        spec = pl.BlockSpec((rows // steps, width), lambda i: (i, 0))
        in_specs += [spec] * 4
        out_specs += [spec] * 3
        out_shape += [sds((rows, width), F32)] * 3
        args += list(group)
    outs = pl.pallas_call(
        adam_kernel,
        grid=(steps,),
        out_shape=out_shape,
        in_specs=in_specs,
        out_specs=out_specs,
        compiler_params=pltpu.CompilerParams(vmem_limit_bytes=VMEM_LIMIT),
        name="adam_matrices",
    )(*args)
    return [outs[3 * index : 3 * index + 3] for index in range(len(groups))]


IN_SPECS = (
            P(("dp", "mp"), None),
            P(("dp", "mp"), None),
            P("dp"),
            P(None, None, "mp"),
            P("mp", None),
            P(None, "mp"),
            P("mp", None),
            P(None, "mp"),
            P("mp"),
            P(),
            P(None, None, "mp"),
            P(None, None, "mp"),
            P("mp", None),
            P("mp", None),
            P(None, "mp"),
            P(None, "mp"),
            P("mp", None),
            P("mp", None),
            P(None, "mp"),
            P(None, "mp"),
            P("mp"),
            P("mp"),
            P(),
            P(),
        )
OUT_SPECS = (
            P(("dp", "mp"), None),
            P(("dp", "mp"), None),
            P(),
            P(None, None, "mp"),
            P(None, None, "mp"),
            P(None, None, "mp"),
            P("mp", None),
            P("mp", None),
            P("mp", None),
            P(None, "mp"),
            P(None, "mp"),
            P(None, "mp"),
            P("mp", None),
            P("mp", None),
            P("mp", None),
            P(None, "mp"),
            P(None, "mp"),
            P(None, "mp"),
            P("mp"),
            P("mp"),
            P("mp"),
            P(),
            P(),
            P(),
        )


def paired(
    patches, cotangent, key_count, w_qkv, w_proj, w_up, w_down, qv_bias, up_bias, vec_params,
    first_qkv, second_qkv, first_proj, second_proj, first_up, second_up, first_down, second_down,
    first_qv_bias, second_qv_bias, first_up_bias, second_up_bias, first_vec, second_vec,
):
    mp = lax.axis_index("mp")
    small = jnp.concatenate(
        [up_bias[None, :], jnp.pad(qv_bias, ((0, 0), (0, 768))), jnp.zeros((5, 1024), F32)], axis=0
    )
    wt, wp, wu, wd, small_all, nt, qt, kt, k, v, ot, lse = forward(
        key_count, w_qkv, w_proj, w_up, w_down, small, patches, vec_params
    )
    activations, dres, dot, g_down, g_up, g_proj, vsum_two, up_sums = mlp(
        patches, cotangent, ot, wp, wu, wd, vec_params, small_all
    )
    input_grad, down, up, proj, qkv, small_total, norm = backward(
        key_count, qt, kt, dot, ot, k, v, lse, nt, wt, g_down, g_up, g_proj, patches, dres, vec_params,
        vsum_two, up_sums,
    )
    qkv = qkv.reshape(1536, 256)
    flat = lambda array: array.reshape(-1, array.shape[-1])
    groups = [
        (flat(w_qkv), flat(first_qkv), flat(second_qkv), qkv),
        (w_proj, first_proj, second_proj, proj),
        (w_up, first_up, second_up, up),
        (w_down, first_down, second_down, down),
    ]
    new_qkv, new_proj, new_up, new_down = adam_matrices(norm, groups)
    grad_norm = norm[0, 0]
    factor = jnp.minimum(1.0, CLIP_NORM / (grad_norm + 1e-06))
    qv_total = lax.dynamic_slice_in_dim(small_total[0:2], mp * 256, 256, 1)
    up_total = lax.dynamic_slice_in_dim(small_total[2:6].reshape(-1), mp * 1024, 1024, 0)
    new_qvb = adam_update(qv_bias, qv_total * factor, first_qv_bias, second_qv_bias, VECTOR_RATE, 0.0)
    new_upb = adam_update(up_bias, up_total * factor, first_up_bias, second_up_bias, VECTOR_RATE, 0.0)
    new_vec = adam_update(
        vec_params, small_total[6:12] * factor, first_vec, second_vec, VECTOR_RATE, 0.0
    )
    return (
        activations, input_grad, grad_norm, *[array.reshape(w_qkv.shape) for array in new_qkv],
        *new_proj, *new_up, *new_down, *new_qvb, *new_upb, *new_vec,
    )


def fits_pairs(mesh, args):
    if dict(mesh.shape) != {"dp": 16, "mp": 2}:
        return False
    return args[0].shape == (40960, 512) and args[2].shape == (80,)


def solution(mesh):
    def run(*args):
        body = paired if fits_pairs(mesh, args) else local
        return jax.shard_map(body, mesh=mesh, in_specs=IN_SPECS, out_specs=OUT_SPECS, check_vma=False)(*args)

    return run
```

```python
import jax
import jax.numpy as jnp
from jax import lax
from jax.experimental import pallas as pl
from jax.experimental.pallas import tpu as pltpu
from jax.sharding import PartitionSpec as P

HD = 32
ADAM_STEP = 10


NORM_EPS = 1e-06
BETA_FIRST = 0.9
BETA_SECOND = 0.95
ADAM_EPS = 1e-08
DECAY_RATE = 0.05
MATRIX_RATE = 0.1
VECTOR_RATE = 0.8
CLIP_NORM = 1.0
MASK_FILL = -1e30
LOG2E = 1.4426950408889634
BF = jnp.bfloat16
F32 = jnp.float32
MESH = pl.DeviceIdType.MESH
SEQ = 512
HALF = 256
VMEM_LIMIT = 58 * 1024 * 1024


def mm_nn(left, right):
    return lax.dot_general(left, right, (((1,), (0,)), ((), ())), preferred_element_type=F32)


def mm_nt(left, right):
    return lax.dot_general(left, right, (((1,), (1,)), ((), ())), preferred_element_type=F32)


def mm_tn(left, right):
    return lax.dot_general(left, right, (((0,), (0,)), ((), ())), preferred_element_type=F32)


def partners(dp):
    core = dp + 1 - 2 * lax.rem(dp, 2)
    x_side = dp + 2 - 4 * lax.rem(lax.div(dp, 2), 2)
    z_near = dp + 4 - 8 * lax.rem(lax.div(dp, 4), 2)
    z_far = dp + 8 - 16 * lax.rem(lax.div(dp, 8), 2)
    return core, x_side, z_near, z_far


def greet(targets):
    barrier = pltpu.get_barrier_semaphore()
    for target in targets:
        pl.semaphore_signal(barrier, inc=1, device_id=target, device_id_type=MESH)
    pl.semaphore_wait(barrier, len(targets))


def full_spec(shape):
    return pl.BlockSpec(shape, lambda *_: (0,) * len(shape))


def sds(shape, dtype):
    return jax.ShapeDtypeStruct(shape, dtype)


def row_block(index, mp):
    return pl.multiple_of(lax.rem(index + 4 * (1 - mp), 5) * HALF, HALF)


def ext_cols(index):
    return pl.multiple_of(jnp.where(index == 0, 0, HALF + HALF * index), HALF)


def norm_forward(values, norm_gain, norm_shift):
    row_mean = jnp.mean(values, axis=-1, keepdims=True)
    centred = values - row_mean
    inverse = lax.rsqrt(jnp.mean(centred * centred, axis=-1, keepdims=True) + NORM_EPS)
    normed = centred * inverse
    return (normed * norm_gain + norm_shift, normed, inverse)


def norm_backward(grad_rows, normed, inverse, norm_gain):
    scaled = grad_rows * norm_gain
    centre_term = jnp.mean(scaled, axis=-1, keepdims=True)
    slope_term = jnp.mean(scaled * normed, axis=-1, keepdims=True)
    return inverse * (scaled - centre_term - normed * slope_term)


def exact_gelu(values):
    return jax.nn.gelu(values, approximate=False)


def key_mask(key_count, length):
    position = lax.broadcasted_iota(jnp.int32, (1, 1, 1, length), 3)
    return position < key_count[:, None, None, None]


def masked_scores(queries, key_rows, key_count):
    raw_scores = jnp.einsum(
        "sqhe,skhe->shqk", queries, key_rows, preferred_element_type=jnp.float32
    )
    scaled = raw_scores * queries.shape[-1] ** (-0.5)
    return jnp.where(key_mask(key_count, key_rows.shape[1]), scaled, MASK_FILL)


def attend_backward(queries, key_rows, value_rows, key_count, log_total, attended_grad):
    scores = masked_scores(queries, key_rows, key_count)
    probs = jnp.exp(scores - log_total)
    probs_low = probs.astype(jnp.bfloat16)
    probs_grad = jnp.einsum(
        "sqhe,skhe->shqk", attended_grad, value_rows, preferred_element_type=jnp.float32
    )
    score_grad = probs * (probs_grad - jnp.sum(probs_grad * probs, axis=-1, keepdims=True))
    visible = key_mask(key_count, key_rows.shape[1])
    raw_grad = jnp.where(visible, score_grad * queries.shape[-1] ** (-0.5), 0.0).astype(
        jnp.bfloat16
    )
    query_grad = jnp.einsum(
        "shqk,skhe->sqhe", raw_grad, key_rows, preferred_element_type=jnp.float32
    )
    key_grad = jnp.einsum("shqk,sqhe->skhe", raw_grad, queries, preferred_element_type=jnp.float32)
    value_grad = jnp.einsum(
        "shqk,sqhe->skhe", probs_low, attended_grad, preferred_element_type=jnp.float32
    )
    return jnp.stack([query_grad, key_grad, value_grad])


def own_slice(values, own_start, own_rows):
    return lax.dynamic_slice_in_dim(values, own_start, own_rows, 0)


def contract_rows(left, right):
    return lax.dot_general(
        left, right, (((0,), (0,)), ((), ())), preferred_element_type=jnp.float32
    )


def contract_cols(left, right):
    return lax.dot_general(
        left, right, (((1,), (1,)), ((), ())), preferred_element_type=jnp.float32
    )


def adam_update(weight, gradient, moment_one, moment_two, step_rate, decay_rate):
    first_new = BETA_FIRST * moment_one + (1.0 - BETA_FIRST) * gradient
    second_new = BETA_SECOND * moment_two + (1.0 - BETA_SECOND) * gradient * gradient
    first_hat = first_new / (1.0 - BETA_FIRST**ADAM_STEP)
    second_hat = second_new / (1.0 - BETA_SECOND**ADAM_STEP)
    weight_new = weight - step_rate * (
        first_hat / (jnp.sqrt(second_hat) + ADAM_EPS) + decay_rate * weight
    )
    return (weight_new, first_new, second_new)


def local(
    patches,
    cotangent,
    key_count,
    w_qkv,
    w_proj,
    w_up,
    w_down,
    qv_bias,
    up_bias,
    vec_params,
    first_qkv,
    second_qkv,
    first_proj,
    second_proj,
    first_up,
    second_up,
    first_down,
    second_down,
    first_qv_bias,
    second_qv_bias,
    first_up_bias,
    second_up_bias,
    first_vec,
    second_vec,
):
    own_rows = patches.shape[0]
    seq_count = key_count.shape[0]
    own_start = lax.axis_index("mp") * own_rows
    local_width = w_proj.shape[0]
    local_heads = local_width // HD
    own_grad = cotangent.astype(jnp.float32)
    qkv_low = w_qkv.astype(jnp.bfloat16)
    proj_low = w_proj.astype(jnp.bfloat16)
    up_low = w_up.astype(jnp.bfloat16)
    down_low = w_down.astype(jnp.bfloat16)
    gain_one, shift_one = (vec_params[0], vec_params[1])
    gain_two, shift_two = (vec_params[2], vec_params[3])
    proj_shift, down_shift = (vec_params[4], vec_params[5])
    qkv_shift = jnp.stack([qv_bias[0], jnp.zeros_like(qv_bias[0]), qv_bias[1]])[:, None, :]
    gathered, grad_all = (
        lax.all_gather(patches, "mp", axis=0, tiled=True),
        lax.all_gather(cotangent, "mp", axis=0, tiled=True),
    )
    whole_rows = gathered.astype(jnp.float32)
    normed_all, unit_one, inverse_one = norm_forward(whole_rows, gain_one, shift_one)
    norm_one = normed_all.astype(jnp.bfloat16)
    projected = (
        jnp.einsum("td,cde->cte", norm_one, qkv_low, preferred_element_type=jnp.float32) + qkv_shift
    )
    shaped = projected.astype(jnp.bfloat16).reshape(3, seq_count, -1, local_heads, HD)
    queries, key_rows, value_rows = (shaped[0], shaped[1], shaped[2])
    scores = masked_scores(queries, key_rows, key_count)
    top_score = jnp.max(scores, axis=-1, keepdims=True)
    log_total = top_score + jnp.log(jnp.sum(jnp.exp(scores - top_score), axis=-1, keepdims=True))
    probs_low = jnp.exp(scores - log_total).astype(jnp.bfloat16)
    attended = jnp.einsum(
        "shqk,skhe->sqhe", probs_low, value_rows, preferred_element_type=jnp.float32
    )
    attended_low = attended.astype(jnp.bfloat16).reshape(-1, local_width)
    proj_part = jnp.dot(attended_low, proj_low, preferred_element_type=jnp.float32)
    resid_all = whole_rows + lax.psum(proj_part, "mp") + proj_shift
    mid_all, unit_two, inverse_two = norm_forward(resid_all, gain_two, shift_two)
    norm_two = mid_all.astype(jnp.bfloat16)
    up_pre = jnp.dot(norm_two, up_low, preferred_element_type=jnp.float32) + up_bias
    hidden_full, gelu_pull = jax.vjp(exact_gelu, up_pre)
    hidden_low = hidden_full.astype(jnp.bfloat16)
    down_part = jnp.dot(hidden_low, down_low, preferred_element_type=jnp.float32)
    out_all = (
        resid_all + lax.psum(down_part.astype(jnp.bfloat16), "mp").astype(jnp.float32) + down_shift
    )
    block_out = own_slice(out_all, own_start, own_rows)
    activations = block_out.astype(jnp.bfloat16)
    down_grad = contract_rows(hidden_low, grad_all)
    hidden_grad = contract_cols(grad_all, down_low)
    up_grad_rows = gelu_pull(hidden_grad)[0].astype(jnp.bfloat16)
    up_grad = contract_rows(norm_two, up_grad_rows)
    up_bias_grad = jnp.sum(up_grad_rows.astype(jnp.float32), axis=0)
    mid_part = contract_cols(up_grad_rows, up_low)
    mid_all_grad = lax.psum(mid_part.astype(jnp.bfloat16), "mp").astype(jnp.float32)
    resid_all_grad = grad_all.astype(jnp.float32) + norm_backward(
        mid_all_grad, unit_two, inverse_two, gain_two
    )
    branch_low = resid_all_grad.astype(jnp.bfloat16)
    own_branch = own_slice(branch_low, own_start, own_rows)
    mid_grad = own_slice(mid_all_grad, own_start, own_rows)
    mid_unit = own_slice(unit_two, own_start, own_rows)
    proj_grad = contract_rows(attended_low, branch_low)
    attended_grad = (
        contract_cols(branch_low, proj_low)
        .astype(jnp.bfloat16)
        .reshape(seq_count, -1, local_heads, HD)
    )
    qkv_grads = attend_backward(queries, key_rows, value_rows, key_count, log_total, attended_grad)
    qkv_grad_rows = qkv_grads.reshape(3, -1, local_width).astype(jnp.bfloat16)
    qkv_grad = jnp.einsum(
        "td,cte->cde", norm_one, qkv_grad_rows, preferred_element_type=jnp.float32
    )
    qkv_grad_sums = jnp.sum(qkv_grad_rows.astype(jnp.float32), axis=1)
    qv_bias_grad = jnp.stack([qkv_grad_sums[0], qkv_grad_sums[2]])
    first_part = jnp.einsum(
        "cte,cde->td", qkv_grad_rows, qkv_low, preferred_element_type=jnp.float32
    )
    first_all = lax.psum(first_part.astype(jnp.bfloat16), "mp").astype(jnp.float32)
    input_all = resid_all_grad + norm_backward(first_all, unit_one, inverse_one, gain_one)
    input_grad = own_slice(input_all, own_start, own_rows)
    own_first_grad = own_slice(first_all, own_start, own_rows)
    own_unit_one = own_slice(unit_one, own_start, own_rows)
    vec_grad = jnp.stack(
        [
            jnp.sum(own_first_grad * own_unit_one, axis=0),
            jnp.sum(own_first_grad, axis=0),
            jnp.sum(mid_grad * mid_unit, axis=0),
            jnp.sum(mid_grad, axis=0),
            jnp.sum(own_branch.astype(jnp.float32), axis=0),
            jnp.sum(own_grad, axis=0),
        ]
    )
    summed = (
        lax.psum(qkv_grad.astype(jnp.bfloat16), "dp").astype(jnp.float32),
        lax.psum(proj_grad.astype(jnp.bfloat16), "dp").astype(jnp.float32),
        lax.psum(up_grad.astype(jnp.bfloat16), "dp").astype(jnp.float32),
        lax.psum(down_grad.astype(jnp.bfloat16), "dp").astype(jnp.float32),
        lax.psum(qv_bias_grad.astype(jnp.bfloat16), "dp").astype(jnp.float32),
        lax.psum(up_bias_grad.astype(jnp.bfloat16), "dp").astype(jnp.float32),
        lax.psum(vec_grad.astype(jnp.bfloat16), "dp").astype(jnp.float32),
    )
    split_square = jnp.float32(0.0)
    for gradient in summed[:6]:
        split_square = split_square + jnp.sum(gradient * gradient)
    vec_total, split_total = lax.psum((summed[6], split_square), "mp")
    grad_norm = jnp.sqrt(split_total + jnp.sum(vec_total * vec_total))
    factor = jnp.minimum(1.0, CLIP_NORM / (grad_norm + 1e-06))
    qkv_new, qkv_first, qkv_second = adam_update(
        w_qkv, summed[0] * factor, first_qkv, second_qkv, MATRIX_RATE, DECAY_RATE
    )
    proj_new, proj_first, proj_second = adam_update(
        w_proj, summed[1] * factor, first_proj, second_proj, MATRIX_RATE, DECAY_RATE
    )
    up_new, up_first, up_second = adam_update(
        w_up, summed[2] * factor, first_up, second_up, MATRIX_RATE, DECAY_RATE
    )
    down_new, down_first, down_second = adam_update(
        w_down, summed[3] * factor, first_down, second_down, MATRIX_RATE, DECAY_RATE
    )
    qvb_new, qvb_first, qvb_second = adam_update(
        qv_bias, summed[4] * factor, first_qv_bias, second_qv_bias, VECTOR_RATE, 0.0
    )
    upb_new, upb_first, upb_second = adam_update(
        up_bias, summed[5] * factor, first_up_bias, second_up_bias, VECTOR_RATE, 0.0
    )
    vec_new, vec_first, vec_second = adam_update(
        vec_params, vec_total * factor, first_vec, second_vec, VECTOR_RATE, 0.0
    )
    return (
        activations,
        input_grad,
        grad_norm,
        qkv_new,
        qkv_first,
        qkv_second,
        proj_new,
        proj_first,
        proj_second,
        up_new,
        up_first,
        up_second,
        down_new,
        down_first,
        down_second,
        qvb_new,
        qvb_first,
        qvb_second,
        upb_new,
        upb_first,
        upb_second,
        vec_new,
        vec_first,
        vec_second,
    )


class Transfers:
    def __init__(self, send_sem, recv_sem):
        self.sems = (send_sem, recv_sem)
        self.all = {}

    def make(self, key):
        index, src, dst, target = self.all[key]
        return pltpu.make_async_remote_copy(
            src_ref=src(), dst_ref=dst(), send_sem=self.sems[0].at[index], recv_sem=self.sems[1].at[index],
            device_id=target, device_id_type=MESH,
        )

    def plan(self, key, src, dst, target):
        self.all[key] = (len(self.all), src, dst, target)

    def start(self, key, *views):
        if views:
            self.plan(key, *views)
        self.make(key).start()

    def arrive(self, key):
        self.make(key).wait_recv()

    def finish(self):
        for key in self.all:
            self.make(key).wait_send()


class Loads:
    def __init__(self, sem):
        self.sem = sem
        self.all = {}

    def make(self, key):
        index, src, dst = self.all[key]
        return pltpu.make_async_copy(src(), dst(), self.sem.at[index])

    def plan(self, key, src, dst):
        self.all[key] = (len(self.all), src, dst)

    def start(self, key, *views):
        if views:
            self.plan(key, *views)
        self.make(key).start()

    def wait(self, key):
        self.make(key).wait()


def layer_norm_rows(rows, gain, shift):
    centred = rows - jnp.mean(rows, axis=-1, keepdims=True)
    inverse = lax.rsqrt(jnp.mean(centred * centred, axis=-1, keepdims=True) + NORM_EPS)
    unit = centred * inverse
    return unit * gain + shift, unit, inverse


def layer_norm_back(grad, unit, inverse, gain):
    scaled = grad * gain
    centre = jnp.mean(scaled, axis=-1, keepdims=True)
    slope = jnp.mean(scaled * unit, axis=-1, keepdims=True)
    return inverse * (scaled - centre - unit * slope)


def head_rows(block, sub):
    return pl.ds(pl.multiple_of(block * 128 + sub * HD, HD), HD)


def head_cols(block):
    return pl.ds(pl.multiple_of(block * 128, 128), 128)


def key_bias(shape, mp, count, shared):
    slot = lax.broadcasted_iota(jnp.int32, shape, 0)
    if shared:
        slot = lax.rem(slot + HALF * mp, SEQ)
    return jnp.where(slot < count, 0.0, MASK_FILL).astype(BF)


def widen(rows, sub):
    zeros = jnp.zeros_like(rows)
    row = lax.broadcasted_iota(jnp.int32, rows.shape, 0)
    ones = jnp.where(row == 0, 1.0, 0.0).astype(BF)
    parts = [zeros] * 4
    parts[sub] = rows
    parts[(sub + 1) % 4] = ones
    return jnp.concatenate(parts, axis=0)


def widen_plain(rows, sub):
    parts = [jnp.zeros_like(rows)] * 4
    parts[sub] = rows
    return jnp.concatenate(parts, axis=0)


def score_tile(key_block, bias, query_rows, sub):
    lane = lax.broadcasted_iota(jnp.int32, key_block.shape, 1)
    keys = jnp.where(lane // HD == (sub + 1) % 4, bias, key_block)
    return mm_nn(keys, widen(query_rows, sub))


def forward_kernel(
    count_ref, qkv_ref, proj_ref, up_ref, down_ref, small_ref, x_ref, vec_ref,
    wt_out, wp_out, wu_out, wd_out, sm_out,
    nt_out, qt_out, kt_out, k_out, v_out, ot_out, lse_out,
    wt_ref, own_proj, own_up, own_down, sm_ref, other_ref,
    norm_ref, nt_ref, qt_ref, kt_ref, vt_ref, k_ref, v_ref, ot_ref, lse_ref, bias_ref, s_ref,
    send_sem, recv_sem, local_sem,
):
    dp, mp = lax.axis_index("dp"), lax.axis_index("mp")
    peer = 1 - mp
    core, x_side, _, _ = partners(dp)
    quarter = lax.rem(dp, 4)
    x_quarter = lax.rem(quarter + 2, 4)
    gain, shift = vec_ref[0:1, :], vec_ref[1:2, :]
    greet([{"mp": peer}, {"dp": core}, {"dp": x_side}])

    remote, local = [], []

    class Transfer:
        def __init__(self, src, dst, target):
            self.index = len(remote)
            self.views = (src, dst, target)
            remote.append(self)
            self.make().start()

        def make(self):
            src, dst, target = self.views
            return pltpu.make_async_remote_copy(
                src_ref=src(), dst_ref=dst(), send_sem=send_sem.at[self.index],
                recv_sem=recv_sem.at[self.index], device_id=target, device_id_type=MESH,
            )

        def wait_recv(self):
            self.make().wait_recv()

        def wait_send(self):
            self.make().wait_send()

    def send(src, dst, target):
        return Transfer(src, dst, target)

    def keep(src, dst):
        copy = pltpu.make_async_copy(src, dst, local_sem.at[len(local)])
        copy.start()
        local.append(copy)

    def span(start, size):
        return pl.ds(pl.multiple_of(start, 16), size)

    pieces = []
    for part in range(3):
        pieces.append((wt_ref.at[mp, part], lambda side, part=part: wt_ref.at[side, part], 64, 0))
    pieces.append((own_proj, lambda side: wp_out.at[side], 64, 0))
    for shard, out, rows in ((own_up, wu_out, 128), (own_down, wd_out, 256)):
        for part in range(2):
            pieces.append((shard, lambda side, out=out: out.at[side], rows // 2, part * rows * 2))

    def place(ref, index, part):
        rows, base = pieces[index][2], pieces[index][3]
        return ref.at[span(base + part * rows, rows), :]

    first, second, third = {}, {}, {}

    def to_peer(index):
        first[index] = send(
            lambda: place(pieces[index][0], index, quarter),
            lambda: place(pieces[index][1](mp), index, quarter), {"mp": peer},
        )

    def to_sides(index):
        first[index].wait_recv()
        at = lambda: place(pieces[index][1](peer), index, quarter)
        second[index] = send(at, at, {"dp": x_side})
        third[index] = [send(at, at, {"dp": core})]

    def to_core(index):
        second[index].wait_recv()
        at = lambda: place(pieces[index][1](peer), index, x_quarter)
        third[index].append(send(at, at, {"dp": core}))

    def arrive(index):
        for copy in third[index]:
            copy.wait_recv()

    own_half = pl.multiple_of((1 - mp) * 4 * HALF, HALF)
    for part in range(3):
        wt_ref[mp, part] = qkv_ref[part].T.astype(BF)
        to_peer(part)
    sm_ref[mp] = small_ref[...]
    small_copy = send(lambda: sm_ref.at[mp], lambda: sm_ref.at[mp], {"mp": peer})
    own_proj[...] = proj_ref[...].astype(BF)
    own_up[...] = up_ref[...].astype(BF)
    own_down[...] = down_ref[...].astype(BF)
    keep(wt_ref.at[mp], wt_out.at[mp])
    keep(own_proj, wp_out.at[mp])
    keep(own_up, wu_out.at[mp])
    keep(own_down, wd_out.at[mp])

    def as_column(row):
        return jnp.broadcast_to(row, (8, row.shape[1])).T[:, 0:1]

    def normalise(group, part, rows):
        base = group * SEQ + part * HALF
        norm = layer_norm_rows(rows.astype(F32), gain, shift)[0].astype(BF)
        norm_ref[span(base, HALF), :] = norm
        nt_ref[:, pl.ds(pl.multiple_of(base, HALF), HALF)] = norm.T

    def project(side, group):
        base = pl.multiple_of(group * SEQ, SEQ)
        at = pl.ds(base, SEQ)
        own = pl.ds(pl.multiple_of(side * 256, 256), 256)
        norm = norm_ref[at, :]
        q_bias, v_bias = sm_ref[side, 1:2, 0:256], sm_ref[side, 2:3, 0:256]
        scale = LOG2E * HD ** (-0.5)
        qt_ref[own, at] = ((mm_nt(wt_ref[side, 0], norm) + as_column(q_bias)) * scale).astype(BF)
        kt_ref[own, at] = mm_nt(wt_ref[side, 1], norm).astype(BF)
        vt_ref[own, :] = (mm_nt(wt_ref[side, 2], norm) + as_column(v_bias)).astype(BF)
        k_ref[at, own] = mm_nt(norm, wt_ref[side, 1]).astype(BF)
        v_ref[at, own] = (mm_nt(norm, wt_ref[side, 2]) + v_bias).astype(BF)

    def attend(side, group, queries, between):
        base = pl.multiple_of(group * SEQ, SEQ)
        keys_at, queries_at = pl.ds(base, SEQ), pl.ds(base, queries)
        bias = bias_ref[group]

        def scores(block, sub):
            return score_tile(
                k_ref[keys_at, head_cols(block)], bias, qt_ref[head_rows(block, sub), queries_at], sub
            )

        s_ref[0, :, :queries] = scores(2 * side, 0)

        def body(step, carry):
            block = 2 * side + step
            for sub in range(4):
                following = (block, sub + 1) if sub < 3 else (2 * side + 1, 0)
                s_ref[(sub + 1) % 2, :, :queries] = scores(*following)
                tile = s_ref[sub % 2, :, :queries]
                top = jnp.max(tile, axis=0, keepdims=True)
                weights = jnp.exp2(tile - top)
                rows = head_rows(block, sub)
                values = jnp.concatenate([vt_ref[rows, :], jnp.ones((16, SEQ), BF)], axis=0)
                mixed = mm_nn(values, weights.astype(BF))
                total = mixed[HD : HD + 1]
                ot_ref[rows, queries_at] = (mixed[:HD] * (1.0 / total)).astype(BF)
                lse_ref[group, block, sub : sub + 1, :queries] = top + jnp.log2(total)

            @pl.when(step == 0)
            def _():
                between()

            return carry

        lax.fori_loop(0, 2, body, 0)

    def nothing():
        pass

    def unit(side, group, queries, early=nothing, between=nothing):
        project(side, group)
        early()
        attend(side, group, queries, between)
        at = pl.ds(pl.multiple_of(group * SEQ, SEQ), SEQ)
        own = pl.ds(pl.multiple_of(side * 256, 256), 256)
        keep(qt_ref.at[own, at], qt_out.at[own, at])
        keep(kt_ref.at[own, at], kt_out.at[own, at])
        keep(ot_ref.at[own, at], ot_out.at[own, at])
        keep(k_ref.at[at, own], k_out.at[at, own])
        keep(v_ref.at[at, own], v_out.at[at, own])

    def in_turn(*calls):
        def run():
            for call, *indices in calls:
                for index in indices:
                    call(index)

        return run

    for group in (1, 2):
        bias_ref[group] = key_bias((SEQ, 128), mp, count_ref[3 * mp + group - 1], False)
        for part in range(2):
            normalise(group, part, x_ref[pl.ds(row_block(2 * group - 1 + part, mp), HALF), :])
        if group == 1:
            to_peer(3)
            to_peer(4)
    bias_ref[0] = key_bias((SEQ, 128), mp, count_ref[2], True)
    normalise(0, 0, x_ref[pl.ds(row_block(0, mp), HALF), :])
    for index in range(3):
        to_sides(index)
    to_peer(5)
    unit(mp, 1, SEQ)
    in_turn((to_sides, 3, 4), (to_peer, 6))()
    unit(mp, 2, SEQ, between=in_turn((to_core, 0, 1, 2), (to_sides, 5), (to_peer, 7)))
    small_copy.wait_recv()
    keep(sm_ref, sm_out)
    for index in range(3):
        arrive(index)
    keep(wt_ref.at[peer], wt_out.at[peer])
    rows_copy = send(lambda: x_ref.at[pl.ds(own_half, HALF), :], lambda: other_ref, {"mp": peer})
    unit(peer, 1, SEQ, early=in_turn((to_sides, 6)), between=in_turn((to_core, 3, 4)))
    in_turn((to_sides, 7))()
    unit(peer, 2, SEQ, early=in_turn((to_core, 5)), between=in_turn((to_core, 6)))
    rows_copy.wait_recv()
    normalise(0, 1, other_ref[...])
    keep(nt_ref, nt_out)
    unit(mp, 0, HALF, between=in_turn((to_core, 7)))
    unit(peer, 0, HALF)
    keep(lse_ref, lse_out)
    for index in range(3, 8):
        arrive(index)
    for copy in remote:
        copy.wait_send()
    for copy in local:
        copy.wait()


def forward(key_count, w_qkv, w_proj, w_up, w_down, small, patches, vec_params):
    ext = 3 * SEQ
    vmem, hbm = pl.BlockSpec(memory_space=pltpu.VMEM), pl.BlockSpec(memory_space=pl.ANY)
    return pl.pallas_call(
        forward_kernel,
        out_shape=[
            sds((2, 3, 256, 512), BF), sds((2, 256, 512), BF), sds((2, 512, 1024), BF),
            sds((2, 1024, 512), BF), sds((2, 8, 1024), F32),
            sds((512, ext), BF), sds((512, ext), BF), sds((512, ext), BF), sds((ext, 512), BF),
            sds((ext, 512), BF), sds((512, ext), BF), sds((3, 4, 8, SEQ), F32),
        ],
        in_specs=[pl.BlockSpec(memory_space=pltpu.SMEM)] + [vmem] * 7,
        out_specs=[hbm] * 12,
        scratch_shapes=[
            pltpu.VMEM((2, 3, 256, 512), BF), pltpu.VMEM((256, 512), BF), pltpu.VMEM((512, 1024), BF),
            pltpu.VMEM((1024, 512), BF), pltpu.VMEM((2, 8, 1024), F32), pltpu.VMEM((HALF, 512), BF),
            pltpu.VMEM((ext, 512), BF), pltpu.VMEM((512, ext), BF), pltpu.VMEM((512, ext), BF),
            pltpu.VMEM((512, ext), BF), pltpu.VMEM((512, SEQ), BF), pltpu.VMEM((ext, 512), BF),
            pltpu.VMEM((ext, 512), BF), pltpu.VMEM((512, ext), BF), pltpu.VMEM((3, 4, 8, SEQ), F32),
            pltpu.VMEM((3, SEQ, 128), BF), pltpu.VMEM((2, SEQ, SEQ), F32),
            pltpu.SemaphoreType.DMA((34,)), pltpu.SemaphoreType.DMA((34,)), pltpu.SemaphoreType.DMA((40,)),
        ],
        compiler_params=pltpu.CompilerParams(
            collective_id=0, has_side_effects=True, vmem_limit_bytes=VMEM_LIMIT
        ),
        name="forward",
    )(key_count, w_qkv, w_proj, w_up, w_down, small, patches, vec_params)


def mlp_kernel(
    x_ref, dy_ref, ot_ref, wp_ref, wu_ref, wd_ref, vec_ref, small_ref,
    act_ref, dres_ref, dot_ref, own_out, fore_out, gp_ref, vsum_ref, bsum_ref,
    res_ref, n2_ref, out_ref, dn_ref, hid_ref, dup_ref, dyc_ref, br_ref,
    g_ref, fore_ref, fore_core, own_core, own_peer, send_sem, recv_sem,
):
    step = pl.program_id(0)
    dp, mp = lax.axis_index("dp"), lax.axis_index("mp")
    peer, core, core_bit = 1 - mp, partners(dp)[0], lax.rem(dp, 2)
    side, part = jnp.where(step < 2, peer, mp), lax.rem(step, 2)
    sent = Transfers(send_sem, recv_sem)
    kept = pl.ds(pl.multiple_of(core_bit * HALF, HALF), HALF)
    away = pl.ds(pl.multiple_of(HALF - core_bit * HALF, HALF), HALF)
    for turn in range(2):
        sent.plan(
            ("F", turn), lambda turn=turn: g_ref.at[turn, :, away, :], lambda turn=turn: fore_core.at[turn],
            {"dp": core},
        )
        sent.plan(
            ("O", turn), lambda turn=turn: g_ref.at[2 + turn, :, away, :],
            lambda turn=turn: own_core.at[turn], {"dp": core},
        )
    sent.plan("peer", lambda: fore_ref, lambda: own_peer, {"mp": peer})
    gain, shift = vec_ref[2:3, :], vec_ref[3:4, :]
    w_proj = wp_ref[...].reshape(512, 512)

    def rows(index):
        return pl.ds(pl.multiple_of(index * HALF, HALF), HALF)

    @pl.when(step == 0)
    def _():
        greet([{"dp": core}, {"mp": peer}])

        def body(index, carry):
            x_rows = x_ref[pl.ds(row_block(index, mp), HALF), :].astype(F32)
            mixed = ot_ref[:, pl.ds(ext_cols(index), HALF)]
            resid = x_rows + mm_tn(mixed, w_proj) + vec_ref[4:5, :]
            res_ref[rows(index), :] = resid
            n2_ref[rows(index), :] = layer_norm_rows(resid, gain, shift)[0].astype(BF)
            out_ref[rows(index), :] = resid + vec_ref[5:6, :]
            dn_ref[rows(index), :] = jnp.zeros((HALF, 512), F32)
            dyc_ref[rows(index), :] = dy_ref[pl.ds(row_block(index, mp), HALF), :]
            return carry

        lax.fori_loop(0, 5, body, 0, unroll=True)

    lanes = pl.ds(pl.multiple_of(part * 512, 512), 512)
    w_up, w_down = wu_ref[side, :, lanes], wd_ref[side, lanes, :]
    up_bias = small_ref[side, 0:1, lanes]

    def up_of(index):
        return mm_nn(n2_ref[index * HALF : index * HALF + HALF, :], w_up) + up_bias

    total = jnp.zeros((8, 512), F32)
    pre = up_of(0)
    for index in range(5):
        at = slice(index * HALF, index * HALF + HALF)
        up_pre = pre
        if index < 4:
            pre = up_of(index + 1)
        dhid = mm_nt(dyc_ref[at, :], w_down)
        cumulative = 0.5 * (1.0 + lax.erf(up_pre * (0.5**0.5)))
        density = jnp.exp(-0.5 * up_pre * up_pre) * 0.3989422804014327
        hidden = (up_pre * cumulative).astype(BF)
        hid_ref[at, :] = hidden
        slope = cumulative + up_pre * density
        dup = (dhid * slope).astype(BF)
        dup_ref[at, :] = dup
        total = total + jnp.sum(dup.astype(F32).reshape(HALF // 8, 8, 512), axis=0)
        out_ref[at, :] += mm_nn(hidden, w_down)
        dn_ref[at, :] += mm_nt(dup, w_up)
        if index == 1:

            @pl.when(step == 1)
            def _():
                sent.arrive(("F", 0))
                fore_ref[...] = g_ref[0, :, kept, :] + fore_core[0]
                sent.start("peer")

            @pl.when(step == 2)
            def _():
                sent.arrive(("F", 1))
                fore_out[...] = g_ref[1, :, kept, :] + fore_core[1]

    bsum_ref[2 * side + part] = total
    g_ref[step, 0] = mm_tn(hid_ref[...], dyc_ref[...]).astype(BF)
    g_ref[step, 1] = mm_tn(n2_ref[...], dup_ref[...]).astype(BF)
    for turn, key in enumerate((("F", 0), ("F", 1), ("O", 0), ("O", 1))):

        @pl.when(step == turn)
        def _():
            sent.start(key)

    @pl.when(step == 3)
    def _():
        vsum_ref[...] = jnp.zeros_like(vsum_ref)

        def body(index, carry):
            at = rows(index)
            act_ref[pl.ds(row_block(index, mp), HALF), :] = out_ref[at, :].astype(BF)
            _, unit, inverse = layer_norm_rows(res_ref[at, :], gain, shift)
            dn = dn_ref[at, :]
            dy = dyc_ref[at, :].astype(F32)
            dres = dy + layer_norm_back(dn, unit, inverse, gain)
            dres_ref[at, :] = dres
            branch = dres.astype(BF)
            br_ref[at, :] = branch
            dot_ref[:, pl.ds(ext_cols(index), HALF)] = mm_nt(w_proj, branch).astype(BF)
            sums = [dn * unit, dn, branch.astype(F32), dy]
            for place, value in enumerate(sums):
                vsum_ref[place] += jnp.sum(value.reshape(HALF // 8, 8, 512), axis=0)
            return carry

        lax.fori_loop(0, 5, body, 0, unroll=True)
        mixed = jnp.concatenate([ot_ref[:, 0:HALF], ot_ref[:, SEQ:]], axis=1)
        gp_ref[...] = mm_nn(mixed, br_ref[...]).astype(BF).reshape(2, 256, 512)
        sent.arrive(("O", 0))
        sent.arrive(("O", 1))
        sent.arrive("peer")
        near = g_ref[2, :, kept, :].astype(F32) + own_core[0].astype(F32)
        own_out[0] = (near + own_peer[...].astype(F32)).astype(BF)
        own_out[1] = g_ref[3, :, kept, :] + own_core[1]
        sent.finish()


def mlp(patches, cotangent, ot, wp, wu, wd, vec_params, small):
    rows = patches.shape[0]
    ext = 3 * SEQ
    return pl.pallas_call(
        mlp_kernel,
        grid=(4,),
        out_shape=[
            sds((rows, 512), BF), sds((rows, 512), F32), sds((512, ext), BF), sds((2, 2, HALF, 512), BF),
            sds((2, HALF, 512), BF), sds((2, 256, 512), BF), sds((4, 8, 512), F32), sds((4, 8, 512), F32),
        ],
        in_specs=[
            full_spec((rows, 512)), full_spec((rows, 512)), full_spec((512, ext)), full_spec(wp.shape),
            full_spec(wu.shape), full_spec(wd.shape), full_spec(vec_params.shape), full_spec(small.shape),
        ],
        out_specs=[
            full_spec((rows, 512)), full_spec((rows, 512)), full_spec((512, ext)),
            full_spec((2, 2, HALF, 512)), full_spec((2, HALF, 512)),
            full_spec((2, 256, 512)), full_spec((4, 8, 512)), full_spec((4, 8, 512)),
        ],
        scratch_shapes=[
            pltpu.VMEM((rows, 512), F32), pltpu.VMEM((rows, 512), BF), pltpu.VMEM((rows, 512), F32),
            pltpu.VMEM((rows, 512), F32), pltpu.VMEM((rows, 512), BF), pltpu.VMEM((rows, 512), BF),
            pltpu.VMEM((rows, 512), BF), pltpu.VMEM((rows, 512), BF), pltpu.VMEM((4, 2, 512, 512), BF),
            pltpu.VMEM((2, HALF, 512), BF), pltpu.VMEM((2, 2, HALF, 512), BF),
            pltpu.VMEM((2, 2, HALF, 512), BF), pltpu.VMEM((2, HALF, 512), BF),
            pltpu.SemaphoreType.DMA((5,)), pltpu.SemaphoreType.DMA((5,)),
        ],
        compiler_params=pltpu.CompilerParams(
            collective_id=2, has_side_effects=True, vmem_limit_bytes=VMEM_LIMIT
        ),
        name="mlp",
    )(patches, cotangent, ot, wp, wu, wd, vec_params, small)


SCHEDULE = (
    (
        ("F", 2, 1), ("F", 4, 0), ("O", 0, 1), ("O", 1, 1), ("O", 4, 0),
    ),
    (
    ),
    (
        ("F", 3, 1),
    ),
    (
        ("O", 0, 2),
    ),
    (
        ("F", 4, 1), ("O", 1, 2), ("O", 2, 1),
    ),
    (
    ),
    (
    ),
    (
        ("O", 0, 3), ("O", 3, 1),
    ),
    (
        ("F", 5, 0), ("O", 1, 3), ("O", 4, 1),
    ),
    (
        ("F", 5, 1), ("O", 2, 2),
    ),
    (
    ),
    (
        ("O", 0, 4), ("O", 3, 2),
    ),
    (
        ("F", 6, 0), ("O", 1, 4), ("O", 4, 2),
    ),
    (
        ("F", 6, 1),
    ),
    (
        ("O", 0, 5), ("O", 2, 3),
    ),
    (
        ("O", 3, 3),
    ),
    (
        ("O", 0, 6), ("O", 1, 5), ("O", 4, 3), ("O", 5, 0),
    ),
    (
    ),
    (
        ("O", 1, 6), ("O", 2, 4), ("O", 5, 1),
    ),
    (
    ),
    (
        ("O", 3, 4), ("O", 6, 0),
    ),
    (
    ),
    (
    ),
    (
        ("O", 2, 5), ("O", 4, 4), ("O", 6, 1),
    ),
    (
    ),
    (
        ("O", 2, 6),
    ),
    (
        ("O", 5, 3), ("O", 3, 5), ("small", 0), ("O", 4, 5), ("O", 3, 6), ("O", 4, 6), ("O", 6, 3),
        ("square", 0), ("square", 1), ("small", 1), ("small", 2), ("O", 5, 5), ("square", 2), ("O", 5, 6),
        ("O", 6, 5), ("O", 6, 6),
    ),
)


def cut(ref, start, size):
    rows = pl.ds(pl.multiple_of(start, 16), size)
    return ref.at[:, rows, :] if len(ref.shape) == 3 else ref.at[rows, :]


WIDE = (5, 6)
PIECES = ((512, 512), (512, 512), (512, 512), (512, 512), (256, 512), (3, 512, 128), (3, 512, 128))


def piece_rows(index, size):
    return (*PIECES[index][:-2], PIECES[index][-2] // size, PIECES[index][-1])


def backward_kernel(
    count_ref, qt_in, kt_in, dot_in, ot_in, k_in, v_in, lse_ref, nt_in, wt_in,
    own_in, fore_in, gp_in, x_in, dres_in, vec_ref, two_ref, up_sum_ref,
    grad_out, down_out, up_out, proj_out, qkv_out, small_out, norm_out,
    qt_ref, kt_ref, dot_ref, ot_ref, k_ref, v_ref, nt_ref, wt_ref, x_ref, dres_ref,
    shared_ref, grads_ref, acc_ref, bias_ref, s_ref, dp_ref, g_ref, bsum_ref,
    far_send, far_recv, small_core, small_part, small_all, square_sum, square_core, square_all, *rest,
):
    buffers, (send_sem, recv_sem, local_sem) = rest[:-3], rest[-3:]
    dp, mp = lax.axis_index("dp"), lax.axis_index("mp")
    peer = 1 - mp
    core, x_side, _, _ = partners(dp)
    to_core, to_peer, to_x = {"dp": core}, {"mp": peer}, {"dp": x_side}
    core_bit, x_bit = lax.rem(dp, 2), lax.rem(lax.div(dp, 2), 2)
    chip, floor = lax.div(dp, 2), lax.div(dp, 4)

    def ring(index):
        return (chip, 8, 2) if index in WIDE else (floor, 4, 4)
    sent, loads = Transfers(send_sem, recv_sem), Loads(local_sem)

    def block_at(place):
        return 2 * jnp.where(place < 2, peer, mp) + lax.rem(place, 2)

    def source(index, side):
        if index == 4:
            return gp_in.at[side]
        return g_ref.at[index - 5 + (0 if side is peer else 2)]

    def result(index):
        if index < 4:
            lanes = slice(index // 2 * 512, index // 2 * 512 + 512)
            return up_out.at[:, lanes] if index % 2 else down_out.at[lanes, :]
        if index == 4:
            return proj_out
        return qkv_out.at[:, :, slice((index - 5) * 128, (index - 5) * 128 + 128)]

    def piece_buffers(index):
        return buffers[8 * index : 8 * index + 8]

    def region(index):
        half = PIECES[index][-2] // 2
        if index in WIDE:
            return core_bit * half, half
        return core_bit * half + x_bit * (half // 2), half // 2

    for place in range(4):
        block = block_at(place)
        rows = pl.ds(pl.multiple_of(block * 128, 128), 128)
        for name, src, dst in (
            ("qt", qt_in, qt_ref), ("kt", kt_in, kt_ref), ("dot", dot_in, dot_ref), ("ot", ot_in, ot_ref)
        ):
            loads.start(
                (name, place), lambda src=src, rows=rows: src.at[rows, :],
                lambda dst=dst, place=place: dst.at[place],
            )
        for name, src, dst in (("k", k_in, k_ref), ("v", v_in, v_ref)):
            loads.start(
                (name, place), lambda src=src, rows=rows: src.at[:, rows],
                lambda dst=dst, place=place: dst.at[place],
            )
        if place == 0:
            loads.start("wt", lambda: wt_in, lambda: wt_ref)
    loads.start("nt", lambda: nt_in, lambda: nt_ref)
    for index in range(4):
        loads.start(
            ("kept", index, 2), lambda index=index: own_in.at[index // 2, index % 2],
            lambda index=index: piece_buffers(index)[2],
        )
        if index > 1:
            loads.start(
                ("kept", index, 0), lambda index=index: fore_in.at[index % 2],
                lambda index=index: piece_buffers(index)[0],
            )
    for index in (4,):
        total = PIECES[index][-2]
        for side, slot in ((peer, 0), (mp, 2)):
            loads.start(
                ("kept", index, slot),
                lambda index=index, side=side, total=total: cut(
                    source(index, side), core_bit * (total // 2), total // 2
                ),
                lambda index=index, slot=slot: piece_buffers(index)[slot],
            )
    loads.start("x", lambda: x_in, lambda: x_ref)
    loads.start("dres", lambda: dres_in, lambda: dres_ref)
    chips = [
        {"dp": lax.rem(dp + 2 * step, 16), "mp": side} for side in (mp, peer) for step in range(8)
    ][1:]
    greet([to_core] + chips)

    def plan_piece(index):
        total = PIECES[index][-2]
        half = total // 2
        kept = core_bit * half
        fore, fore_core, own, own_core, own_peer, own_x, landing, out = piece_buffers(index)
        away = (1 - core_bit) * half
        if index > 1:
            sent.plan(("F", index, 1), lambda: fore, lambda: own_peer, to_peer)
        if index > 3:
            sent.plan(("F", index, 0), lambda: cut(source(index, peer), away, half), lambda: fore_core, to_core)
            sent.plan(("O", index, 0), lambda: cut(source(index, mp), away, half), lambda: own_core, to_core)
        if index not in WIDE:
            other_x = (1 - x_bit) * (half // 2)
            sent.plan(("O", index, 1), lambda: cut(own, other_x, half // 2), lambda: own_x, to_x)
        first, size = region(index)
        me, members, stride = ring(index)
        size //= members
        for step in range(1, members):
            target = {"dp": lax.rem(dp + stride * step, 16)}
            their = lax.rem(me + step, members) * size + first
            mine = me * size + first
            sent.plan(
                ("O", index, 2, step), lambda their=their: cut(own, their - kept, size),
                lambda step=step: landing.at[step - 1], target,
            )
            place = lambda mine=mine: cut(out, mine, size)
            sent.plan(("O", index, 3, step), place, place, target)
        if index not in WIDE:
            across = lambda: cut(out, region(index)[0], half // 2)
            sent.plan(("O", index, 4), across, across, to_x)
        whole = lambda: cut(out, kept, half)
        sent.plan(("O", index, 5), whole, whole, to_core)
        loads.plan(("out", index), lambda: out, lambda: result(index))

    def event(kind, index, stage):
        total = PIECES[index][-2]
        half = total // 2
        kept = core_bit * half
        wide = index in WIDE
        fore, fore_core, own, own_core, own_peer, own_x, landing, out = piece_buffers(index)
        first, size = region(index)
        me, members, _ = ring(index)
        size //= members

        def each(stage, call):
            for step in range(1, members):
                call(("O", index, stage, step))

        if stage == 0:
            sent.start((kind, index, 0))
        elif kind == "F":
            if index > 3:
                sent.arrive((kind, index, 0))
            if index < 4:
                loads.wait(("kept", index, 0))
            elif index < 5:
                loads.wait(("kept", index, 0))
                fore[...] += fore_core[...]
            else:
                fore[...] = cut(source(index, peer), kept, half)[...] + fore_core[...]
            sent.start((kind, index, 1))
        elif stage == 1:
            if index > 3:
                sent.arrive((kind, index, 0))
            if index > 1:
                sent.arrive(("F", index, 1))
            if index < 5:
                loads.wait(("kept", index, 2))
            if index > 1:
                base = (own if index < 5 else cut(source(index, mp), kept, half))[...].astype(F32)
                if index > 3:
                    base = base + own_core[...].astype(F32)
                own[...] = (base + own_peer[...].astype(F32)).astype(BF)
            if wide:
                each(2, sent.start)
            else:
                sent.start((kind, index, 1))
        elif stage == 2:
            sent.arrive((kind, index, 1))
            at = x_bit * (half // 2)
            cut(own, at, half // 2)[...] += own_x[...]
            each(2, sent.start)
        elif stage == 3:
            each(2, sent.arrive)
            value = cut(own, first - kept + me * size, size)[...].astype(F32)
            for step in range(members - 1):
                value = value + landing[step].astype(F32)
            value = value.astype(BF)
            cut(out, first + me * size, size)[...] = value
            each(3, sent.start)
            squared = value.astype(F32)
            square = jnp.sum((squared * squared).reshape(-1, 8, squared.shape[-1]), axis=0)
            folded = square[:, 0:128]
            for lane in range(1, square.shape[1] // 128):
                folded = folded + square[:, lane * 128 : lane * 128 + 128]
            square_sum[...] += folded
        elif stage == 4:
            each(3, sent.arrive)
            sent.start((kind, index, 4))
        elif stage == 5:
            if wide:
                each(3, sent.arrive)
            else:
                sent.arrive((kind, index, 4))
            sent.start((kind, index, 5))
        else:
            sent.arrive((kind, index, 5))
            loads.start(("out", index))

    for index in range(7):
        plan_piece(index)

    def run(events):
        for item in events:
            event(*item)

    square_sum[...] = jnp.zeros((8, 128), F32)
    bias_ref[0] = key_bias((SEQ, 128), mp, count_ref[2], True)
    for group in (1, 2):
        bias_ref[group] = key_bias((SEQ, 128), mp, count_ref[3 * mp + group - 1], False)
    run(SCHEDULE[0])

    def heads(place, group, queries, out, out_base, between):
        block = block_at(place)
        base = pl.multiple_of(group * SEQ, SEQ)
        keys_at, queries_at = pl.ds(base, SEQ), pl.ds(base, queries)
        out_keys = pl.ds(out_base, SEQ)
        out_queries = pl.ds(out_base, queries)
        bias = bias_ref[group]

        def tiles(sub):
            own = slice(sub * HD, sub * HD + HD)
            s_ref[sub % 2, :, :queries] = score_tile(
                k_ref[place, keys_at, :], bias, qt_ref[place, own, queries_at], sub
            )
            dp_ref[sub % 2, :, :queries] = mm_nn(
                v_ref[place, keys_at, :], widen_plain(dot_ref[place, own, queries_at], sub)
            )

        tiles(0)
        for sub in range(4):
            if sub < 3:
                tiles(sub + 1)
            own = slice(sub * HD, sub * HD + HD)
            q_rows, do_rows = qt_ref[place, own, queries_at], dot_ref[place, own, queries_at]
            delta = jnp.sum(
                do_rows.astype(F32) * ot_ref[place, own, queries_at].astype(F32), axis=0, keepdims=True
            )
            probs = jnp.exp2(
                s_ref[sub % 2, :, :queries] - lse_ref[group, block, sub : sub + 1, :queries]
            )
            draw = (probs * (dp_ref[sub % 2, :, :queries] - delta)).astype(BF)
            dq = mm_nn(kt_ref[place, own, keys_at], draw) * (HD ** (-0.5))
            out[own, out_queries] = dq.astype(BF)
            dk = mm_nt(q_rows, draw) * (1.0 / LOG2E)
            out[128 + sub * HD : 160 + sub * HD, out_keys] = dk.astype(BF)
            dv = mm_nt(do_rows, probs.astype(BF))
            out[256 + sub * HD : 288 + sub * HD, out_keys] = dv.astype(BF)
            if sub == 1:
                between()

    def weights_of(place):
        block = block_at(place)
        side, part = lax.div(block, 2), lax.rem(block, 2)
        return wt_ref[side, :, pl.ds(pl.multiple_of(part * 128, 128), 128), :].reshape(384, 512)

    acc_ref[...] = jnp.zeros_like(acc_ref)
    for place in range(4):
        for name in ("qt", "kt", "dot", "ot", "k", "v"):
            loads.wait((name, place))
        if place == 0:
            loads.wait("wt")
        shared_ref[place, 0:128, HALF:SEQ] = jnp.zeros((128, HALF), BF)

    def shared_step(place, carry):
        heads(place, 0, HALF, shared_ref.at[place], 0, lambda: None)
        acc_ref[0:SEQ] += mm_tn(shared_ref[place], weights_of(place))
        for turn in range(4):

            @pl.when(place == turn)
            def _():
                run(SCHEDULE[1 + turn])

        return carry

    lax.fori_loop(0, 4, shared_step, 0)
    far_send[...] = acc_ref[HALF:SEQ].astype(BF)
    sent.start("far", lambda: far_send, lambda: far_recv, to_peer)
    loads.wait("nt")

    def main_step(step, carry):
        place, group = lax.div(step, 2), 1 + lax.rem(step, 2)

        def pump(first):
            for turn in range(8):

                @pl.when(step == turn)
                def _():
                    run(SCHEDULE[first + 2 * turn])

        out_base = pl.multiple_of((group - 1) * SEQ, SEQ)
        heads(place, group, SEQ, grads_ref, out_base, lambda: pump(5))

        @pl.when(group == 2)
        def _():
            for part in range(3):
                rows = slice(part * 128, part * 128 + 128)
                total = mm_nt(nt_ref[:, 0:SEQ], shared_ref[place, rows, :])
                total += mm_nt(nt_ref[:, SEQ:], grads_ref[rows, :])
                g_ref[place, part] = total.astype(BF)
            ones = jnp.ones((8, 2 * SEQ), BF)
            bsum_ref[place] = mm_nt(ones[:, :SEQ], shared_ref[place]) + mm_nt(ones, grads_ref[...])
            acc_ref[SEQ:] += mm_tn(grads_ref[...], weights_of(place))

        pump(6)
        return carry

    lax.fori_loop(0, 8, main_step, 0)

    gain, shift = vec_ref[0:1, :], vec_ref[1:2, :]
    loads.wait("x")
    loads.wait("dres")
    run(SCHEDULE[21])

    def finish_rows(index, dn, sums):
        at = pl.ds(pl.multiple_of(index * HALF, HALF), HALF)
        place = pl.ds(row_block(index, mp), HALF)
        _, unit, inverse = layer_norm_rows(x_ref[place, :].astype(F32), gain, shift)
        grad_out[place, :] = dres_ref[at, :] + layer_norm_back(dn, unit, inverse, gain)
        folded = [jnp.sum(value.reshape(HALF // 8, 8, 512), axis=0) for value in (dn * unit, dn)]
        return sums[0] + folded[0], sums[1] + folded[1]

    def finish_step(index, sums):
        sums = finish_rows(
            index, acc_ref[pl.ds(pl.multiple_of(HALF * index + HALF, HALF), HALF), :], sums
        )
        for turn in range(1, 5):

            @pl.when(index == turn)
            def _():
                run(SCHEDULE[21 + turn])

        return sums

    zero = jnp.zeros((8, 512), F32)
    sums = lax.fori_loop(1, 5, finish_step, (zero, zero))
    sent.arrive("far")
    sums = finish_rows(0, acc_ref[0:HALF] + far_recv[...].astype(F32), sums)

    def small_row(place, value):
        small_core[0, place : place + 1, :] = value

    small_core[0] = jnp.zeros((16, 512), F32)
    for place in range(4):
        lanes = pl.ds(pl.multiple_of(block_at(place) * 128, 128), 128)
        small_core[0, 0:1, lanes] = bsum_ref[place, 0:1, 0:128]
        small_core[0, 1:2, lanes] = bsum_ref[place, 0:1, 256:384]
        small_row(2 + place, jnp.sum(up_sum_ref[place], axis=0, keepdims=True))
        small_row(8 + place, jnp.sum(two_ref[place], axis=0, keepdims=True))
    for place in range(2):
        small_row(6 + place, jnp.sum(sums[place], axis=0, keepdims=True))

    me = mp * 8 + chip
    rows_mine = pl.ds(pl.multiple_of(core_bit * 8, 8), 8)
    rows_other = pl.ds(pl.multiple_of(8 - core_bit * 8, 8), 8)
    sent.plan("small core", lambda: small_core.at[0, rows_other], lambda: small_core.at[1, rows_other], to_core)
    sent.plan("square core", lambda: square_sum, lambda: square_core, to_core)
    sent.plan("small back", lambda: small_part.at[rows_mine], lambda: small_part.at[rows_mine], to_core)
    for place, target in enumerate(chips):
        sent.plan(("small", place), lambda: small_all.at[me], lambda: small_all.at[me], target)
        sent.plan(("square", place), lambda: square_all.at[me], lambda: square_all.at[me], target)

    def everywhere(name, call):
        for place in range(len(chips)):
            call((name, place))

    def small_stage(stage):
        if stage == 0:
            sent.arrive("small core")
            small_all[me] = small_core[0, rows_mine] + small_core[1, rows_mine]
            everywhere("small", sent.start)
        elif stage == 1:
            everywhere("small", sent.arrive)
            small_part[rows_mine] = jnp.sum(small_all[...], axis=0)
            sent.start("small back")
        else:
            sent.arrive("small back")

    def square_stage(stage):
        if stage == 0:
            sent.start("square core")
        elif stage == 1:
            sent.arrive("square core")
            square_all[me] = square_sum[...] + square_core[...]
            everywhere("square", sent.start)
        else:
            everywhere("square", sent.arrive)
            small = small_part[...]
            small_out[...] = small
            total = jnp.sum(small * small) + jnp.sum(jnp.sum(square_all[...], axis=0))
            norm_out[...] = jnp.sqrt(jnp.full((8, 128), total, F32))

    sent.start("small core")
    for item in SCHEDULE[26]:
        if item[0] == "small":
            small_stage(item[1])
        elif item[0] == "square":
            square_stage(item[1])
        else:
            event(*item)
    sent.finish()
    for index in range(7):
        loads.wait(("out", index))


def backward(key_count, qt, kt, dot, ot, k, v, lse, nt, wt, owns, fores, gp, patches, dres, vec_params, two, ups):
    ext, rows = 3 * SEQ, patches.shape[0]
    vmem, hbm = pl.BlockSpec(memory_space=pltpu.VMEM), pl.BlockSpec(memory_space=pl.ANY)
    buffers = []
    for index in range(7):
        for size in (2, 2, 2, 2, 2, 4):
            buffers.append(pltpu.VMEM(piece_rows(index, size), BF))
        members = 7 if index in WIDE else 3
        buffers.append(pltpu.VMEM((members, *piece_rows(index, 16)), BF))
        buffers.append(pltpu.VMEM(piece_rows(index, 1), BF))
    return pl.pallas_call(
        backward_kernel,
        out_shape=[
            sds((rows, 512), F32), sds((1024, 512), BF), sds((512, 1024), BF), sds((256, 512), BF),
            sds((3, 512, 256), BF), sds((16, 512), F32), sds((8, 128), F32),
        ],
        in_specs=[pl.BlockSpec(memory_space=pltpu.SMEM)] + [hbm] * 6 + [vmem] + [hbm] * 7 + [vmem] * 3,
        out_specs=[vmem] + [hbm] * 4 + [vmem] * 2,
        scratch_shapes=[
            *[pltpu.VMEM((4, 128, ext), BF)] * 4, *[pltpu.VMEM((4, ext, 128), BF)] * 2,
            pltpu.VMEM((512, ext), BF), pltpu.VMEM((2, 3, 256, 512), BF), pltpu.VMEM((rows, 512), BF),
            pltpu.VMEM((rows, 512), F32), pltpu.VMEM((4, 384, SEQ), BF), pltpu.VMEM((384, 2 * SEQ), BF),
            pltpu.VMEM((ext, 512), F32), pltpu.VMEM((3, SEQ, 128), BF), pltpu.VMEM((2, SEQ, SEQ), F32),
            pltpu.VMEM((2, SEQ, SEQ), F32), pltpu.VMEM((4, 3, 512, 128), BF), pltpu.VMEM((4, 8, 384), F32),
            pltpu.VMEM((HALF, 512), BF), pltpu.VMEM((HALF, 512), BF), pltpu.VMEM((2, 16, 512), F32),
            pltpu.VMEM((16, 512), F32), pltpu.VMEM((16, 8, 512), F32), pltpu.VMEM((8, 128), F32),
            pltpu.VMEM((8, 128), F32), pltpu.VMEM((16, 8, 128), F32), *buffers,
            pltpu.SemaphoreType.DMA((120,)), pltpu.SemaphoreType.DMA((120,)), pltpu.SemaphoreType.DMA((48,)),
        ],
        compiler_params=pltpu.CompilerParams(
            collective_id=1, has_side_effects=True, vmem_limit_bytes=VMEM_LIMIT
        ),
        name="backward",
    )(key_count, qt, kt, dot, ot, k, v, lse, nt, wt, owns, fores, gp, patches, dres, vec_params, two, ups)


def adam_kernel(norm_ref, *refs):
    factor = jnp.minimum(1.0, CLIP_NORM / (norm_ref[0:1, 0:1] + 1e-06))
    for index in range(4):
        weight_ref, one_ref, two_ref, grad_ref = refs[4 * index : 4 * index + 4]
        outs = refs[16 + 3 * index : 19 + 3 * index]
        results = adam_update(
            weight_ref[...], grad_ref[...].astype(F32) * factor, one_ref[...], two_ref[...],
            MATRIX_RATE, DECAY_RATE,
        )
        for out, value in zip(outs, results):
            out[...] = value


def adam_matrices(norm, groups):
    steps = 8
    in_specs, out_specs, out_shape, args = [full_spec((8, 128))], [], [], [norm]
    for group in groups:
        rows, width = group[0].shape
        spec = pl.BlockSpec((rows // steps, width), lambda i: (i, 0))
        in_specs += [spec] * 4
        out_specs += [spec] * 3
        out_shape += [sds((rows, width), F32)] * 3
        args += list(group)
    outs = pl.pallas_call(
        adam_kernel,
        grid=(steps,),
        out_shape=out_shape,
        in_specs=in_specs,
        out_specs=out_specs,
        compiler_params=pltpu.CompilerParams(vmem_limit_bytes=VMEM_LIMIT),
        name="adam_matrices",
    )(*args)
    return [outs[3 * index : 3 * index + 3] for index in range(len(groups))]


IN_SPECS = (
            P(("dp", "mp"), None),
            P(("dp", "mp"), None),
            P("dp"),
            P(None, None, "mp"),
            P("mp", None),
            P(None, "mp"),
            P("mp", None),
            P(None, "mp"),
            P("mp"),
            P(),
            P(None, None, "mp"),
            P(None, None, "mp"),
            P("mp", None),
            P("mp", None),
            P(None, "mp"),
            P(None, "mp"),
            P("mp", None),
            P("mp", None),
            P(None, "mp"),
            P(None, "mp"),
            P("mp"),
            P("mp"),
            P(),
            P(),
        )
OUT_SPECS = (
            P(("dp", "mp"), None),
            P(("dp", "mp"), None),
            P(),
            P(None, None, "mp"),
            P(None, None, "mp"),
            P(None, None, "mp"),
            P("mp", None),
            P("mp", None),
            P("mp", None),
            P(None, "mp"),
            P(None, "mp"),
            P(None, "mp"),
            P("mp", None),
            P("mp", None),
            P("mp", None),
            P(None, "mp"),
            P(None, "mp"),
            P(None, "mp"),
            P("mp"),
            P("mp"),
            P("mp"),
            P(),
            P(),
            P(),
        )


def paired(
    patches, cotangent, key_count, w_qkv, w_proj, w_up, w_down, qv_bias, up_bias, vec_params,
    first_qkv, second_qkv, first_proj, second_proj, first_up, second_up, first_down, second_down,
    first_qv_bias, second_qv_bias, first_up_bias, second_up_bias, first_vec, second_vec,
):
    mp = lax.axis_index("mp")
    small = jnp.concatenate(
        [up_bias[None, :], jnp.pad(qv_bias, ((0, 0), (0, 768))), jnp.zeros((5, 1024), F32)], axis=0
    )
    wt, wp, wu, wd, small_all, nt, qt, kt, k, v, ot, lse = forward(
        key_count, w_qkv, w_proj, w_up, w_down, small, patches, vec_params
    )
    activations, dres, dot, owns, fores, g_proj, vsum_two, up_sums = mlp(
        patches, cotangent, ot, wp, wu, wd, vec_params, small_all
    )
    input_grad, down, up, proj, qkv, small_total, norm = backward(
        key_count, qt, kt, dot, ot, k, v, lse, nt, wt, owns, fores, g_proj, patches, dres, vec_params,
        vsum_two, up_sums,
    )
    qkv = qkv.reshape(1536, 256)
    flat = lambda array: array.reshape(-1, array.shape[-1])
    groups = [
        (flat(w_qkv), flat(first_qkv), flat(second_qkv), qkv),
        (w_proj, first_proj, second_proj, proj),
        (w_up, first_up, second_up, up),
        (w_down, first_down, second_down, down),
    ]
    new_qkv, new_proj, new_up, new_down = adam_matrices(norm, groups)
    grad_norm = norm[0, 0]
    factor = jnp.minimum(1.0, CLIP_NORM / (grad_norm + 1e-06))
    qv_total = lax.dynamic_slice_in_dim(small_total[0:2], mp * 256, 256, 1)
    up_total = lax.dynamic_slice_in_dim(small_total[2:6].reshape(-1), mp * 1024, 1024, 0)
    new_qvb = adam_update(qv_bias, qv_total * factor, first_qv_bias, second_qv_bias, VECTOR_RATE, 0.0)
    new_upb = adam_update(up_bias, up_total * factor, first_up_bias, second_up_bias, VECTOR_RATE, 0.0)
    new_vec = adam_update(
        vec_params, small_total[6:12] * factor, first_vec, second_vec, VECTOR_RATE, 0.0
    )
    return (
        activations, input_grad, grad_norm, *[array.reshape(w_qkv.shape) for array in new_qkv],
        *new_proj, *new_up, *new_down, *new_qvb, *new_upb, *new_vec,
    )


def fits_pairs(mesh, args):
    if dict(mesh.shape) != {"dp": 16, "mp": 2}:
        return False
    return args[0].shape == (40960, 512) and args[2].shape == (80,)


def solution(mesh):
    def run(*args):
        body = paired if fits_pairs(mesh, args) else local
        return jax.shard_map(body, mesh=mesh, in_specs=IN_SPECS, out_specs=OUT_SPECS, check_vma=False)(*args)

    return run
```

```python
import jax
import jax.numpy as jnp
from jax import lax
from jax.experimental import pallas as pl
from jax.experimental.pallas import tpu as pltpu
from jax.sharding import PartitionSpec as P

HD = 32
ADAM_STEP = 10


NORM_EPS = 1e-06
BETA_FIRST = 0.9
BETA_SECOND = 0.95
ADAM_EPS = 1e-08
DECAY_RATE = 0.05
MATRIX_RATE = 0.1
VECTOR_RATE = 0.8
CLIP_NORM = 1.0
MASK_FILL = -1e30
LOG2E = 1.4426950408889634
BF = jnp.bfloat16
F32 = jnp.float32
MESH = pl.DeviceIdType.MESH
SEQ = 512
HALF = 256
VMEM_LIMIT = 58 * 1024 * 1024


def mm_nn(left, right):
    return lax.dot_general(left, right, (((1,), (0,)), ((), ())), preferred_element_type=F32)


def mm_nt(left, right):
    return lax.dot_general(left, right, (((1,), (1,)), ((), ())), preferred_element_type=F32)


def mm_tn(left, right):
    return lax.dot_general(left, right, (((0,), (0,)), ((), ())), preferred_element_type=F32)


def partners(dp):
    core = dp + 1 - 2 * lax.rem(dp, 2)
    x_side = dp + 2 - 4 * lax.rem(lax.div(dp, 2), 2)
    z_near = dp + 4 - 8 * lax.rem(lax.div(dp, 4), 2)
    z_far = dp + 8 - 16 * lax.rem(lax.div(dp, 8), 2)
    return core, x_side, z_near, z_far


def greet(targets):
    barrier = pltpu.get_barrier_semaphore()
    for target in targets:
        pl.semaphore_signal(barrier, inc=1, device_id=target, device_id_type=MESH)
    pl.semaphore_wait(barrier, len(targets))


def full_spec(shape):
    return pl.BlockSpec(shape, lambda *_: (0,) * len(shape))


def sds(shape, dtype):
    return jax.ShapeDtypeStruct(shape, dtype)


def row_block(index, mp):
    return pl.multiple_of(lax.rem(index + 4 * (1 - mp), 5) * HALF, HALF)


def ext_cols(index):
    return pl.multiple_of(jnp.where(index == 0, 0, HALF + HALF * index), HALF)


def norm_forward(values, norm_gain, norm_shift):
    row_mean = jnp.mean(values, axis=-1, keepdims=True)
    centred = values - row_mean
    inverse = lax.rsqrt(jnp.mean(centred * centred, axis=-1, keepdims=True) + NORM_EPS)
    normed = centred * inverse
    return (normed * norm_gain + norm_shift, normed, inverse)


def norm_backward(grad_rows, normed, inverse, norm_gain):
    scaled = grad_rows * norm_gain
    centre_term = jnp.mean(scaled, axis=-1, keepdims=True)
    slope_term = jnp.mean(scaled * normed, axis=-1, keepdims=True)
    return inverse * (scaled - centre_term - normed * slope_term)


def exact_gelu(values):
    return jax.nn.gelu(values, approximate=False)


def key_mask(key_count, length):
    position = lax.broadcasted_iota(jnp.int32, (1, 1, 1, length), 3)
    return position < key_count[:, None, None, None]


def masked_scores(queries, key_rows, key_count):
    raw_scores = jnp.einsum(
        "sqhe,skhe->shqk", queries, key_rows, preferred_element_type=jnp.float32
    )
    scaled = raw_scores * queries.shape[-1] ** (-0.5)
    return jnp.where(key_mask(key_count, key_rows.shape[1]), scaled, MASK_FILL)


def attend_backward(queries, key_rows, value_rows, key_count, log_total, attended_grad):
    scores = masked_scores(queries, key_rows, key_count)
    probs = jnp.exp(scores - log_total)
    probs_low = probs.astype(jnp.bfloat16)
    probs_grad = jnp.einsum(
        "sqhe,skhe->shqk", attended_grad, value_rows, preferred_element_type=jnp.float32
    )
    score_grad = probs * (probs_grad - jnp.sum(probs_grad * probs, axis=-1, keepdims=True))
    visible = key_mask(key_count, key_rows.shape[1])
    raw_grad = jnp.where(visible, score_grad * queries.shape[-1] ** (-0.5), 0.0).astype(
        jnp.bfloat16
    )
    query_grad = jnp.einsum(
        "shqk,skhe->sqhe", raw_grad, key_rows, preferred_element_type=jnp.float32
    )
    key_grad = jnp.einsum("shqk,sqhe->skhe", raw_grad, queries, preferred_element_type=jnp.float32)
    value_grad = jnp.einsum(
        "shqk,sqhe->skhe", probs_low, attended_grad, preferred_element_type=jnp.float32
    )
    return jnp.stack([query_grad, key_grad, value_grad])


def own_slice(values, own_start, own_rows):
    return lax.dynamic_slice_in_dim(values, own_start, own_rows, 0)


def contract_rows(left, right):
    return lax.dot_general(
        left, right, (((0,), (0,)), ((), ())), preferred_element_type=jnp.float32
    )


def contract_cols(left, right):
    return lax.dot_general(
        left, right, (((1,), (1,)), ((), ())), preferred_element_type=jnp.float32
    )


def adam_update(weight, gradient, moment_one, moment_two, step_rate, decay_rate):
    first_new = BETA_FIRST * moment_one + (1.0 - BETA_FIRST) * gradient
    second_new = BETA_SECOND * moment_two + (1.0 - BETA_SECOND) * gradient * gradient
    first_hat = first_new / (1.0 - BETA_FIRST**ADAM_STEP)
    second_hat = second_new / (1.0 - BETA_SECOND**ADAM_STEP)
    weight_new = weight - step_rate * (
        first_hat / (jnp.sqrt(second_hat) + ADAM_EPS) + decay_rate * weight
    )
    return (weight_new, first_new, second_new)


def local(
    patches,
    cotangent,
    key_count,
    w_qkv,
    w_proj,
    w_up,
    w_down,
    qv_bias,
    up_bias,
    vec_params,
    first_qkv,
    second_qkv,
    first_proj,
    second_proj,
    first_up,
    second_up,
    first_down,
    second_down,
    first_qv_bias,
    second_qv_bias,
    first_up_bias,
    second_up_bias,
    first_vec,
    second_vec,
):
    own_rows = patches.shape[0]
    seq_count = key_count.shape[0]
    own_start = lax.axis_index("mp") * own_rows
    local_width = w_proj.shape[0]
    local_heads = local_width // HD
    own_grad = cotangent.astype(jnp.float32)
    qkv_low = w_qkv.astype(jnp.bfloat16)
    proj_low = w_proj.astype(jnp.bfloat16)
    up_low = w_up.astype(jnp.bfloat16)
    down_low = w_down.astype(jnp.bfloat16)
    gain_one, shift_one = (vec_params[0], vec_params[1])
    gain_two, shift_two = (vec_params[2], vec_params[3])
    proj_shift, down_shift = (vec_params[4], vec_params[5])
    qkv_shift = jnp.stack([qv_bias[0], jnp.zeros_like(qv_bias[0]), qv_bias[1]])[:, None, :]
    gathered, grad_all = (
        lax.all_gather(patches, "mp", axis=0, tiled=True),
        lax.all_gather(cotangent, "mp", axis=0, tiled=True),
    )
    whole_rows = gathered.astype(jnp.float32)
    normed_all, unit_one, inverse_one = norm_forward(whole_rows, gain_one, shift_one)
    norm_one = normed_all.astype(jnp.bfloat16)
    projected = (
        jnp.einsum("td,cde->cte", norm_one, qkv_low, preferred_element_type=jnp.float32) + qkv_shift
    )
    shaped = projected.astype(jnp.bfloat16).reshape(3, seq_count, -1, local_heads, HD)
    queries, key_rows, value_rows = (shaped[0], shaped[1], shaped[2])
    scores = masked_scores(queries, key_rows, key_count)
    top_score = jnp.max(scores, axis=-1, keepdims=True)
    log_total = top_score + jnp.log(jnp.sum(jnp.exp(scores - top_score), axis=-1, keepdims=True))
    probs_low = jnp.exp(scores - log_total).astype(jnp.bfloat16)
    attended = jnp.einsum(
        "shqk,skhe->sqhe", probs_low, value_rows, preferred_element_type=jnp.float32
    )
    attended_low = attended.astype(jnp.bfloat16).reshape(-1, local_width)
    proj_part = jnp.dot(attended_low, proj_low, preferred_element_type=jnp.float32)
    resid_all = whole_rows + lax.psum(proj_part, "mp") + proj_shift
    mid_all, unit_two, inverse_two = norm_forward(resid_all, gain_two, shift_two)
    norm_two = mid_all.astype(jnp.bfloat16)
    up_pre = jnp.dot(norm_two, up_low, preferred_element_type=jnp.float32) + up_bias
    hidden_full, gelu_pull = jax.vjp(exact_gelu, up_pre)
    hidden_low = hidden_full.astype(jnp.bfloat16)
    down_part = jnp.dot(hidden_low, down_low, preferred_element_type=jnp.float32)
    out_all = (
        resid_all + lax.psum(down_part.astype(jnp.bfloat16), "mp").astype(jnp.float32) + down_shift
    )
    block_out = own_slice(out_all, own_start, own_rows)
    activations = block_out.astype(jnp.bfloat16)
    down_grad = contract_rows(hidden_low, grad_all)
    hidden_grad = contract_cols(grad_all, down_low)
    up_grad_rows = gelu_pull(hidden_grad)[0].astype(jnp.bfloat16)
    up_grad = contract_rows(norm_two, up_grad_rows)
    up_bias_grad = jnp.sum(up_grad_rows.astype(jnp.float32), axis=0)
    mid_part = contract_cols(up_grad_rows, up_low)
    mid_all_grad = lax.psum(mid_part.astype(jnp.bfloat16), "mp").astype(jnp.float32)
    resid_all_grad = grad_all.astype(jnp.float32) + norm_backward(
        mid_all_grad, unit_two, inverse_two, gain_two
    )
    branch_low = resid_all_grad.astype(jnp.bfloat16)
    own_branch = own_slice(branch_low, own_start, own_rows)
    mid_grad = own_slice(mid_all_grad, own_start, own_rows)
    mid_unit = own_slice(unit_two, own_start, own_rows)
    proj_grad = contract_rows(attended_low, branch_low)
    attended_grad = (
        contract_cols(branch_low, proj_low)
        .astype(jnp.bfloat16)
        .reshape(seq_count, -1, local_heads, HD)
    )
    qkv_grads = attend_backward(queries, key_rows, value_rows, key_count, log_total, attended_grad)
    qkv_grad_rows = qkv_grads.reshape(3, -1, local_width).astype(jnp.bfloat16)
    qkv_grad = jnp.einsum(
        "td,cte->cde", norm_one, qkv_grad_rows, preferred_element_type=jnp.float32
    )
    qkv_grad_sums = jnp.sum(qkv_grad_rows.astype(jnp.float32), axis=1)
    qv_bias_grad = jnp.stack([qkv_grad_sums[0], qkv_grad_sums[2]])
    first_part = jnp.einsum(
        "cte,cde->td", qkv_grad_rows, qkv_low, preferred_element_type=jnp.float32
    )
    first_all = lax.psum(first_part.astype(jnp.bfloat16), "mp").astype(jnp.float32)
    input_all = resid_all_grad + norm_backward(first_all, unit_one, inverse_one, gain_one)
    input_grad = own_slice(input_all, own_start, own_rows)
    own_first_grad = own_slice(first_all, own_start, own_rows)
    own_unit_one = own_slice(unit_one, own_start, own_rows)
    vec_grad = jnp.stack(
        [
            jnp.sum(own_first_grad * own_unit_one, axis=0),
            jnp.sum(own_first_grad, axis=0),
            jnp.sum(mid_grad * mid_unit, axis=0),
            jnp.sum(mid_grad, axis=0),
            jnp.sum(own_branch.astype(jnp.float32), axis=0),
            jnp.sum(own_grad, axis=0),
        ]
    )
    summed = (
        lax.psum(qkv_grad.astype(jnp.bfloat16), "dp").astype(jnp.float32),
        lax.psum(proj_grad.astype(jnp.bfloat16), "dp").astype(jnp.float32),
        lax.psum(up_grad.astype(jnp.bfloat16), "dp").astype(jnp.float32),
        lax.psum(down_grad.astype(jnp.bfloat16), "dp").astype(jnp.float32),
        lax.psum(qv_bias_grad.astype(jnp.bfloat16), "dp").astype(jnp.float32),
        lax.psum(up_bias_grad.astype(jnp.bfloat16), "dp").astype(jnp.float32),
        lax.psum(vec_grad.astype(jnp.bfloat16), "dp").astype(jnp.float32),
    )
    split_square = jnp.float32(0.0)
    for gradient in summed[:6]:
        split_square = split_square + jnp.sum(gradient * gradient)
    vec_total, split_total = lax.psum((summed[6], split_square), "mp")
    grad_norm = jnp.sqrt(split_total + jnp.sum(vec_total * vec_total))
    factor = jnp.minimum(1.0, CLIP_NORM / (grad_norm + 1e-06))
    qkv_new, qkv_first, qkv_second = adam_update(
        w_qkv, summed[0] * factor, first_qkv, second_qkv, MATRIX_RATE, DECAY_RATE
    )
    proj_new, proj_first, proj_second = adam_update(
        w_proj, summed[1] * factor, first_proj, second_proj, MATRIX_RATE, DECAY_RATE
    )
    up_new, up_first, up_second = adam_update(
        w_up, summed[2] * factor, first_up, second_up, MATRIX_RATE, DECAY_RATE
    )
    down_new, down_first, down_second = adam_update(
        w_down, summed[3] * factor, first_down, second_down, MATRIX_RATE, DECAY_RATE
    )
    qvb_new, qvb_first, qvb_second = adam_update(
        qv_bias, summed[4] * factor, first_qv_bias, second_qv_bias, VECTOR_RATE, 0.0
    )
    upb_new, upb_first, upb_second = adam_update(
        up_bias, summed[5] * factor, first_up_bias, second_up_bias, VECTOR_RATE, 0.0
    )
    vec_new, vec_first, vec_second = adam_update(
        vec_params, vec_total * factor, first_vec, second_vec, VECTOR_RATE, 0.0
    )
    return (
        activations,
        input_grad,
        grad_norm,
        qkv_new,
        qkv_first,
        qkv_second,
        proj_new,
        proj_first,
        proj_second,
        up_new,
        up_first,
        up_second,
        down_new,
        down_first,
        down_second,
        qvb_new,
        qvb_first,
        qvb_second,
        upb_new,
        upb_first,
        upb_second,
        vec_new,
        vec_first,
        vec_second,
    )


class Transfers:
    def __init__(self, send_sem, recv_sem):
        self.sems = (send_sem, recv_sem)
        self.all = {}

    def make(self, key):
        index, src, dst, target = self.all[key]
        return pltpu.make_async_remote_copy(
            src_ref=src(), dst_ref=dst(), send_sem=self.sems[0].at[index], recv_sem=self.sems[1].at[index],
            device_id=target, device_id_type=MESH,
        )

    def plan(self, key, src, dst, target):
        self.all[key] = (len(self.all), src, dst, target)

    def start(self, key, *views):
        if views:
            self.plan(key, *views)
        self.make(key).start()

    def arrive(self, key):
        self.make(key).wait_recv()

    def finish(self):
        for key in self.all:
            self.make(key).wait_send()


class Loads:
    def __init__(self, sem):
        self.sem = sem
        self.all = {}

    def make(self, key):
        index, src, dst = self.all[key]
        return pltpu.make_async_copy(src(), dst(), self.sem.at[index])

    def plan(self, key, src, dst):
        self.all[key] = (len(self.all), src, dst)

    def start(self, key, *views):
        if views:
            self.plan(key, *views)
        self.make(key).start()

    def wait(self, key):
        self.make(key).wait()


def layer_norm_rows(rows, gain, shift):
    centred = rows - jnp.mean(rows, axis=-1, keepdims=True)
    inverse = lax.rsqrt(jnp.mean(centred * centred, axis=-1, keepdims=True) + NORM_EPS)
    unit = centred * inverse
    return unit * gain + shift, unit, inverse


def layer_norm_back(grad, unit, inverse, gain):
    scaled = grad * gain
    centre = jnp.mean(scaled, axis=-1, keepdims=True)
    slope = jnp.mean(scaled * unit, axis=-1, keepdims=True)
    return inverse * (scaled - centre - unit * slope)


def head_rows(block, sub):
    return pl.ds(pl.multiple_of(block * 128 + sub * HD, HD), HD)


def head_cols(block):
    return pl.ds(pl.multiple_of(block * 128, 128), 128)


def key_bias(shape, mp, count, shared):
    slot = lax.broadcasted_iota(jnp.int32, shape, 0)
    if shared:
        slot = lax.rem(slot + HALF * mp, SEQ)
    return jnp.where(slot < count, 0.0, MASK_FILL).astype(BF)


def widen(rows, sub):
    zeros = jnp.zeros_like(rows)
    row = lax.broadcasted_iota(jnp.int32, rows.shape, 0)
    ones = jnp.where(row == 0, 1.0, 0.0).astype(BF)
    parts = [zeros] * 4
    parts[sub] = rows
    parts[(sub + 1) % 4] = ones
    return jnp.concatenate(parts, axis=0)


def widen_plain(rows, sub):
    parts = [jnp.zeros_like(rows)] * 4
    parts[sub] = rows
    return jnp.concatenate(parts, axis=0)


def score_tile(key_block, bias, query_rows, sub):
    lane = lax.broadcasted_iota(jnp.int32, key_block.shape, 1)
    keys = jnp.where(lane // HD == (sub + 1) % 4, bias, key_block)
    return mm_nn(keys, widen(query_rows, sub))


def forward_kernel(
    count_ref, qkv_ref, proj_ref, up_ref, down_ref, qv_ref, up_bias_ref, x_ref, vec_ref,
    wt_out, wp_out, wu_out, wd_out, sm_out,
    nt_out, qt_out, kt_out, k_out, v_out, ot_out, lse_out,
    wt_ref, own_proj, own_up, own_down, sm_ref, other_ref,
    norm_ref, nt_ref, qt_ref, kt_ref, vt_ref, k_ref, v_ref, ot_ref, lse_ref, bias_ref, s_ref,
    send_sem, recv_sem, local_sem,
):
    dp, mp = lax.axis_index("dp"), lax.axis_index("mp")
    peer = 1 - mp
    core, x_side, _, _ = partners(dp)
    quarter = lax.rem(dp, 4)
    x_quarter = lax.rem(quarter + 2, 4)
    gain, shift = vec_ref[0:1, :], vec_ref[1:2, :]
    greet([{"mp": peer}, {"dp": core}, {"dp": x_side}])

    remote, local = [], []

    class Transfer:
        def __init__(self, src, dst, target):
            self.index = len(remote)
            self.views = (src, dst, target)
            remote.append(self)
            self.make().start()

        def make(self):
            src, dst, target = self.views
            return pltpu.make_async_remote_copy(
                src_ref=src(), dst_ref=dst(), send_sem=send_sem.at[self.index],
                recv_sem=recv_sem.at[self.index], device_id=target, device_id_type=MESH,
            )

        def wait_recv(self):
            self.make().wait_recv()

        def wait_send(self):
            self.make().wait_send()

    def send(src, dst, target):
        return Transfer(src, dst, target)

    def keep(src, dst):
        copy = pltpu.make_async_copy(src, dst, local_sem.at[len(local)])
        copy.start()
        local.append(copy)

    def span(start, size):
        return pl.ds(pl.multiple_of(start, 16), size)

    pieces = []
    for part in range(3):
        pieces.append((wt_ref.at[mp, part], lambda side, part=part: wt_ref.at[side, part], 64, 0))
    pieces.append((own_proj, lambda side: wp_out.at[side], 64, 0))
    for shard, out, rows in ((own_up, wu_out, 128), (own_down, wd_out, 256)):
        for part in range(2):
            pieces.append((shard, lambda side, out=out: out.at[side], rows // 2, part * rows * 2))

    def place(ref, index, part):
        rows, base = pieces[index][2], pieces[index][3]
        return ref.at[span(base + part * rows, rows), :]

    first, second, third = {}, {}, {}

    def to_peer(index):
        first[index] = send(
            lambda: place(pieces[index][0], index, quarter),
            lambda: place(pieces[index][1](mp), index, quarter), {"mp": peer},
        )

    def to_sides(index):
        first[index].wait_recv()
        at = lambda: place(pieces[index][1](peer), index, quarter)
        second[index] = send(at, at, {"dp": x_side})
        third[index] = [send(at, at, {"dp": core})]

    def to_core(index):
        second[index].wait_recv()
        at = lambda: place(pieces[index][1](peer), index, x_quarter)
        third[index].append(send(at, at, {"dp": core}))

    def arrive(index):
        for copy in third[index]:
            copy.wait_recv()

    own_half = pl.multiple_of((1 - mp) * 4 * HALF, HALF)
    for part in range(3):
        wt_ref[mp, part] = qkv_ref[part].T.astype(BF)
        to_peer(part)
    sm_ref[mp] = jnp.zeros((8, 1024), F32)
    sm_ref[mp, 0:1, :] = up_bias_ref[...]
    sm_ref[mp, 1:3, 0:256] = qv_ref[...]
    small_copy = send(lambda: sm_ref.at[mp], lambda: sm_ref.at[mp], {"mp": peer})
    own_proj[...] = proj_ref[...].astype(BF)
    own_up[...] = up_ref[...].astype(BF)
    own_down[...] = down_ref[...].astype(BF)
    keep(wt_ref.at[mp], wt_out.at[mp])
    keep(own_proj, wp_out.at[mp])
    keep(own_up, wu_out.at[mp])
    keep(own_down, wd_out.at[mp])

    def as_column(row):
        return jnp.broadcast_to(row, (8, row.shape[1])).T[:, 0:1]

    def normalise(group, part, rows):
        base = group * SEQ + part * HALF
        norm = layer_norm_rows(rows.astype(F32), gain, shift)[0].astype(BF)
        norm_ref[span(base, HALF), :] = norm
        nt_ref[:, pl.ds(pl.multiple_of(base, HALF), HALF)] = norm.T

    def project(side, group):
        base = pl.multiple_of(group * SEQ, SEQ)
        at = pl.ds(base, SEQ)
        own = pl.ds(pl.multiple_of(side * 256, 256), 256)
        norm = norm_ref[at, :]
        q_bias, v_bias = sm_ref[side, 1:2, 0:256], sm_ref[side, 2:3, 0:256]
        scale = LOG2E * HD ** (-0.5)
        qt_ref[own, at] = ((mm_nt(wt_ref[side, 0], norm) + as_column(q_bias)) * scale).astype(BF)
        kt_ref[own, at] = mm_nt(wt_ref[side, 1], norm).astype(BF)
        vt_ref[own, :] = (mm_nt(wt_ref[side, 2], norm) + as_column(v_bias)).astype(BF)
        k_ref[at, own] = mm_nt(norm, wt_ref[side, 1]).astype(BF)
        v_ref[at, own] = (mm_nt(norm, wt_ref[side, 2]) + v_bias).astype(BF)

    def attend(side, group, queries, between):
        base = pl.multiple_of(group * SEQ, SEQ)
        keys_at, queries_at = pl.ds(base, SEQ), pl.ds(base, queries)
        bias = bias_ref[group]

        def scores(block, sub):
            return score_tile(
                k_ref[keys_at, head_cols(block)], bias, qt_ref[head_rows(block, sub), queries_at], sub
            )

        s_ref[0, :, :queries] = scores(2 * side, 0)

        def body(step, carry):
            block = 2 * side + step
            for sub in range(4):
                following = (block, sub + 1) if sub < 3 else (2 * side + 1, 0)
                s_ref[(sub + 1) % 2, :, :queries] = scores(*following)
                tile = s_ref[sub % 2, :, :queries]
                top = jnp.max(tile, axis=0, keepdims=True)
                weights = jnp.exp2(tile - top)
                rows = head_rows(block, sub)
                values = jnp.concatenate([vt_ref[rows, :], jnp.ones((16, SEQ), BF)], axis=0)
                mixed = mm_nn(values, weights.astype(BF))
                total = mixed[HD : HD + 1]
                ot_ref[rows, queries_at] = (mixed[:HD] * (1.0 / total)).astype(BF)
                lse_ref[group, block, sub : sub + 1, :queries] = top + jnp.log2(total)

            @pl.when(step == 0)
            def _():
                between()

            return carry

        lax.fori_loop(0, 2, body, 0)

    def nothing():
        pass

    def unit(side, group, queries, early=nothing, between=nothing):
        project(side, group)
        early()
        attend(side, group, queries, between)
        at = pl.ds(pl.multiple_of(group * SEQ, SEQ), SEQ)
        own = pl.ds(pl.multiple_of(side * 256, 256), 256)
        keep(qt_ref.at[own, at], qt_out.at[own, at])
        keep(kt_ref.at[own, at], kt_out.at[own, at])
        keep(ot_ref.at[own, at], ot_out.at[own, at])
        keep(k_ref.at[at, own], k_out.at[at, own])
        keep(v_ref.at[at, own], v_out.at[at, own])

    def in_turn(*calls):
        def run():
            for call, *indices in calls:
                for index in indices:
                    call(index)

        return run

    for group in (1, 2):
        bias_ref[group] = key_bias((SEQ, 128), mp, count_ref[3 * mp + group - 1], False)
        for part in range(2):
            normalise(group, part, x_ref[pl.ds(row_block(2 * group - 1 + part, mp), HALF), :])
        if group == 1:
            to_peer(3)
            to_peer(4)
    bias_ref[0] = key_bias((SEQ, 128), mp, count_ref[2], True)
    normalise(0, 0, x_ref[pl.ds(row_block(0, mp), HALF), :])
    for index in range(3):
        to_sides(index)
    to_peer(5)
    unit(mp, 1, SEQ)
    in_turn((to_sides, 3, 4), (to_peer, 6))()
    unit(mp, 2, SEQ, between=in_turn((to_core, 0, 1, 2), (to_sides, 5), (to_peer, 7)))
    small_copy.wait_recv()
    keep(sm_ref, sm_out)
    for index in range(3):
        arrive(index)
    keep(wt_ref.at[peer], wt_out.at[peer])
    rows_copy = send(lambda: x_ref.at[pl.ds(own_half, HALF), :], lambda: other_ref, {"mp": peer})
    unit(peer, 1, SEQ, early=in_turn((to_sides, 6)), between=in_turn((to_core, 3, 4)))
    in_turn((to_sides, 7))()
    unit(peer, 2, SEQ, early=in_turn((to_core, 5)), between=in_turn((to_core, 6)))
    rows_copy.wait_recv()
    normalise(0, 1, other_ref[...])
    keep(nt_ref, nt_out)
    unit(mp, 0, HALF, between=in_turn((to_core, 7)))
    unit(peer, 0, HALF)
    keep(lse_ref, lse_out)
    for index in range(3, 8):
        arrive(index)
    for copy in remote:
        copy.wait_send()
    for copy in local:
        copy.wait()


def forward(key_count, w_qkv, w_proj, w_up, w_down, qv_bias, up_bias, patches, vec_params):
    ext = 3 * SEQ
    vmem, hbm = pl.BlockSpec(memory_space=pltpu.VMEM), pl.BlockSpec(memory_space=pl.ANY)
    return pl.pallas_call(
        forward_kernel,
        out_shape=[
            sds((2, 3, 256, 512), BF), sds((2, 256, 512), BF), sds((2, 512, 1024), BF),
            sds((2, 1024, 512), BF), sds((2, 8, 1024), F32),
            sds((512, ext), BF), sds((512, ext), BF), sds((512, ext), BF), sds((ext, 512), BF),
            sds((ext, 512), BF), sds((512, ext), BF), sds((3, 4, 8, SEQ), F32),
        ],
        in_specs=[pl.BlockSpec(memory_space=pltpu.SMEM)] + [vmem] * 8,
        out_specs=[hbm] * 12,
        scratch_shapes=[
            pltpu.VMEM((2, 3, 256, 512), BF), pltpu.VMEM((256, 512), BF), pltpu.VMEM((512, 1024), BF),
            pltpu.VMEM((1024, 512), BF), pltpu.VMEM((2, 8, 1024), F32), pltpu.VMEM((HALF, 512), BF),
            pltpu.VMEM((ext, 512), BF), pltpu.VMEM((512, ext), BF), pltpu.VMEM((512, ext), BF),
            pltpu.VMEM((512, ext), BF), pltpu.VMEM((512, SEQ), BF), pltpu.VMEM((ext, 512), BF),
            pltpu.VMEM((ext, 512), BF), pltpu.VMEM((512, ext), BF), pltpu.VMEM((3, 4, 8, SEQ), F32),
            pltpu.VMEM((3, SEQ, 128), BF), pltpu.VMEM((2, SEQ, SEQ), F32),
            pltpu.SemaphoreType.DMA((34,)), pltpu.SemaphoreType.DMA((34,)), pltpu.SemaphoreType.DMA((40,)),
        ],
        compiler_params=pltpu.CompilerParams(
            collective_id=0, has_side_effects=True, vmem_limit_bytes=VMEM_LIMIT
        ),
        name="forward",
    )(key_count, w_qkv, w_proj, w_up, w_down, qv_bias, up_bias, patches, vec_params)


def mlp_kernel(
    x_ref, dy_ref, ot_ref, wp_ref, wu_ref, wd_ref, vec_ref, small_ref,
    act_ref, dres_ref, dot_ref, own_out, fore_out, gp_ref, vsum_ref, bsum_ref,
    res_ref, n2_ref, out_ref, dn_ref, hid_ref, dup_ref, dyc_ref, br_ref,
    g_ref, fore_ref, fore_core, own_core, own_peer, send_sem, recv_sem,
):
    step = pl.program_id(0)
    dp, mp = lax.axis_index("dp"), lax.axis_index("mp")
    peer, core, core_bit = 1 - mp, partners(dp)[0], lax.rem(dp, 2)
    side, part = jnp.where(step < 2, peer, mp), lax.rem(step, 2)
    sent = Transfers(send_sem, recv_sem)
    kept = pl.ds(pl.multiple_of(core_bit * HALF, HALF), HALF)
    away = pl.ds(pl.multiple_of(HALF - core_bit * HALF, HALF), HALF)
    for turn in range(2):
        sent.plan(
            ("F", turn), lambda turn=turn: g_ref.at[turn, :, away, :], lambda turn=turn: fore_core.at[turn],
            {"dp": core},
        )
        sent.plan(
            ("O", turn), lambda turn=turn: g_ref.at[2 + turn, :, away, :],
            lambda turn=turn: own_core.at[turn], {"dp": core},
        )
    sent.plan("peer", lambda: fore_ref, lambda: own_peer, {"mp": peer})
    gain, shift = vec_ref[2:3, :], vec_ref[3:4, :]
    w_proj = wp_ref[...].reshape(512, 512)

    def rows(index):
        return pl.ds(pl.multiple_of(index * HALF, HALF), HALF)

    @pl.when(step == 0)
    def _():
        greet([{"dp": core}, {"mp": peer}])

        def body(index, carry):
            x_rows = x_ref[pl.ds(row_block(index, mp), HALF), :].astype(F32)
            mixed = ot_ref[:, pl.ds(ext_cols(index), HALF)]
            resid = x_rows + mm_tn(mixed, w_proj) + vec_ref[4:5, :]
            res_ref[rows(index), :] = resid
            n2_ref[rows(index), :] = layer_norm_rows(resid, gain, shift)[0].astype(BF)
            out_ref[rows(index), :] = resid + vec_ref[5:6, :]
            dn_ref[rows(index), :] = jnp.zeros((HALF, 512), F32)
            dyc_ref[rows(index), :] = dy_ref[pl.ds(row_block(index, mp), HALF), :]
            return carry

        lax.fori_loop(0, 5, body, 0, unroll=True)

    lanes = pl.ds(pl.multiple_of(part * 512, 512), 512)
    w_up, w_down = wu_ref[side, :, lanes], wd_ref[side, lanes, :]
    up_bias = small_ref[side, 0:1, lanes]

    def up_of(index):
        return mm_nn(n2_ref[index * HALF : index * HALF + HALF, :], w_up) + up_bias

    total = jnp.zeros((8, 512), F32)
    pre = up_of(0)
    for index in range(5):
        at = slice(index * HALF, index * HALF + HALF)
        up_pre = pre
        if index < 4:
            pre = up_of(index + 1)
        dhid = mm_nt(dyc_ref[at, :], w_down)
        cumulative = 0.5 * (1.0 + lax.erf(up_pre * (0.5**0.5)))
        density = jnp.exp(-0.5 * up_pre * up_pre) * 0.3989422804014327
        hidden = (up_pre * cumulative).astype(BF)
        hid_ref[at, :] = hidden
        slope = cumulative + up_pre * density
        dup = (dhid * slope).astype(BF)
        dup_ref[at, :] = dup
        total = total + jnp.sum(dup.astype(F32).reshape(HALF // 8, 8, 512), axis=0)
        out_ref[at, :] += mm_nn(hidden, w_down)
        dn_ref[at, :] += mm_nt(dup, w_up)
        if index == 1:

            @pl.when(step == 1)
            def _():
                sent.arrive(("F", 0))
                fore_ref[...] = g_ref[0, :, kept, :] + fore_core[0]
                sent.start("peer")

            @pl.when(step == 2)
            def _():
                sent.arrive(("F", 1))
                fore_out[...] = g_ref[1, :, kept, :] + fore_core[1]

    bsum_ref[2 * side + part] = total
    g_ref[step, 0] = mm_tn(hid_ref[...], dyc_ref[...]).astype(BF)
    g_ref[step, 1] = mm_tn(n2_ref[...], dup_ref[...]).astype(BF)
    for turn, key in enumerate((("F", 0), ("F", 1), ("O", 0), ("O", 1))):

        @pl.when(step == turn)
        def _():
            sent.start(key)

    @pl.when(step == 3)
    def _():
        vsum_ref[...] = jnp.zeros_like(vsum_ref)

        def body(index, carry):
            at = rows(index)
            act_ref[pl.ds(row_block(index, mp), HALF), :] = out_ref[at, :].astype(BF)
            _, unit, inverse = layer_norm_rows(res_ref[at, :], gain, shift)
            dn = dn_ref[at, :]
            dy = dyc_ref[at, :].astype(F32)
            dres = dy + layer_norm_back(dn, unit, inverse, gain)
            dres_ref[at, :] = dres
            branch = dres.astype(BF)
            br_ref[at, :] = branch
            dot_ref[:, pl.ds(ext_cols(index), HALF)] = mm_nt(w_proj, branch).astype(BF)
            sums = [dn * unit, dn, branch.astype(F32), dy]
            for place, value in enumerate(sums):
                vsum_ref[place] += jnp.sum(value.reshape(HALF // 8, 8, 512), axis=0)
            return carry

        lax.fori_loop(0, 5, body, 0, unroll=True)
        mixed = jnp.concatenate([ot_ref[:, 0:HALF], ot_ref[:, SEQ:]], axis=1)
        gp_ref[...] = mm_nn(mixed, br_ref[...]).astype(BF).reshape(2, 256, 512)
        sent.arrive(("O", 0))
        sent.arrive(("O", 1))
        sent.arrive("peer")
        near = g_ref[2, :, kept, :].astype(F32) + own_core[0].astype(F32)
        own_out[0] = (near + own_peer[...].astype(F32)).astype(BF)
        own_out[1] = g_ref[3, :, kept, :] + own_core[1]
        sent.finish()


def mlp(patches, cotangent, ot, wp, wu, wd, vec_params, small):
    rows = patches.shape[0]
    ext = 3 * SEQ
    return pl.pallas_call(
        mlp_kernel,
        grid=(4,),
        out_shape=[
            sds((rows, 512), BF), sds((rows, 512), F32), sds((512, ext), BF), sds((2, 2, HALF, 512), BF),
            sds((2, HALF, 512), BF), sds((2, 256, 512), BF), sds((4, 8, 512), F32), sds((4, 8, 512), F32),
        ],
        in_specs=[
            full_spec((rows, 512)), full_spec((rows, 512)), full_spec((512, ext)), full_spec(wp.shape),
            full_spec(wu.shape), full_spec(wd.shape), full_spec(vec_params.shape), full_spec(small.shape),
        ],
        out_specs=[
            full_spec((rows, 512)), full_spec((rows, 512)), full_spec((512, ext)),
            full_spec((2, 2, HALF, 512)), full_spec((2, HALF, 512)),
            full_spec((2, 256, 512)), full_spec((4, 8, 512)), full_spec((4, 8, 512)),
        ],
        scratch_shapes=[
            pltpu.VMEM((rows, 512), F32), pltpu.VMEM((rows, 512), BF), pltpu.VMEM((rows, 512), F32),
            pltpu.VMEM((rows, 512), F32), pltpu.VMEM((rows, 512), BF), pltpu.VMEM((rows, 512), BF),
            pltpu.VMEM((rows, 512), BF), pltpu.VMEM((rows, 512), BF), pltpu.VMEM((4, 2, 512, 512), BF),
            pltpu.VMEM((2, HALF, 512), BF), pltpu.VMEM((2, 2, HALF, 512), BF),
            pltpu.VMEM((2, 2, HALF, 512), BF), pltpu.VMEM((2, HALF, 512), BF),
            pltpu.SemaphoreType.DMA((5,)), pltpu.SemaphoreType.DMA((5,)),
        ],
        compiler_params=pltpu.CompilerParams(
            collective_id=2, has_side_effects=True, vmem_limit_bytes=VMEM_LIMIT
        ),
        name="mlp",
    )(patches, cotangent, ot, wp, wu, wd, vec_params, small)


SCHEDULE = (
    (
        ("F", 2, 1), ("F", 4, 0), ("O", 0, 1), ("O", 1, 1), ("O", 4, 0),
    ),
    (
    ),
    (
        ("F", 3, 1),
    ),
    (
        ("O", 0, 2),
    ),
    (
    ),
    (
        ("F", 4, 1), ("O", 1, 2), ("O", 2, 1),
    ),
    (
    ),
    (
    ),
    (
        ("F", 5, 0), ("O", 0, 3), ("O", 3, 1),
    ),
    (
        ("O", 1, 3),
    ),
    (
        ("F", 5, 1), ("O", 4, 1),
    ),
    (
        ("O", 2, 2),
    ),
    (
        ("F", 6, 0), ("O", 0, 4),
    ),
    (
        ("O", 3, 2),
    ),
    (
        ("F", 6, 1), ("O", 1, 4),
    ),
    (
        ("O", 4, 2),
    ),
    (
        ("O", 0, 5), ("O", 2, 3), ("O", 5, 0),
    ),
    (
    ),
    (
        ("O", 0, 6), ("O", 1, 5), ("O", 3, 3),
    ),
    (
        ("O", 4, 3),
    ),
    (
        ("O", 1, 6), ("O", 2, 4), ("O", 6, 0),
    ),
    (
        ("O", 5, 1),
    ),
    (
    ),
    (
        ("O", 3, 4),
    ),
    (
        ("O", 6, 1),
    ),
    (
        ("O", 4, 4),
    ),
    (
        ("O", 2, 5), ("small", 0), ("O", 5, 3), ("O", 2, 6), ("O", 3, 5), ("O", 4, 5), ("O", 3, 6),
        ("small", 1), ("O", 4, 6), ("O", 6, 3), ("small", 2), ("square", 0), ("square", 1), ("O", 5, 5),
        ("square", 2), ("O", 5, 6), ("O", 6, 5), ("O", 6, 6),
    ),
)


def cut(ref, start, size):
    rows = pl.ds(pl.multiple_of(start, 16), size)
    return ref.at[:, rows, :] if len(ref.shape) == 3 else ref.at[rows, :]


WIDE = (5, 6)
PIECES = ((512, 512), (512, 512), (512, 512), (512, 512), (256, 512), (3, 512, 128), (3, 512, 128))


def piece_rows(index, size):
    return (*PIECES[index][:-2], PIECES[index][-2] // size, PIECES[index][-1])


def backward_kernel(
    count_ref, qt_in, kt_in, dot_in, ot_in, k_in, v_in, lse_ref, nt_in, wt_in,
    own_in, fore_in, gp_in, x_in, dres_in, vec_ref, two_ref, up_sum_ref,
    grad_out, down_out, up_out, proj_out, qkv_out, small_out, norm_out,
    qt_ref, kt_ref, dot_ref, ot_ref, k_ref, v_ref, nt_ref, wt_ref, x_ref, dres_ref,
    shared_ref, grads_ref, bias_ref, s_ref, dp_ref, g_ref, bsum_ref,
    far_send, far_recv, early_core, early_part, early_all, late_core, late_part, late_all, square_sum, square_core, square_all, *rest,
):
    buffers, (send_sem, recv_sem, local_sem) = rest[:-3], rest[-3:]
    dp, mp = lax.axis_index("dp"), lax.axis_index("mp")
    peer = 1 - mp
    core, x_side, _, _ = partners(dp)
    to_core, to_peer, to_x = {"dp": core}, {"mp": peer}, {"dp": x_side}
    core_bit, x_bit = lax.rem(dp, 2), lax.rem(lax.div(dp, 2), 2)
    chip, floor = lax.div(dp, 2), lax.div(dp, 4)

    def ring(index):
        return (chip, 8, 2) if index in WIDE else (floor, 4, 4)
    sent, loads = Transfers(send_sem, recv_sem), Loads(local_sem)

    def block_at(place):
        return 2 * jnp.where(place < 2, peer, mp) + lax.rem(place, 2)

    def source(index, side):
        if index == 4:
            return gp_in.at[side]
        return g_ref.at[index - 5 + (0 if side is peer else 2)]

    def result(index):
        if index < 4:
            lanes = slice(index // 2 * 512, index // 2 * 512 + 512)
            return up_out.at[:, lanes] if index % 2 else down_out.at[lanes, :]
        if index == 4:
            return proj_out
        return qkv_out.at[:, :, slice((index - 5) * 128, (index - 5) * 128 + 128)]

    def piece_buffers(index):
        return buffers[8 * index : 8 * index + 8]

    def region(index):
        half = PIECES[index][-2] // 2
        if index in WIDE:
            return core_bit * half, half
        return core_bit * half + x_bit * (half // 2), half // 2

    names = ("qt", "kt", "dot", "ot", "k", "v")
    sources = (qt_in, kt_in, dot_in, ot_in, k_in, v_in)
    homes = (qt_ref, kt_ref, dot_ref, ot_ref, k_ref, v_ref)
    for place in range(4):
        rows = pl.ds(pl.multiple_of(block_at(place) * 128, 128), 128)
        for name, src, dst in zip(names, sources, homes):
            loads.plan(
                (name, place),
                lambda src=src, rows=rows: src.at[rows, :] if src.shape[0] == 512 else src.at[:, rows],
                lambda dst=dst, place=place: dst.at[place],
            )

    def load_block(place):
        for name in names:
            loads.start((name, place))

    def loaded(place):
        for name in names:
            loads.wait((name, place))

    load_block(0)
    loads.start("wt", lambda: wt_in, lambda: wt_ref)
    for index in range(4):
        loads.plan(
            ("kept", index, 2), lambda index=index: own_in.at[index // 2, index % 2],
            lambda index=index: piece_buffers(index)[2],
        )
        if index > 1:
            loads.plan(
                ("kept", index, 0), lambda index=index: fore_in.at[index % 2],
                lambda index=index: piece_buffers(index)[0],
            )
    half = PIECES[4][-2] // 2
    for side, slot in ((peer, 0), (mp, 2)):
        loads.plan(
            ("kept", 4, slot), lambda side=side: cut(source(4, side), core_bit * half, half),
            lambda slot=slot: piece_buffers(4)[slot],
        )
    for key in ((2, 0), (0, 2), (1, 2), (3, 0), (2, 2), (3, 2), (4, 0), (4, 2)):
        loads.start(("kept", *key))
    loads.plan("nt", lambda: nt_in, lambda: nt_ref)
    loads.plan("x", lambda: x_in, lambda: x_ref)
    loads.plan("dres", lambda: dres_in, lambda: dres_ref)
    chips = [
        {"dp": lax.rem(dp + 2 * step, 16), "mp": side} for side in (mp, peer) for step in range(8)
    ][1:]
    greet([to_core] + chips)

    def plan_piece(index):
        total = PIECES[index][-2]
        half = total // 2
        kept = core_bit * half
        fore, fore_core, own, own_core, own_peer, own_x, landing, out = piece_buffers(index)
        away = (1 - core_bit) * half
        if index > 1:
            sent.plan(("F", index, 1), lambda: fore, lambda: own_peer, to_peer)
        if index > 3:
            sent.plan(("F", index, 0), lambda: cut(source(index, peer), away, half), lambda: fore_core, to_core)
            sent.plan(("O", index, 0), lambda: cut(source(index, mp), away, half), lambda: own_core, to_core)
        if index not in WIDE:
            other_x = (1 - x_bit) * (half // 2)
            sent.plan(("O", index, 1), lambda: cut(own, other_x, half // 2), lambda: own_x, to_x)
        first, size = region(index)
        me, members, stride = ring(index)
        size //= members
        for step in range(1, members):
            target = {"dp": lax.rem(dp + stride * step, 16)}
            their = lax.rem(me + step, members) * size + first
            mine = me * size + first
            sent.plan(
                ("O", index, 2, step), lambda their=their: cut(own, their - kept, size),
                lambda step=step: landing.at[step - 1], target,
            )
            place = lambda mine=mine: cut(out, mine, size)
            sent.plan(("O", index, 3, step), place, place, target)
        if index not in WIDE:
            across = lambda: cut(out, region(index)[0], half // 2)
            sent.plan(("O", index, 4), across, across, to_x)
        whole = lambda: cut(out, kept, half)
        sent.plan(("O", index, 5), whole, whole, to_core)
        loads.plan(("out", index), lambda: out, lambda: result(index))

    def event(kind, index, stage):
        total = PIECES[index][-2]
        half = total // 2
        kept = core_bit * half
        wide = index in WIDE
        fore, fore_core, own, own_core, own_peer, own_x, landing, out = piece_buffers(index)
        first, size = region(index)
        me, members, _ = ring(index)
        size //= members

        def each(stage, call):
            for step in range(1, members):
                call(("O", index, stage, step))

        if stage == 0:
            sent.start((kind, index, 0))
        elif kind == "F":
            if index > 3:
                sent.arrive((kind, index, 0))
            if index < 4:
                loads.wait(("kept", index, 0))
            elif index < 5:
                loads.wait(("kept", index, 0))
                fore[...] += fore_core[...]
            else:
                fore[...] = cut(source(index, peer), kept, half)[...] + fore_core[...]
            sent.start((kind, index, 1))
        elif stage == 1:
            if index > 3:
                sent.arrive((kind, index, 0))
            if index > 1:
                sent.arrive(("F", index, 1))
            if index < 5:
                loads.wait(("kept", index, 2))
            if index > 1:
                base = (own if index < 5 else cut(source(index, mp), kept, half))[...].astype(F32)
                if index > 3:
                    base = base + own_core[...].astype(F32)
                own[...] = (base + own_peer[...].astype(F32)).astype(BF)
            if wide:
                each(2, sent.start)
            else:
                sent.start((kind, index, 1))
        elif stage == 2:
            sent.arrive((kind, index, 1))
            at = x_bit * (half // 2)
            cut(own, at, half // 2)[...] += own_x[...]
            each(2, sent.start)
        elif stage == 3:
            each(2, sent.arrive)
            value = cut(own, first - kept + me * size, size)[...].astype(F32)
            for step in range(members - 1):
                value = value + landing[step].astype(F32)
            value = value.astype(BF)
            cut(out, first + me * size, size)[...] = value
            each(3, sent.start)
            squared = value.astype(F32)
            square = jnp.sum((squared * squared).reshape(-1, 8, squared.shape[-1]), axis=0)
            folded = square[:, 0:128]
            for lane in range(1, square.shape[1] // 128):
                folded = folded + square[:, lane * 128 : lane * 128 + 128]
            square_sum[...] += folded
        elif stage == 4:
            each(3, sent.arrive)
            sent.start((kind, index, 4))
        elif stage == 5:
            if wide:
                each(3, sent.arrive)
            else:
                sent.arrive((kind, index, 4))
            sent.start((kind, index, 5))
        else:
            sent.arrive((kind, index, 5))
            loads.start(("out", index))

    for index in range(7):
        plan_piece(index)

    me = mp * 8 + chip
    rows_mine = pl.ds(pl.multiple_of(core_bit * 8, 8), 8)
    rows_other = pl.ds(pl.multiple_of(8 - core_bit * 8, 8), 8)
    sums_of = {"early": (early_core, early_part, early_all), "late": (late_core, late_part, late_all)}
    sent.plan("square core", lambda: square_sum, lambda: square_core, to_core)
    for name, (both, part, everyone) in sums_of.items():
        sent.plan(
            (name, "core"), lambda both=both: both.at[0, rows_other],
            lambda both=both: both.at[1, rows_other], to_core,
        )
        back = lambda part=part: part.at[rows_mine]
        sent.plan((name, "back"), back, back, to_core)
        for place, target in enumerate(chips):
            slot = lambda everyone=everyone: everyone.at[me]
            sent.plan((name, place), slot, slot, target)
    for place, target in enumerate(chips):
        sent.plan(("square", place), lambda: square_all.at[me], lambda: square_all.at[me], target)

    def everywhere(name, call):
        for place in range(len(chips)):
            call((name, place))

    def spread(name, stage):
        both, part, everyone = sums_of[name]
        if stage == 0:
            sent.arrive((name, "core"))
            everyone[me] = both[0, rows_mine] + both[1, rows_mine]
            everywhere(name, sent.start)
        elif stage == 1:
            everywhere(name, sent.arrive)
            part[rows_mine] = jnp.sum(everyone[...], axis=0)
            sent.start((name, "back"))
        else:
            sent.arrive((name, "back"))

    for row in range(8):
        value = jnp.sum(up_sum_ref[row] if row < 4 else two_ref[row - 4], axis=0, keepdims=True)
        early_core[0, row : row + 1, :] = value[:, 0:256]
        early_core[0, 8 + row : 9 + row, :] = value[:, 256:512]

    def run(events):
        for item in events:
            event(*item)

    square_sum[...] = jnp.zeros((8, 128), F32)
    bias_ref[0] = key_bias((SEQ, 128), mp, count_ref[2], True)
    for group in (1, 2):
        bias_ref[group] = key_bias((SEQ, 128), mp, count_ref[3 * mp + group - 1], False)
    sent.start(("early", "core"))
    run(SCHEDULE[0])

    def tiles(place, group, queries, sub):
        base = pl.multiple_of(group * SEQ, SEQ)
        keys_at, queries_at = pl.ds(base, SEQ), pl.ds(base, queries)
        own = slice(sub * HD, sub * HD + HD)
        s_ref[sub % 2, :, :queries] = score_tile(
            k_ref[place, keys_at, :], bias_ref[group], qt_ref[place, own, queries_at], sub
        )
        dp_ref[sub % 2, :, :queries] = mm_nn(
            v_ref[place, keys_at, :], widen_plain(dot_ref[place, own, queries_at], sub)
        )

    def heads(place, group, queries, out, out_base, following, between):
        block = block_at(place)
        base = pl.multiple_of(group * SEQ, SEQ)
        keys_at, queries_at = pl.ds(base, SEQ), pl.ds(base, queries)
        out_keys = pl.ds(out_base, SEQ)
        out_queries = pl.ds(out_base, queries)
        for sub in range(4):
            if sub < 3:
                tiles(place, group, queries, sub + 1)
            else:
                tiles(*following, queries, 0)
            own = slice(sub * HD, sub * HD + HD)
            q_rows, do_rows = qt_ref[place, own, queries_at], dot_ref[place, own, queries_at]
            delta = jnp.sum(
                do_rows.astype(F32) * ot_ref[place, own, queries_at].astype(F32), axis=0, keepdims=True
            )
            probs = jnp.exp2(
                s_ref[sub % 2, :, :queries] - lse_ref[group, block, sub : sub + 1, :queries]
            )
            draw = (probs * (dp_ref[sub % 2, :, :queries] - delta)).astype(BF)
            dq = mm_nn(kt_ref[place, own, keys_at], draw) * (HD ** (-0.5))
            out[own, out_queries] = dq.astype(BF)
            dk = mm_nt(q_rows, draw) * (1.0 / LOG2E)
            out[128 + sub * HD : 160 + sub * HD, out_keys] = dk.astype(BF)
            dv = mm_nt(do_rows, probs.astype(BF))
            out[256 + sub * HD : 288 + sub * HD, out_keys] = dv.astype(BF)
            if sub == 1:
                between()

    def weights_of(place):
        block = block_at(place)
        side, part = lax.div(block, 2), lax.rem(block, 2)
        return wt_ref[side, :, pl.ds(pl.multiple_of(part * 128, 128), 128), :].reshape(384, 512)

    for place in range(4):
        shared_ref[place, 0:128, HALF:SEQ] = jnp.zeros((128, HALF), BF)

    loaded(0)
    load_block(1)
    loads.wait("wt")

    def shared_step(place, carry):
        for turn in range(3):

            @pl.when(place == turn)
            def _():
                loaded(turn + 1)
                if turn < 2:
                    load_block(turn + 2)
                else:
                    loads.start("nt")
                    loads.start("x")
                    loads.start("dres")

        heads(place, 0, HALF, shared_ref.at[place], 0, (jnp.minimum(place + 1, 3), 0), lambda: None)
        for turn in range(4):

            @pl.when(place == turn)
            def _():
                run(SCHEDULE[1 + turn])
                if turn == 0:
                    spread("early", 0)
                elif turn == 3:
                    spread("early", 1)

        return carry

    tiles(0, 0, HALF, 0)
    lax.fori_loop(0, 4, shared_step, 0)
    tiles(0, 1, SEQ, 0)
    def rows_grad(grads, columns):
        total = mm_tn(grads[0, :, columns], weights_of(0))
        for place in range(1, 4):
            total += mm_tn(grads[place, :, columns], weights_of(place))
        return total

    far_send[...] = rows_grad(shared_ref, slice(HALF, SEQ)).astype(BF)
    spread("early", 2)
    sent.start("far", lambda: far_send, lambda: far_recv, to_peer)
    loads.wait("nt")

    def main_step(step, carry):
        place, group = lax.div(step, 2), 1 + lax.rem(step, 2)

        def pump(first):
            for turn in range(8):

                @pl.when(step == turn)
                def _():
                    run(SCHEDULE[first + 2 * turn])

        out_base = pl.multiple_of((group - 1) * SEQ, SEQ)
        after = jnp.minimum(step + 1, 7)
        following = (lax.div(after, 2), 1 + lax.rem(after, 2))
        heads(place, group, SEQ, grads_ref.at[place], out_base, following, lambda: pump(5))

        @pl.when(group == 2)
        def _():
            for part in range(3):
                rows = slice(part * 128, part * 128 + 128)
                total = mm_nt(nt_ref[:, 0:SEQ], shared_ref[place, rows, :])
                total += mm_nt(nt_ref[:, SEQ:], grads_ref[place, rows, :])
                g_ref[place, part] = total.astype(BF)
            ones = jnp.ones((8, 2 * SEQ), BF)
            bsum_ref[place] = mm_nt(ones[:, :SEQ], shared_ref[place]) + mm_nt(ones, grads_ref[place])

        pump(6)
        return carry

    lax.fori_loop(0, 8, main_step, 0)

    gain, shift = vec_ref[0:1, :], vec_ref[1:2, :]
    loads.wait("x")
    loads.wait("dres")
    run(SCHEDULE[21])

    def finish_rows(index, dn, sums):
        at = pl.ds(pl.multiple_of(index * HALF, HALF), HALF)
        place = pl.ds(row_block(index, mp), HALF)
        _, unit, inverse = layer_norm_rows(x_ref[place, :].astype(F32), gain, shift)
        grad_out[place, :] = dres_ref[at, :] + layer_norm_back(dn, unit, inverse, gain)
        folded = [jnp.sum(value.reshape(HALF // 8, 8, 512), axis=0) for value in (dn * unit, dn)]
        return sums[0] + folded[0], sums[1] + folded[1]

    def finish_step(index, sums):
        columns = pl.ds(pl.multiple_of(HALF * index - HALF, HALF), HALF)
        sums = finish_rows(index, rows_grad(grads_ref, columns), sums)
        for turn in range(1, 5):

            @pl.when(index == turn)
            def _():
                run(SCHEDULE[21 + turn])

        return sums

    zero = jnp.zeros((8, 512), F32)
    sums = lax.fori_loop(1, 5, finish_step, (zero, zero))
    sent.arrive("far")
    sums = finish_rows(0, rows_grad(shared_ref, slice(0, HALF)) + far_recv[...].astype(F32), sums)

    for place in range(4):
        lanes = slice(place * 128, place * 128 + 128)
        for row, value in enumerate((sums[0], sums[1])):
            late_core[0, 8 + 4 * row + place : 9 + 4 * row + place, :] = jnp.sum(
                value[:, lanes], axis=0, keepdims=True
            )
        for row, columns in enumerate((slice(0, 128), slice(256, 384))):
            late_core[0, 4 * row + place : 4 * row + place + 1, :] = jnp.where(
                mp == 0, bsum_ref[(place + 2) % 4, 0:1, columns], bsum_ref[place, 0:1, columns]
            )

    def square_stage(stage):
        if stage == 0:
            sent.start("square core")
        elif stage == 1:
            sent.arrive("square core")
            square_all[me] = square_sum[...] + square_core[...]
            everywhere("square", sent.start)
        else:
            everywhere("square", sent.arrive)
            for row in range(4):
                at = (0, 1, 6, 7)[row]
                for lane in range(4):
                    small_out[at : at + 1, lane * 128 : lane * 128 + 128] = late_part[
                        4 * row + lane : 4 * row + lane + 1, :
                    ]
            for row in range(8):
                at = 2 + row if row < 4 else 4 + row
                small_out[at : at + 1, 0:256] = early_part[row : row + 1, :]
                small_out[at : at + 1, 256:512] = early_part[8 + row : 9 + row, :]
            small_out[12:16, :] = jnp.zeros((4, 512), F32)
            small = small_out[...]
            total = jnp.sum(small * small) + jnp.sum(jnp.sum(square_all[...], axis=0))
            norm_out[...] = jnp.sqrt(jnp.full((8, 128), total, F32))

    sent.start(("late", "core"))
    for item in SCHEDULE[26]:
        if item[0] == "small":
            spread("late", item[1])
        elif item[0] == "square":
            square_stage(item[1])
        else:
            event(*item)
    sent.finish()
    for index in range(7):
        loads.wait(("out", index))


def backward(key_count, qt, kt, dot, ot, k, v, lse, nt, wt, owns, fores, gp, patches, dres, vec_params, two, ups):
    ext, rows = 3 * SEQ, patches.shape[0]
    vmem, hbm = pl.BlockSpec(memory_space=pltpu.VMEM), pl.BlockSpec(memory_space=pl.ANY)
    buffers = []
    for index in range(7):
        for size in (2, 2, 2, 2, 2, 4):
            buffers.append(pltpu.VMEM(piece_rows(index, size), BF))
        members = 7 if index in WIDE else 3
        buffers.append(pltpu.VMEM((members, *piece_rows(index, 16)), BF))
        buffers.append(pltpu.VMEM(piece_rows(index, 1), BF))
    return pl.pallas_call(
        backward_kernel,
        out_shape=[
            sds((rows, 512), F32), sds((1024, 512), BF), sds((512, 1024), BF), sds((256, 512), BF),
            sds((3, 512, 256), BF), sds((16, 512), F32), sds((8, 128), F32),
        ],
        in_specs=[pl.BlockSpec(memory_space=pltpu.SMEM)] + [hbm] * 6 + [vmem] + [hbm] * 7 + [vmem] * 3,
        out_specs=[vmem] + [hbm] * 4 + [vmem] * 2,
        scratch_shapes=[
            *[pltpu.VMEM((4, 128, ext), BF)] * 4, *[pltpu.VMEM((4, ext, 128), BF)] * 2,
            pltpu.VMEM((512, ext), BF), pltpu.VMEM((2, 3, 256, 512), BF), pltpu.VMEM((rows, 512), BF),
            pltpu.VMEM((rows, 512), F32), pltpu.VMEM((4, 384, SEQ), BF), pltpu.VMEM((4, 384, 2 * SEQ), BF),
            pltpu.VMEM((3, SEQ, 128), BF), pltpu.VMEM((2, SEQ, SEQ), F32),
            pltpu.VMEM((2, SEQ, SEQ), F32), pltpu.VMEM((4, 3, 512, 128), BF), pltpu.VMEM((4, 8, 384), F32),
            pltpu.VMEM((HALF, 512), BF), pltpu.VMEM((HALF, 512), BF), pltpu.VMEM((2, 16, 256), F32),
            pltpu.VMEM((16, 256), F32), pltpu.VMEM((16, 8, 256), F32), pltpu.VMEM((2, 16, 128), F32),
            pltpu.VMEM((16, 128), F32), pltpu.VMEM((16, 8, 128), F32), pltpu.VMEM((8, 128), F32),
            pltpu.VMEM((8, 128), F32), pltpu.VMEM((16, 8, 128), F32), *buffers,
            pltpu.SemaphoreType.DMA((137,)), pltpu.SemaphoreType.DMA((137,)), pltpu.SemaphoreType.DMA((48,)),
        ],
        compiler_params=pltpu.CompilerParams(
            collective_id=1, has_side_effects=True, vmem_limit_bytes=VMEM_LIMIT
        ),
        name="backward",
    )(key_count, qt, kt, dot, ot, k, v, lse, nt, wt, owns, fores, gp, patches, dres, vec_params, two, ups)


ADAM_STEPS = 4


def adam_step(weight, gradient, moment_one, moment_two, step_rate, decay_rate):
    first_new = BETA_FIRST * moment_one + (1.0 - BETA_FIRST) * gradient
    second_new = BETA_SECOND * moment_two + (1.0 - BETA_SECOND) * gradient * gradient
    root = jnp.sqrt(second_new * (1.0 / (1.0 - BETA_SECOND**ADAM_STEP))) + ADAM_EPS
    change = first_new * (step_rate / (1.0 - BETA_FIRST**ADAM_STEP)) / root
    return weight * (1.0 - step_rate * decay_rate) - change, first_new, second_new


def adam_kernel(norm_ref, small_ref, *refs):
    mp = lax.axis_index("mp")
    factor = jnp.minimum(1.0, CLIP_NORM / (norm_ref[0:1, 0:1] + 1e-06))
    vectors, refs = refs[:9], refs[9:]
    matrices, refs = refs[:16], refs[16:]
    results, vector_results, norm_out = refs[:12], refs[12:21], refs[21]
    for index in range(4):
        weight_ref, one_ref, two_ref, grad_ref = matrices[4 * index : 4 * index + 4]
        values = adam_step(
            weight_ref[...], grad_ref[...].astype(F32) * factor, one_ref[...], two_ref[...],
            MATRIX_RATE, DECAY_RATE,
        )
        for out, value in zip(results[3 * index : 3 * index + 3], values):
            out[...] = value

    @pl.when(pl.program_id(0) == 0)
    def _():
        norm_out[...] = norm_ref[0:1, 0:1]
        first = mp == 0
        qv = jnp.where(first, small_ref[0:2, 0:256], small_ref[0:2, 256:512])
        up = jnp.where(first, small_ref[2:4, :], small_ref[4:6, :])
        up = jnp.concatenate(
            [up[row : row + 1, lane * 128 : lane * 128 + 128] for row in range(2) for lane in range(4)], axis=0
        )
        for index, total in enumerate((qv, up, small_ref[6:12, :])):
            weight_ref, one_ref, two_ref = vectors[3 * index : 3 * index + 3]
            values = adam_step(
                weight_ref[...], total * factor, one_ref[...], two_ref[...], VECTOR_RATE, 0.0
            )
            for out, value in zip(vector_results[3 * index : 3 * index + 3], values):
                out[...] = value


def adam_all(norm, small, vectors, groups):
    steps = ADAM_STEPS
    in_specs, out_specs, out_shape = [full_spec((8, 128)), full_spec(small.shape)], [], []
    args = [norm, small]
    for vector in vectors:
        in_specs += [full_spec(array.shape) for array in vector]
        args += list(vector)
    for group in groups:
        rows, width = group[0].shape
        spec = pl.BlockSpec((rows // steps, width), lambda i: (i, 0))
        in_specs += [spec] * 4
        out_specs += [spec] * 3
        out_shape += [sds((rows, width), F32)] * 3
        args += list(group)
    for vector in vectors:
        out_specs += [full_spec(array.shape) for array in vector]
        out_shape += [sds(array.shape, F32) for array in vector]
    return pl.pallas_call(
        adam_kernel,
        grid=(steps,),
        out_shape=out_shape + [sds((1, 1), F32)],
        in_specs=in_specs,
        out_specs=out_specs + [full_spec((1, 1))],
        compiler_params=pltpu.CompilerParams(vmem_limit_bytes=VMEM_LIMIT),
        name="adam_all",
    )(*args)


IN_SPECS = (
            P(("dp", "mp"), None),
            P(("dp", "mp"), None),
            P("dp"),
            P(None, None, "mp"),
            P("mp", None),
            P(None, "mp"),
            P("mp", None),
            P(None, "mp"),
            P("mp"),
            P(),
            P(None, None, "mp"),
            P(None, None, "mp"),
            P("mp", None),
            P("mp", None),
            P(None, "mp"),
            P(None, "mp"),
            P("mp", None),
            P("mp", None),
            P(None, "mp"),
            P(None, "mp"),
            P("mp"),
            P("mp"),
            P(),
            P(),
        )
OUT_SPECS = (
            P(("dp", "mp"), None),
            P(("dp", "mp"), None),
            P(),
            P(None, None, "mp"),
            P(None, None, "mp"),
            P(None, None, "mp"),
            P("mp", None),
            P("mp", None),
            P("mp", None),
            P(None, "mp"),
            P(None, "mp"),
            P(None, "mp"),
            P("mp", None),
            P("mp", None),
            P("mp", None),
            P(None, "mp"),
            P(None, "mp"),
            P(None, "mp"),
            P("mp"),
            P("mp"),
            P("mp"),
            P(),
            P(),
            P(),
        )


def paired(
    patches, cotangent, key_count, w_qkv, w_proj, w_up, w_down, qv_bias, up_bias, vec_params,
    first_qkv, second_qkv, first_proj, second_proj, first_up, second_up, first_down, second_down,
    first_qv_bias, second_qv_bias, first_up_bias, second_up_bias, first_vec, second_vec,
):
    wt, wp, wu, wd, small_all, nt, qt, kt, k, v, ot, lse = forward(
        key_count, w_qkv, w_proj, w_up, w_down, qv_bias, up_bias.reshape(1, 1024), patches, vec_params
    )
    activations, dres, dot, owns, fores, g_proj, vsum_two, up_sums = mlp(
        patches, cotangent, ot, wp, wu, wd, vec_params, small_all
    )
    input_grad, down, up, proj, qkv, small_total, norm = backward(
        key_count, qt, kt, dot, ot, k, v, lse, nt, wt, owns, fores, g_proj, patches, dres, vec_params,
        vsum_two, up_sums,
    )
    qkv = qkv.reshape(1536, 256)
    flat = lambda array: array.reshape(-1, array.shape[-1])
    groups = [
        (flat(w_qkv), flat(first_qkv), flat(second_qkv), qkv),
        (w_proj, first_proj, second_proj, proj),
        (w_up, first_up, second_up, up),
        (w_down, first_down, second_down, down),
    ]
    square = lambda array: array.reshape(8, 128)
    vectors = [
        (qv_bias, first_qv_bias, second_qv_bias),
        (square(up_bias), square(first_up_bias), square(second_up_bias)),
        (vec_params, first_vec, second_vec),
    ]
    outs = adam_all(norm, small_total, vectors, groups)
    return (
        activations, input_grad, outs[21].reshape(()), *[array.reshape(w_qkv.shape) for array in outs[0:3]],
        *outs[3:12], *outs[12:15], *[array.reshape(up_bias.shape) for array in outs[15:18]], *outs[18:21],
    )


def fits_pairs(mesh, args):
    if dict(mesh.shape) != {"dp": 16, "mp": 2}:
        return False
    return args[0].shape == (40960, 512) and args[2].shape == (80,)


def solution(mesh):
    def run(*args):
        body = paired if fits_pairs(mesh, args) else local
        return jax.shard_map(body, mesh=mesh, in_specs=IN_SPECS, out_specs=OUT_SPECS, check_vma=False)(*args)

    return run
```

```python
import jax
import jax.numpy as jnp
from jax import lax
from jax.experimental import pallas as pl
from jax.experimental.pallas import tpu as pltpu
from jax.sharding import PartitionSpec as P

HD = 32
ADAM_STEP = 10


NORM_EPS = 1e-06
BETA_FIRST = 0.9
BETA_SECOND = 0.95
ADAM_EPS = 1e-08
DECAY_RATE = 0.05
MATRIX_RATE = 0.1
VECTOR_RATE = 0.8
CLIP_NORM = 1.0
MASK_FILL = -1e30
LOG2E = 1.4426950408889634
BF = jnp.bfloat16
F32 = jnp.float32
MESH = pl.DeviceIdType.MESH
SEQ = 512
HALF = 256
VMEM_LIMIT = 58 * 1024 * 1024


def mm_nn(left, right):
    return lax.dot_general(left, right, (((1,), (0,)), ((), ())), preferred_element_type=F32)


def mm_nt(left, right):
    return lax.dot_general(left, right, (((1,), (1,)), ((), ())), preferred_element_type=F32)


def mm_tn(left, right):
    return lax.dot_general(left, right, (((0,), (0,)), ((), ())), preferred_element_type=F32)


def partners(dp):
    core = dp + 1 - 2 * lax.rem(dp, 2)
    x_side = dp + 2 - 4 * lax.rem(lax.div(dp, 2), 2)
    z_near = dp + 4 - 8 * lax.rem(lax.div(dp, 4), 2)
    z_far = dp + 8 - 16 * lax.rem(lax.div(dp, 8), 2)
    return core, x_side, z_near, z_far


def greet(targets):
    barrier = pltpu.get_barrier_semaphore()
    for target in targets:
        pl.semaphore_signal(barrier, inc=1, device_id=target, device_id_type=MESH)
    pl.semaphore_wait(barrier, len(targets))


def full_spec(shape):
    return pl.BlockSpec(shape, lambda *_: (0,) * len(shape))


def sds(shape, dtype):
    return jax.ShapeDtypeStruct(shape, dtype)


def row_block(index, mp):
    return pl.multiple_of(lax.rem(index + 4 * (1 - mp), 5) * HALF, HALF)


def ext_cols(index):
    return pl.multiple_of(jnp.where(index == 0, 0, HALF + HALF * index), HALF)


def norm_forward(values, norm_gain, norm_shift):
    row_mean = jnp.mean(values, axis=-1, keepdims=True)
    centred = values - row_mean
    inverse = lax.rsqrt(jnp.mean(centred * centred, axis=-1, keepdims=True) + NORM_EPS)
    normed = centred * inverse
    return (normed * norm_gain + norm_shift, normed, inverse)


def norm_backward(grad_rows, normed, inverse, norm_gain):
    scaled = grad_rows * norm_gain
    centre_term = jnp.mean(scaled, axis=-1, keepdims=True)
    slope_term = jnp.mean(scaled * normed, axis=-1, keepdims=True)
    return inverse * (scaled - centre_term - normed * slope_term)


def exact_gelu(values):
    return jax.nn.gelu(values, approximate=False)


def key_mask(key_count, length):
    position = lax.broadcasted_iota(jnp.int32, (1, 1, 1, length), 3)
    return position < key_count[:, None, None, None]


def masked_scores(queries, key_rows, key_count):
    raw_scores = jnp.einsum(
        "sqhe,skhe->shqk", queries, key_rows, preferred_element_type=jnp.float32
    )
    scaled = raw_scores * queries.shape[-1] ** (-0.5)
    return jnp.where(key_mask(key_count, key_rows.shape[1]), scaled, MASK_FILL)


def attend_backward(queries, key_rows, value_rows, key_count, log_total, attended_grad):
    scores = masked_scores(queries, key_rows, key_count)
    probs = jnp.exp(scores - log_total)
    probs_low = probs.astype(jnp.bfloat16)
    probs_grad = jnp.einsum(
        "sqhe,skhe->shqk", attended_grad, value_rows, preferred_element_type=jnp.float32
    )
    score_grad = probs * (probs_grad - jnp.sum(probs_grad * probs, axis=-1, keepdims=True))
    visible = key_mask(key_count, key_rows.shape[1])
    raw_grad = jnp.where(visible, score_grad * queries.shape[-1] ** (-0.5), 0.0).astype(
        jnp.bfloat16
    )
    query_grad = jnp.einsum(
        "shqk,skhe->sqhe", raw_grad, key_rows, preferred_element_type=jnp.float32
    )
    key_grad = jnp.einsum("shqk,sqhe->skhe", raw_grad, queries, preferred_element_type=jnp.float32)
    value_grad = jnp.einsum(
        "shqk,sqhe->skhe", probs_low, attended_grad, preferred_element_type=jnp.float32
    )
    return jnp.stack([query_grad, key_grad, value_grad])


def own_slice(values, own_start, own_rows):
    return lax.dynamic_slice_in_dim(values, own_start, own_rows, 0)


def contract_rows(left, right):
    return lax.dot_general(
        left, right, (((0,), (0,)), ((), ())), preferred_element_type=jnp.float32
    )


def contract_cols(left, right):
    return lax.dot_general(
        left, right, (((1,), (1,)), ((), ())), preferred_element_type=jnp.float32
    )


def adam_update(weight, gradient, moment_one, moment_two, step_rate, decay_rate):
    first_new = BETA_FIRST * moment_one + (1.0 - BETA_FIRST) * gradient
    second_new = BETA_SECOND * moment_two + (1.0 - BETA_SECOND) * gradient * gradient
    first_hat = first_new / (1.0 - BETA_FIRST**ADAM_STEP)
    second_hat = second_new / (1.0 - BETA_SECOND**ADAM_STEP)
    weight_new = weight - step_rate * (
        first_hat / (jnp.sqrt(second_hat) + ADAM_EPS) + decay_rate * weight
    )
    return (weight_new, first_new, second_new)


def local(
    patches,
    cotangent,
    key_count,
    w_qkv,
    w_proj,
    w_up,
    w_down,
    qv_bias,
    up_bias,
    vec_params,
    first_qkv,
    second_qkv,
    first_proj,
    second_proj,
    first_up,
    second_up,
    first_down,
    second_down,
    first_qv_bias,
    second_qv_bias,
    first_up_bias,
    second_up_bias,
    first_vec,
    second_vec,
):
    own_rows = patches.shape[0]
    seq_count = key_count.shape[0]
    own_start = lax.axis_index("mp") * own_rows
    local_width = w_proj.shape[0]
    local_heads = local_width // HD
    own_grad = cotangent.astype(jnp.float32)
    qkv_low = w_qkv.astype(jnp.bfloat16)
    proj_low = w_proj.astype(jnp.bfloat16)
    up_low = w_up.astype(jnp.bfloat16)
    down_low = w_down.astype(jnp.bfloat16)
    gain_one, shift_one = (vec_params[0], vec_params[1])
    gain_two, shift_two = (vec_params[2], vec_params[3])
    proj_shift, down_shift = (vec_params[4], vec_params[5])
    qkv_shift = jnp.stack([qv_bias[0], jnp.zeros_like(qv_bias[0]), qv_bias[1]])[:, None, :]
    gathered, grad_all = (
        lax.all_gather(patches, "mp", axis=0, tiled=True),
        lax.all_gather(cotangent, "mp", axis=0, tiled=True),
    )
    whole_rows = gathered.astype(jnp.float32)
    normed_all, unit_one, inverse_one = norm_forward(whole_rows, gain_one, shift_one)
    norm_one = normed_all.astype(jnp.bfloat16)
    projected = (
        jnp.einsum("td,cde->cte", norm_one, qkv_low, preferred_element_type=jnp.float32) + qkv_shift
    )
    shaped = projected.astype(jnp.bfloat16).reshape(3, seq_count, -1, local_heads, HD)
    queries, key_rows, value_rows = (shaped[0], shaped[1], shaped[2])
    scores = masked_scores(queries, key_rows, key_count)
    top_score = jnp.max(scores, axis=-1, keepdims=True)
    log_total = top_score + jnp.log(jnp.sum(jnp.exp(scores - top_score), axis=-1, keepdims=True))
    probs_low = jnp.exp(scores - log_total).astype(jnp.bfloat16)
    attended = jnp.einsum(
        "shqk,skhe->sqhe", probs_low, value_rows, preferred_element_type=jnp.float32
    )
    attended_low = attended.astype(jnp.bfloat16).reshape(-1, local_width)
    proj_part = jnp.dot(attended_low, proj_low, preferred_element_type=jnp.float32)
    resid_all = whole_rows + lax.psum(proj_part, "mp") + proj_shift
    mid_all, unit_two, inverse_two = norm_forward(resid_all, gain_two, shift_two)
    norm_two = mid_all.astype(jnp.bfloat16)
    up_pre = jnp.dot(norm_two, up_low, preferred_element_type=jnp.float32) + up_bias
    hidden_full, gelu_pull = jax.vjp(exact_gelu, up_pre)
    hidden_low = hidden_full.astype(jnp.bfloat16)
    down_part = jnp.dot(hidden_low, down_low, preferred_element_type=jnp.float32)
    out_all = (
        resid_all + lax.psum(down_part.astype(jnp.bfloat16), "mp").astype(jnp.float32) + down_shift
    )
    block_out = own_slice(out_all, own_start, own_rows)
    activations = block_out.astype(jnp.bfloat16)
    down_grad = contract_rows(hidden_low, grad_all)
    hidden_grad = contract_cols(grad_all, down_low)
    up_grad_rows = gelu_pull(hidden_grad)[0].astype(jnp.bfloat16)
    up_grad = contract_rows(norm_two, up_grad_rows)
    up_bias_grad = jnp.sum(up_grad_rows.astype(jnp.float32), axis=0)
    mid_part = contract_cols(up_grad_rows, up_low)
    mid_all_grad = lax.psum(mid_part.astype(jnp.bfloat16), "mp").astype(jnp.float32)
    resid_all_grad = grad_all.astype(jnp.float32) + norm_backward(
        mid_all_grad, unit_two, inverse_two, gain_two
    )
    branch_low = resid_all_grad.astype(jnp.bfloat16)
    own_branch = own_slice(branch_low, own_start, own_rows)
    mid_grad = own_slice(mid_all_grad, own_start, own_rows)
    mid_unit = own_slice(unit_two, own_start, own_rows)
    proj_grad = contract_rows(attended_low, branch_low)
    attended_grad = (
        contract_cols(branch_low, proj_low)
        .astype(jnp.bfloat16)
        .reshape(seq_count, -1, local_heads, HD)
    )
    qkv_grads = attend_backward(queries, key_rows, value_rows, key_count, log_total, attended_grad)
    qkv_grad_rows = qkv_grads.reshape(3, -1, local_width).astype(jnp.bfloat16)
    qkv_grad = jnp.einsum(
        "td,cte->cde", norm_one, qkv_grad_rows, preferred_element_type=jnp.float32
    )
    qkv_grad_sums = jnp.sum(qkv_grad_rows.astype(jnp.float32), axis=1)
    qv_bias_grad = jnp.stack([qkv_grad_sums[0], qkv_grad_sums[2]])
    first_part = jnp.einsum(
        "cte,cde->td", qkv_grad_rows, qkv_low, preferred_element_type=jnp.float32
    )
    first_all = lax.psum(first_part.astype(jnp.bfloat16), "mp").astype(jnp.float32)
    input_all = resid_all_grad + norm_backward(first_all, unit_one, inverse_one, gain_one)
    input_grad = own_slice(input_all, own_start, own_rows)
    own_first_grad = own_slice(first_all, own_start, own_rows)
    own_unit_one = own_slice(unit_one, own_start, own_rows)
    vec_grad = jnp.stack(
        [
            jnp.sum(own_first_grad * own_unit_one, axis=0),
            jnp.sum(own_first_grad, axis=0),
            jnp.sum(mid_grad * mid_unit, axis=0),
            jnp.sum(mid_grad, axis=0),
            jnp.sum(own_branch.astype(jnp.float32), axis=0),
            jnp.sum(own_grad, axis=0),
        ]
    )
    summed = (
        lax.psum(qkv_grad.astype(jnp.bfloat16), "dp").astype(jnp.float32),
        lax.psum(proj_grad.astype(jnp.bfloat16), "dp").astype(jnp.float32),
        lax.psum(up_grad.astype(jnp.bfloat16), "dp").astype(jnp.float32),
        lax.psum(down_grad.astype(jnp.bfloat16), "dp").astype(jnp.float32),
        lax.psum(qv_bias_grad.astype(jnp.bfloat16), "dp").astype(jnp.float32),
        lax.psum(up_bias_grad.astype(jnp.bfloat16), "dp").astype(jnp.float32),
        lax.psum(vec_grad.astype(jnp.bfloat16), "dp").astype(jnp.float32),
    )
    split_square = jnp.float32(0.0)
    for gradient in summed[:6]:
        split_square = split_square + jnp.sum(gradient * gradient)
    vec_total, split_total = lax.psum((summed[6], split_square), "mp")
    grad_norm = jnp.sqrt(split_total + jnp.sum(vec_total * vec_total))
    factor = jnp.minimum(1.0, CLIP_NORM / (grad_norm + 1e-06))
    qkv_new, qkv_first, qkv_second = adam_update(
        w_qkv, summed[0] * factor, first_qkv, second_qkv, MATRIX_RATE, DECAY_RATE
    )
    proj_new, proj_first, proj_second = adam_update(
        w_proj, summed[1] * factor, first_proj, second_proj, MATRIX_RATE, DECAY_RATE
    )
    up_new, up_first, up_second = adam_update(
        w_up, summed[2] * factor, first_up, second_up, MATRIX_RATE, DECAY_RATE
    )
    down_new, down_first, down_second = adam_update(
        w_down, summed[3] * factor, first_down, second_down, MATRIX_RATE, DECAY_RATE
    )
    qvb_new, qvb_first, qvb_second = adam_update(
        qv_bias, summed[4] * factor, first_qv_bias, second_qv_bias, VECTOR_RATE, 0.0
    )
    upb_new, upb_first, upb_second = adam_update(
        up_bias, summed[5] * factor, first_up_bias, second_up_bias, VECTOR_RATE, 0.0
    )
    vec_new, vec_first, vec_second = adam_update(
        vec_params, vec_total * factor, first_vec, second_vec, VECTOR_RATE, 0.0
    )
    return (
        activations,
        input_grad,
        grad_norm,
        qkv_new,
        qkv_first,
        qkv_second,
        proj_new,
        proj_first,
        proj_second,
        up_new,
        up_first,
        up_second,
        down_new,
        down_first,
        down_second,
        qvb_new,
        qvb_first,
        qvb_second,
        upb_new,
        upb_first,
        upb_second,
        vec_new,
        vec_first,
        vec_second,
    )


class Transfers:
    def __init__(self, send_sem, recv_sem):
        self.sems = (send_sem, recv_sem)
        self.all = {}

    def make(self, key):
        index, src, dst, target = self.all[key]
        return pltpu.make_async_remote_copy(
            src_ref=src(), dst_ref=dst(), send_sem=self.sems[0].at[index], recv_sem=self.sems[1].at[index],
            device_id=target, device_id_type=MESH,
        )

    def plan(self, key, src, dst, target):
        self.all[key] = (len(self.all), src, dst, target)

    def start(self, key, *views):
        if views:
            self.plan(key, *views)
        self.make(key).start()

    def arrive(self, key):
        self.make(key).wait_recv()

    def finish(self):
        for key in self.all:
            self.make(key).wait_send()


class Loads:
    def __init__(self, sem):
        self.sem = sem
        self.all = {}

    def make(self, key):
        index, src, dst = self.all[key]
        return pltpu.make_async_copy(src(), dst(), self.sem.at[index])

    def plan(self, key, src, dst):
        self.all[key] = (len(self.all), src, dst)

    def start(self, key, *views):
        if views:
            self.plan(key, *views)
        self.make(key).start()

    def wait(self, key):
        self.make(key).wait()


def layer_norm_rows(rows, gain, shift):
    centred = rows - jnp.mean(rows, axis=-1, keepdims=True)
    inverse = lax.rsqrt(jnp.mean(centred * centred, axis=-1, keepdims=True) + NORM_EPS)
    unit = centred * inverse
    return unit * gain + shift, unit, inverse


def layer_norm_back(grad, unit, inverse, gain):
    scaled = grad * gain
    centre = jnp.mean(scaled, axis=-1, keepdims=True)
    slope = jnp.mean(scaled * unit, axis=-1, keepdims=True)
    return inverse * (scaled - centre - unit * slope)


def head_rows(block, sub):
    return pl.ds(pl.multiple_of(block * 128 + sub * HD, HD), HD)


def head_cols(block):
    return pl.ds(pl.multiple_of(block * 128, 128), 128)


def key_bias(shape, mp, count, shared):
    slot = lax.broadcasted_iota(jnp.int32, shape, 0)
    if shared:
        slot = lax.rem(slot + HALF * mp, SEQ)
    return jnp.where(slot < count, 0.0, MASK_FILL).astype(BF)


def widen(rows, sub):
    zeros = jnp.zeros_like(rows)
    row = lax.broadcasted_iota(jnp.int32, rows.shape, 0)
    ones = jnp.where(row == 0, 1.0, 0.0).astype(BF)
    parts = [zeros] * 4
    parts[sub] = rows
    parts[(sub + 1) % 4] = ones
    return jnp.concatenate(parts, axis=0)


def widen_plain(rows, sub):
    parts = [jnp.zeros_like(rows)] * 4
    parts[sub] = rows
    return jnp.concatenate(parts, axis=0)


def score_tile(key_block, bias, query_rows, sub):
    lane = lax.broadcasted_iota(jnp.int32, key_block.shape, 1)
    keys = jnp.where(lane // HD == (sub + 1) % 4, bias, key_block)
    return mm_nn(keys, widen(query_rows, sub))


def forward_kernel(
    count_ref, qkv_ref, proj_in, up_in, down_in, qv_ref, up_bias_ref, x_in, vec_ref,
    wt_out, wp_out, wu_out, wd_out, sm_out,
    nt_out, qt_out, kt_out, k_out, v_out, ot_out, lse_out,
    wt_ref, own_proj, own_up, own_down, sm_ref, other_ref,
    norm_ref, nt_ref, qt_ref, kt_ref, vt_ref, k_ref, v_ref, ot_ref, lse_ref, bias_ref, s_ref,
    proj_ref, up_ref, down_ref, x_ref, send_sem, recv_sem, local_sem, input_sem,
):
    dp, mp = lax.axis_index("dp"), lax.axis_index("mp")
    inputs = Loads(input_sem)
    for name, src, dst in (
        ("x", x_in, x_ref), ("proj", proj_in, proj_ref), ("up", up_in, up_ref), ("down", down_in, down_ref)
    ):
        inputs.start(name, lambda src=src: src, lambda dst=dst: dst)
    peer = 1 - mp
    core, x_side, _, _ = partners(dp)
    quarter = lax.rem(dp, 4)
    x_quarter = lax.rem(quarter + 2, 4)
    gain, shift = vec_ref[0:1, :], vec_ref[1:2, :]
    greet([{"mp": peer}, {"dp": core}, {"dp": x_side}])

    remote, local = [], []

    class Transfer:
        def __init__(self, src, dst, target):
            self.index = len(remote)
            self.views = (src, dst, target)
            remote.append(self)
            self.make().start()

        def make(self):
            src, dst, target = self.views
            return pltpu.make_async_remote_copy(
                src_ref=src(), dst_ref=dst(), send_sem=send_sem.at[self.index],
                recv_sem=recv_sem.at[self.index], device_id=target, device_id_type=MESH,
            )

        def wait_recv(self):
            self.make().wait_recv()

        def wait_send(self):
            self.make().wait_send()

    def send(src, dst, target):
        return Transfer(src, dst, target)

    def keep(src, dst):
        copy = pltpu.make_async_copy(src, dst, local_sem.at[len(local)])
        copy.start()
        local.append(copy)

    def span(start, size):
        return pl.ds(pl.multiple_of(start, 16), size)

    pieces = []
    for part in range(3):
        pieces.append((wt_ref.at[mp, part], lambda side, part=part: wt_ref.at[side, part], 64, 0))
    pieces.append((own_proj, lambda side: wp_out.at[side], 64, 0))
    for shard, out, rows in ((own_up, wu_out, 128), (own_down, wd_out, 256)):
        for part in range(2):
            pieces.append((shard, lambda side, out=out: out.at[side], rows // 2, part * rows * 2))

    def place(ref, index, part):
        rows, base = pieces[index][2], pieces[index][3]
        return ref.at[span(base + part * rows, rows), :]

    first, second, third = {}, {}, {}

    def to_peer(index):
        first[index] = send(
            lambda: place(pieces[index][0], index, quarter),
            lambda: place(pieces[index][1](mp), index, quarter), {"mp": peer},
        )

    def to_sides(index):
        first[index].wait_recv()
        at = lambda: place(pieces[index][1](peer), index, quarter)
        second[index] = send(at, at, {"dp": x_side})
        third[index] = [send(at, at, {"dp": core})]

    def to_core(index):
        second[index].wait_recv()
        at = lambda: place(pieces[index][1](peer), index, x_quarter)
        third[index].append(send(at, at, {"dp": core}))

    def arrive(index):
        for copy in third[index]:
            copy.wait_recv()

    own_half = pl.multiple_of((1 - mp) * 4 * HALF, HALF)
    for part in range(3):
        wt_ref[mp, part] = qkv_ref[part].T.astype(BF)
        to_peer(part)
    sm_ref[mp] = jnp.zeros((8, 1024), F32)
    sm_ref[mp, 0:1, :] = up_bias_ref[...]
    sm_ref[mp, 1:3, 0:256] = qv_ref[...]
    small_copy = send(lambda: sm_ref.at[mp], lambda: sm_ref.at[mp], {"mp": peer})
    inputs.wait("proj")
    own_proj[...] = proj_ref[...].astype(BF)
    inputs.wait("up")
    own_up[...] = up_ref[...].astype(BF)
    inputs.wait("down")
    own_down[...] = down_ref[...].astype(BF)
    inputs.wait("x")
    keep(wt_ref.at[mp], wt_out.at[mp])
    keep(own_proj, wp_out.at[mp])
    keep(own_up, wu_out.at[mp])
    keep(own_down, wd_out.at[mp])

    def as_column(row):
        return jnp.broadcast_to(row, (8, row.shape[1])).T[:, 0:1]

    def normalise(group, part, rows):
        base = group * SEQ + part * HALF
        norm = layer_norm_rows(rows.astype(F32), gain, shift)[0].astype(BF)
        norm_ref[span(base, HALF), :] = norm
        nt_ref[:, pl.ds(pl.multiple_of(base, HALF), HALF)] = norm.T

    def project(side, group):
        base = pl.multiple_of(group * SEQ, SEQ)
        at = pl.ds(base, SEQ)
        own = pl.ds(pl.multiple_of(side * 256, 256), 256)
        norm = norm_ref[at, :]
        q_bias, v_bias = sm_ref[side, 1:2, 0:256], sm_ref[side, 2:3, 0:256]
        scale = LOG2E * HD ** (-0.5)
        qt_ref[own, at] = ((mm_nt(wt_ref[side, 0], norm) + as_column(q_bias)) * scale).astype(BF)
        kt_ref[own, at] = mm_nt(wt_ref[side, 1], norm).astype(BF)
        vt_ref[own, :] = (mm_nt(wt_ref[side, 2], norm) + as_column(v_bias)).astype(BF)
        k_ref[at, own] = mm_nt(norm, wt_ref[side, 1]).astype(BF)
        v_ref[at, own] = (mm_nt(norm, wt_ref[side, 2]) + v_bias).astype(BF)

    def attend(side, group, queries, between):
        base = pl.multiple_of(group * SEQ, SEQ)
        keys_at, queries_at = pl.ds(base, SEQ), pl.ds(base, queries)
        bias = bias_ref[group]

        def scores(block, sub):
            return score_tile(
                k_ref[keys_at, head_cols(block)], bias, qt_ref[head_rows(block, sub), queries_at], sub
            )

        s_ref[0, :, :queries] = scores(2 * side, 0)

        def body(step, carry):
            block = 2 * side + step
            for sub in range(4):
                following = (block, sub + 1) if sub < 3 else (2 * side + 1, 0)
                s_ref[(sub + 1) % 2, :, :queries] = scores(*following)
                tile = s_ref[sub % 2, :, :queries]
                top = jnp.max(tile, axis=0, keepdims=True)
                weights = jnp.exp2(tile - top)
                rows = head_rows(block, sub)
                values = jnp.concatenate([vt_ref[rows, :], jnp.ones((16, SEQ), BF)], axis=0)
                mixed = mm_nn(values, weights.astype(BF))
                total = mixed[HD : HD + 1]
                ot_ref[rows, queries_at] = (mixed[:HD] * (1.0 / total)).astype(BF)
                lse_ref[group, block, sub : sub + 1, :queries] = top + jnp.log2(total)

            @pl.when(step == 0)
            def _():
                between()

            return carry

        lax.fori_loop(0, 2, body, 0)

    def nothing():
        pass

    def unit(side, group, queries, early=nothing, between=nothing):
        project(side, group)
        early()
        attend(side, group, queries, between)
        at = pl.ds(pl.multiple_of(group * SEQ, SEQ), SEQ)
        own = pl.ds(pl.multiple_of(side * 256, 256), 256)
        keep(qt_ref.at[own, at], qt_out.at[own, at])
        keep(kt_ref.at[own, at], kt_out.at[own, at])
        keep(ot_ref.at[own, at], ot_out.at[own, at])
        keep(k_ref.at[at, own], k_out.at[at, own])
        keep(v_ref.at[at, own], v_out.at[at, own])

    def in_turn(*calls):
        def run():
            for call, *indices in calls:
                for index in indices:
                    call(index)

        return run

    for group in (1, 2):
        bias_ref[group] = key_bias((SEQ, 128), mp, count_ref[3 * mp + group - 1], False)
        for part in range(2):
            normalise(group, part, x_ref[pl.ds(row_block(2 * group - 1 + part, mp), HALF), :])
        if group == 1:
            to_peer(3)
            to_peer(4)
    bias_ref[0] = key_bias((SEQ, 128), mp, count_ref[2], True)
    normalise(0, 0, x_ref[pl.ds(row_block(0, mp), HALF), :])
    for index in range(3):
        to_sides(index)
    to_peer(5)
    unit(mp, 1, SEQ)
    in_turn((to_sides, 3, 4), (to_peer, 6))()
    unit(mp, 2, SEQ, between=in_turn((to_core, 0, 1, 2), (to_sides, 5), (to_peer, 7)))
    small_copy.wait_recv()
    keep(sm_ref, sm_out)
    for index in range(3):
        arrive(index)
    keep(wt_ref.at[peer], wt_out.at[peer])
    rows_copy = send(lambda: x_ref.at[pl.ds(own_half, HALF), :], lambda: other_ref, {"mp": peer})
    unit(peer, 1, SEQ, early=in_turn((to_sides, 6)), between=in_turn((to_core, 3, 4)))
    in_turn((to_sides, 7))()
    unit(peer, 2, SEQ, early=in_turn((to_core, 5)), between=in_turn((to_core, 6)))
    rows_copy.wait_recv()
    normalise(0, 1, other_ref[...])
    keep(nt_ref, nt_out)
    unit(mp, 0, HALF, between=in_turn((to_core, 7)))
    unit(peer, 0, HALF)
    keep(lse_ref, lse_out)
    for index in range(3, 8):
        arrive(index)
    for copy in remote:
        copy.wait_send()
    for copy in local:
        copy.wait()


def forward(key_count, w_qkv, w_proj, w_up, w_down, qv_bias, up_bias, patches, vec_params):
    ext = 3 * SEQ
    vmem, hbm = pl.BlockSpec(memory_space=pltpu.VMEM), pl.BlockSpec(memory_space=pl.ANY)
    return pl.pallas_call(
        forward_kernel,
        out_shape=[
            sds((2, 3, 256, 512), BF), sds((2, 256, 512), BF), sds((2, 512, 1024), BF),
            sds((2, 1024, 512), BF), sds((2, 8, 1024), F32),
            sds((512, ext), BF), sds((512, ext), BF), sds((512, ext), BF), sds((ext, 512), BF),
            sds((ext, 512), BF), sds((512, ext), BF), sds((3, 4, 8, SEQ), F32),
        ],
        in_specs=[pl.BlockSpec(memory_space=pltpu.SMEM), vmem, hbm, hbm, hbm, vmem, vmem, hbm, vmem],
        out_specs=[hbm] * 12,
        scratch_shapes=[
            pltpu.VMEM((2, 3, 256, 512), BF), pltpu.VMEM((256, 512), BF), pltpu.VMEM((512, 1024), BF),
            pltpu.VMEM((1024, 512), BF), pltpu.VMEM((2, 8, 1024), F32), pltpu.VMEM((HALF, 512), BF),
            pltpu.VMEM((ext, 512), BF), pltpu.VMEM((512, ext), BF), pltpu.VMEM((512, ext), BF),
            pltpu.VMEM((512, ext), BF), pltpu.VMEM((512, SEQ), BF), pltpu.VMEM((ext, 512), BF),
            pltpu.VMEM((ext, 512), BF), pltpu.VMEM((512, ext), BF), pltpu.VMEM((3, 4, 8, SEQ), F32),
            pltpu.VMEM((3, SEQ, 128), BF), pltpu.VMEM((2, SEQ, SEQ), F32),
            pltpu.VMEM((256, 512), F32), pltpu.VMEM((512, 1024), F32), pltpu.VMEM((1024, 512), F32),
            pltpu.VMEM(patches.shape, BF), pltpu.SemaphoreType.DMA((34,)), pltpu.SemaphoreType.DMA((34,)),
            pltpu.SemaphoreType.DMA((40,)), pltpu.SemaphoreType.DMA((4,)),
        ],
        compiler_params=pltpu.CompilerParams(
            collective_id=0, has_side_effects=True, vmem_limit_bytes=VMEM_LIMIT
        ),
        name="forward",
    )(key_count, w_qkv, w_proj, w_up, w_down, qv_bias, up_bias, patches, vec_params)


def mlp_kernel(
    x_ref, dy_ref, ot_ref, wp_ref, wu_in, wd_in, vec_ref, small_ref,
    act_ref, dres_ref, dot_ref, own_out, fore_out, gp_ref, vsum_ref, bsum_ref,
    res_ref, n2_ref, out_ref, dn_ref, hid_ref, dup_ref, dyc_ref, br_ref,
    g_ref, fore_ref, fore_core, own_core, own_peer, wu_ref, wd_ref, send_sem, recv_sem, input_sem,
):
    step = pl.program_id(0)
    dp, mp = lax.axis_index("dp"), lax.axis_index("mp")
    peer, core, core_bit = 1 - mp, partners(dp)[0], lax.rem(dp, 2)
    side, part = jnp.where(step < 2, peer, mp), lax.rem(step, 2)
    sent = Transfers(send_sem, recv_sem)
    kept = pl.ds(pl.multiple_of(core_bit * HALF, HALF), HALF)
    away = pl.ds(pl.multiple_of(HALF - core_bit * HALF, HALF), HALF)
    for turn in range(2):
        sent.plan(
            ("F", turn), lambda turn=turn: g_ref.at[turn, :, away, :], lambda turn=turn: fore_core.at[turn],
            {"dp": core},
        )
        sent.plan(
            ("O", turn), lambda turn=turn: g_ref.at[2 + turn, :, away, :],
            lambda turn=turn: own_core.at[turn], {"dp": core},
        )
    sent.plan("peer", lambda: fore_ref, lambda: own_peer, {"mp": peer})
    gain, shift = vec_ref[2:3, :], vec_ref[3:4, :]
    w_proj = wp_ref[...].reshape(512, 512)

    def rows(index):
        return pl.ds(pl.multiple_of(index * HALF, HALF), HALF)

    inputs = Loads(input_sem)
    for turn in range(4):
        at, columns = (peer, mp)[turn // 2], slice(turn % 2 * 512, turn % 2 * 512 + 512)
        inputs.plan(
            ("up", turn), lambda at=at, columns=columns: wu_in.at[at, :, columns],
            lambda at=at, columns=columns: wu_ref.at[at, :, columns],
        )
        inputs.plan(
            ("down", turn), lambda at=at, columns=columns: wd_in.at[at, columns, :],
            lambda at=at, columns=columns: wd_ref.at[at, columns, :],
        )

    @pl.when(step == 0)
    def _():
        for turn in range(4):
            inputs.start(("up", turn))
            inputs.start(("down", turn))
        greet([{"dp": core}, {"mp": peer}])

        def body(index, carry):
            x_rows = x_ref[pl.ds(row_block(index, mp), HALF), :].astype(F32)
            mixed = ot_ref[:, pl.ds(ext_cols(index), HALF)]
            resid = x_rows + mm_tn(mixed, w_proj) + vec_ref[4:5, :]
            res_ref[rows(index), :] = resid
            n2_ref[rows(index), :] = layer_norm_rows(resid, gain, shift)[0].astype(BF)
            out_ref[rows(index), :] = resid + vec_ref[5:6, :]
            dn_ref[rows(index), :] = jnp.zeros((HALF, 512), F32)
            dyc_ref[rows(index), :] = dy_ref[pl.ds(row_block(index, mp), HALF), :]
            return carry

        lax.fori_loop(0, 5, body, 0, unroll=True)

    for turn in range(4):

        @pl.when(step == turn)
        def _():
            inputs.wait(("up", turn))
            inputs.wait(("down", turn))

    lanes = pl.ds(pl.multiple_of(part * 512, 512), 512)
    w_up, w_down = wu_ref[side, :, lanes], wd_ref[side, lanes, :]
    up_bias = small_ref[side, 0:1, lanes]

    def up_of(index):
        return mm_nn(n2_ref[index * HALF : index * HALF + HALF, :], w_up) + up_bias

    total = jnp.zeros((8, 512), F32)
    pre = up_of(0)
    for index in range(5):
        at = slice(index * HALF, index * HALF + HALF)
        up_pre = pre
        if index < 4:
            pre = up_of(index + 1)
        dhid = mm_nt(dyc_ref[at, :], w_down)
        cumulative = 0.5 * (1.0 + lax.erf(up_pre * (0.5**0.5)))
        density = jnp.exp(-0.5 * up_pre * up_pre) * 0.3989422804014327
        hidden = (up_pre * cumulative).astype(BF)
        hid_ref[at, :] = hidden
        slope = cumulative + up_pre * density
        dup = (dhid * slope).astype(BF)
        dup_ref[at, :] = dup
        total = total + jnp.sum(dup.astype(F32).reshape(HALF // 8, 8, 512), axis=0)
        out_ref[at, :] += mm_nn(hidden, w_down)
        dn_ref[at, :] += mm_nt(dup, w_up)
        if index == 1:

            @pl.when(step == 1)
            def _():
                sent.arrive(("F", 0))
                fore_ref[...] = g_ref[0, :, kept, :] + fore_core[0]
                sent.start("peer")

            @pl.when(step == 2)
            def _():
                sent.arrive(("F", 1))
                fore_out[...] = g_ref[1, :, kept, :] + fore_core[1]

    bsum_ref[2 * side + part] = total
    g_ref[step, 0] = mm_tn(hid_ref[...], dyc_ref[...]).astype(BF)
    g_ref[step, 1] = mm_tn(n2_ref[...], dup_ref[...]).astype(BF)
    for turn, key in enumerate((("F", 0), ("F", 1), ("O", 0), ("O", 1))):

        @pl.when(step == turn)
        def _():
            sent.start(key)

    @pl.when(step == 3)
    def _():
        vsum_ref[...] = jnp.zeros_like(vsum_ref)

        def body(index, carry):
            at = rows(index)
            act_ref[pl.ds(row_block(index, mp), HALF), :] = out_ref[at, :].astype(BF)
            _, unit, inverse = layer_norm_rows(res_ref[at, :], gain, shift)
            dn = dn_ref[at, :]
            dy = dyc_ref[at, :].astype(F32)
            dres = dy + layer_norm_back(dn, unit, inverse, gain)
            dres_ref[at, :] = dres
            branch = dres.astype(BF)
            br_ref[at, :] = branch
            dot_ref[:, pl.ds(ext_cols(index), HALF)] = mm_nt(w_proj, branch).astype(BF)
            sums = [dn * unit, dn, branch.astype(F32), dy]
            for place, value in enumerate(sums):
                vsum_ref[place] += jnp.sum(value.reshape(HALF // 8, 8, 512), axis=0)
            return carry

        lax.fori_loop(0, 5, body, 0, unroll=True)
        mixed = jnp.concatenate([ot_ref[:, 0:HALF], ot_ref[:, SEQ:]], axis=1)
        gp_ref[...] = mm_nn(mixed, br_ref[...]).astype(BF).reshape(2, 256, 512)
        sent.arrive(("O", 0))
        sent.arrive(("O", 1))
        sent.arrive("peer")
        near = g_ref[2, :, kept, :].astype(F32) + own_core[0].astype(F32)
        own_out[0] = (near + own_peer[...].astype(F32)).astype(BF)
        own_out[1] = g_ref[3, :, kept, :] + own_core[1]
        sent.finish()


def mlp(patches, cotangent, ot, wp, wu, wd, vec_params, small):
    rows = patches.shape[0]
    ext = 3 * SEQ
    hbm = pl.BlockSpec(memory_space=pl.ANY)
    return pl.pallas_call(
        mlp_kernel,
        grid=(4,),
        out_shape=[
            sds((rows, 512), BF), sds((rows, 512), F32), sds((512, ext), BF), sds((2, 2, HALF, 512), BF),
            sds((2, HALF, 512), BF), sds((2, 256, 512), BF), sds((4, 8, 512), F32), sds((4, 8, 512), F32),
        ],
        in_specs=[
            full_spec((rows, 512)), full_spec((rows, 512)), full_spec((512, ext)), full_spec(wp.shape),
            hbm, hbm, full_spec(vec_params.shape), full_spec(small.shape),
        ],
        out_specs=[
            full_spec((rows, 512)), full_spec((rows, 512)), full_spec((512, ext)),
            full_spec((2, 2, HALF, 512)), full_spec((2, HALF, 512)),
            full_spec((2, 256, 512)), full_spec((4, 8, 512)), full_spec((4, 8, 512)),
        ],
        scratch_shapes=[
            pltpu.VMEM((rows, 512), F32), pltpu.VMEM((rows, 512), BF), pltpu.VMEM((rows, 512), F32),
            pltpu.VMEM((rows, 512), F32), pltpu.VMEM((rows, 512), BF), pltpu.VMEM((rows, 512), BF),
            pltpu.VMEM((rows, 512), BF), pltpu.VMEM((rows, 512), BF), pltpu.VMEM((4, 2, 512, 512), BF),
            pltpu.VMEM((2, HALF, 512), BF), pltpu.VMEM((2, 2, HALF, 512), BF),
            pltpu.VMEM((2, 2, HALF, 512), BF), pltpu.VMEM((2, HALF, 512), BF),
            pltpu.VMEM(wu.shape, BF), pltpu.VMEM(wd.shape, BF), pltpu.SemaphoreType.DMA((5,)),
            pltpu.SemaphoreType.DMA((5,)), pltpu.SemaphoreType.DMA((8,)),
        ],
        compiler_params=pltpu.CompilerParams(
            collective_id=2, has_side_effects=True, vmem_limit_bytes=VMEM_LIMIT
        ),
        name="mlp",
    )(patches, cotangent, ot, wp, wu, wd, vec_params, small)


SCHEDULE = (
    (
        ("F", 2, 1), ("F", 4, 0), ("O", 0, 1), ("O", 1, 1), ("O", 4, 0),
    ),
    (
    ),
    (
        ("F", 3, 1),
    ),
    (
        ("O", 0, 2),
    ),
    (
    ),
    (
        ("F", 4, 1), ("O", 1, 2), ("O", 2, 1),
    ),
    (
    ),
    (
    ),
    (
        ("F", 5, 0), ("O", 0, 3), ("O", 3, 1),
    ),
    (
        ("O", 1, 3),
    ),
    (
        ("F", 5, 1), ("O", 4, 1),
    ),
    (
        ("O", 2, 2),
    ),
    (
        ("F", 6, 0), ("O", 0, 4),
    ),
    (
        ("O", 3, 2),
    ),
    (
        ("F", 6, 1), ("O", 1, 4),
    ),
    (
        ("O", 4, 2),
    ),
    (
        ("O", 0, 5), ("O", 2, 3), ("O", 5, 0),
    ),
    (
    ),
    (
        ("O", 0, 6), ("O", 1, 5), ("O", 3, 3),
    ),
    (
        ("O", 4, 3),
    ),
    (
        ("O", 1, 6), ("O", 2, 4), ("O", 6, 0),
    ),
    (
        ("O", 5, 1),
    ),
    (
    ),
    (
        ("O", 3, 4),
    ),
    (
        ("O", 6, 1),
    ),
    (
        ("O", 4, 4),
    ),
    (
        ("O", 2, 5), ("small", 0), ("O", 5, 3), ("O", 2, 6), ("O", 3, 5), ("O", 4, 5), ("O", 3, 6),
        ("small", 1), ("O", 4, 6), ("O", 6, 3), ("small", 2), ("square", 0), ("square", 1), ("O", 5, 5),
        ("square", 2), ("O", 5, 6), ("O", 6, 5), ("O", 6, 6),
    ),
)


def cut(ref, start, size):
    rows = pl.ds(pl.multiple_of(start, 16), size)
    return ref.at[:, rows, :] if len(ref.shape) == 3 else ref.at[rows, :]


WIDE = (5, 6)
PIECES = ((512, 512), (512, 512), (512, 512), (512, 512), (256, 512), (3, 512, 128), (3, 512, 128))


def piece_rows(index, size):
    return (*PIECES[index][:-2], PIECES[index][-2] // size, PIECES[index][-1])


def backward_kernel(
    count_ref, qt_in, kt_in, dot_in, ot_in, k_in, v_in, lse_ref, nt_in, wt_in,
    own_in, fore_in, gp_in, x_in, dres_in, vec_ref, two_ref, up_sum_ref,
    grad_out, down_out, up_out, proj_out, qkv_out, small_out, norm_out,
    qt_ref, kt_ref, dot_ref, ot_ref, k_ref, v_ref, nt_ref, wt_ref, x_ref, dres_ref, grad_ref,
    shared_ref, grads_ref, bias_ref, s_ref, dp_ref, g_ref, bsum_ref,
    far_send, far_recv, early_core, early_part, early_all, late_core, late_part, late_all, square_sum, square_core, square_all, *rest,
):
    buffers, (send_sem, recv_sem, local_sem) = rest[:-3], rest[-3:]
    dp, mp = lax.axis_index("dp"), lax.axis_index("mp")
    peer = 1 - mp
    core, x_side, _, _ = partners(dp)
    to_core, to_peer, to_x = {"dp": core}, {"mp": peer}, {"dp": x_side}
    core_bit, x_bit = lax.rem(dp, 2), lax.rem(lax.div(dp, 2), 2)
    chip, floor = lax.div(dp, 2), lax.div(dp, 4)

    def ring(index):
        return (chip, 8, 2) if index in WIDE else (floor, 4, 4)
    sent, loads = Transfers(send_sem, recv_sem), Loads(local_sem)

    def block_at(place):
        return 2 * jnp.where(place < 2, peer, mp) + lax.rem(place, 2)

    def source(index, side):
        if index == 4:
            return gp_in.at[side]
        return g_ref.at[index - 5 + (0 if side is peer else 2)]

    def result(index):
        if index < 4:
            lanes = slice(index // 2 * 512, index // 2 * 512 + 512)
            return up_out.at[:, lanes] if index % 2 else down_out.at[lanes, :]
        if index == 4:
            return proj_out
        return qkv_out.at[:, :, slice((index - 5) * 128, (index - 5) * 128 + 128)]

    def piece_buffers(index):
        return buffers[8 * index : 8 * index + 8]

    def region(index):
        half = PIECES[index][-2] // 2
        if index in WIDE:
            return core_bit * half, half
        return core_bit * half + x_bit * (half // 2), half // 2

    names = ("qt", "kt", "dot", "ot", "k", "v")
    sources = (qt_in, kt_in, dot_in, ot_in, k_in, v_in)
    homes = (qt_ref, kt_ref, dot_ref, ot_ref, k_ref, v_ref)
    for place in range(4):
        rows = pl.ds(pl.multiple_of(block_at(place) * 128, 128), 128)
        for name, src, dst in zip(names, sources, homes):
            loads.plan(
                (name, place),
                lambda src=src, rows=rows: src.at[rows, :] if src.shape[0] == 512 else src.at[:, rows],
                lambda dst=dst, place=place: dst.at[place],
            )

    def load_block(place):
        for name in names:
            loads.start((name, place))

    def loaded(place):
        for name in names:
            loads.wait((name, place))

    load_block(0)
    loads.start("wt", lambda: wt_in, lambda: wt_ref)
    for index in range(4):
        loads.plan(
            ("kept", index, 2), lambda index=index: own_in.at[index // 2, index % 2],
            lambda index=index: piece_buffers(index)[2],
        )
        if index > 1:
            loads.plan(
                ("kept", index, 0), lambda index=index: fore_in.at[index % 2],
                lambda index=index: piece_buffers(index)[0],
            )
    half = PIECES[4][-2] // 2
    for side, slot in ((peer, 0), (mp, 2)):
        loads.plan(
            ("kept", 4, slot), lambda side=side: cut(source(4, side), core_bit * half, half),
            lambda slot=slot: piece_buffers(4)[slot],
        )
    for key in ((2, 0), (0, 2), (1, 2), (3, 0), (2, 2), (3, 2), (4, 0), (4, 2)):
        loads.start(("kept", *key))
    loads.plan("nt", lambda: nt_in, lambda: nt_ref)
    loads.plan("x", lambda: x_in, lambda: x_ref)
    loads.plan("dres", lambda: dres_in, lambda: dres_ref)
    chips = [
        {"dp": lax.rem(dp + 2 * step, 16), "mp": side} for side in (mp, peer) for step in range(8)
    ][1:]
    greet([to_core] + chips)

    def plan_piece(index):
        total = PIECES[index][-2]
        half = total // 2
        kept = core_bit * half
        fore, fore_core, own, own_core, own_peer, own_x, landing, out = piece_buffers(index)
        away = (1 - core_bit) * half
        if index > 1:
            sent.plan(("F", index, 1), lambda: fore, lambda: own_peer, to_peer)
        if index > 3:
            sent.plan(("F", index, 0), lambda: cut(source(index, peer), away, half), lambda: fore_core, to_core)
            sent.plan(("O", index, 0), lambda: cut(source(index, mp), away, half), lambda: own_core, to_core)
        if index not in WIDE:
            other_x = (1 - x_bit) * (half // 2)
            sent.plan(("O", index, 1), lambda: cut(own, other_x, half // 2), lambda: own_x, to_x)
        first, size = region(index)
        me, members, stride = ring(index)
        size //= members
        for step in range(1, members):
            target = {"dp": lax.rem(dp + stride * step, 16)}
            their = lax.rem(me + step, members) * size + first
            mine = me * size + first
            sent.plan(
                ("O", index, 2, step), lambda their=their: cut(own, their - kept, size),
                lambda step=step: landing.at[step - 1], target,
            )
            place = lambda mine=mine: cut(out, mine, size)
            sent.plan(("O", index, 3, step), place, place, target)
        if index not in WIDE:
            across = lambda: cut(out, region(index)[0], half // 2)
            sent.plan(("O", index, 4), across, across, to_x)
        whole = lambda: cut(out, kept, half)
        sent.plan(("O", index, 5), whole, whole, to_core)
        loads.plan(("out", index), lambda: out, lambda: result(index))

    def event(kind, index, stage):
        total = PIECES[index][-2]
        half = total // 2
        kept = core_bit * half
        wide = index in WIDE
        fore, fore_core, own, own_core, own_peer, own_x, landing, out = piece_buffers(index)
        first, size = region(index)
        me, members, _ = ring(index)
        size //= members

        def each(stage, call):
            for step in range(1, members):
                call(("O", index, stage, step))

        if stage == 0:
            sent.start((kind, index, 0))
        elif kind == "F":
            if index > 3:
                sent.arrive((kind, index, 0))
            if index < 4:
                loads.wait(("kept", index, 0))
            elif index < 5:
                loads.wait(("kept", index, 0))
                fore[...] += fore_core[...]
            else:
                fore[...] = cut(source(index, peer), kept, half)[...] + fore_core[...]
            sent.start((kind, index, 1))
        elif stage == 1:
            if index > 3:
                sent.arrive((kind, index, 0))
            if index > 1:
                sent.arrive(("F", index, 1))
            if index < 5:
                loads.wait(("kept", index, 2))
            if index > 1:
                base = (own if index < 5 else cut(source(index, mp), kept, half))[...].astype(F32)
                if index > 3:
                    base = base + own_core[...].astype(F32)
                own[...] = (base + own_peer[...].astype(F32)).astype(BF)
            if wide:
                each(2, sent.start)
            else:
                sent.start((kind, index, 1))
        elif stage == 2:
            sent.arrive((kind, index, 1))
            at = x_bit * (half // 2)
            cut(own, at, half // 2)[...] += own_x[...]
            each(2, sent.start)
        elif stage == 3:
            each(2, sent.arrive)
            value = cut(own, first - kept + me * size, size)[...].astype(F32)
            for step in range(members - 1):
                value = value + landing[step].astype(F32)
            value = value.astype(BF)
            cut(out, first + me * size, size)[...] = value
            each(3, sent.start)
            squared = value.astype(F32)
            square = jnp.sum((squared * squared).reshape(-1, 8, squared.shape[-1]), axis=0)
            folded = square[:, 0:128]
            for lane in range(1, square.shape[1] // 128):
                folded = folded + square[:, lane * 128 : lane * 128 + 128]
            square_sum[...] += folded
        elif stage == 4:
            each(3, sent.arrive)
            sent.start((kind, index, 4))
        elif stage == 5:
            if wide:
                each(3, sent.arrive)
            else:
                sent.arrive((kind, index, 4))
            sent.start((kind, index, 5))
        else:
            sent.arrive((kind, index, 5))
            loads.start(("out", index))

    for index in range(7):
        plan_piece(index)

    me = mp * 8 + chip
    rows_mine = pl.ds(pl.multiple_of(core_bit * 8, 8), 8)
    rows_other = pl.ds(pl.multiple_of(8 - core_bit * 8, 8), 8)
    sums_of = {"early": (early_core, early_part, early_all), "late": (late_core, late_part, late_all)}
    sent.plan("square core", lambda: square_sum, lambda: square_core, to_core)
    for name, (both, part, everyone) in sums_of.items():
        sent.plan(
            (name, "core"), lambda both=both: both.at[0, rows_other],
            lambda both=both: both.at[1, rows_other], to_core,
        )
        back = lambda part=part: part.at[rows_mine]
        sent.plan((name, "back"), back, back, to_core)
        for place, target in enumerate(chips):
            slot = lambda everyone=everyone: everyone.at[me]
            sent.plan((name, place), slot, slot, target)
    for place, target in enumerate(chips):
        sent.plan(("square", place), lambda: square_all.at[me], lambda: square_all.at[me], target)

    def everywhere(name, call):
        for place in range(len(chips)):
            call((name, place))

    def spread(name, stage):
        both, part, everyone = sums_of[name]
        if stage == 0:
            sent.arrive((name, "core"))
            everyone[me] = both[0, rows_mine] + both[1, rows_mine]
            everywhere(name, sent.start)
        elif stage == 1:
            everywhere(name, sent.arrive)
            part[rows_mine] = jnp.sum(everyone[...], axis=0)
            sent.start((name, "back"))
        else:
            sent.arrive((name, "back"))

    for row in range(8):
        value = jnp.sum(up_sum_ref[row] if row < 4 else two_ref[row - 4], axis=0, keepdims=True)
        early_core[0, row : row + 1, :] = value[:, 0:256]
        early_core[0, 8 + row : 9 + row, :] = value[:, 256:512]

    def run(events):
        for item in events:
            event(*item)

    square_sum[...] = jnp.zeros((8, 128), F32)
    bias_ref[0] = key_bias((SEQ, 128), mp, count_ref[2], True)
    for group in (1, 2):
        bias_ref[group] = key_bias((SEQ, 128), mp, count_ref[3 * mp + group - 1], False)
    sent.start(("early", "core"))
    run(SCHEDULE[0])

    def tiles(place, group, queries, sub):
        base = pl.multiple_of(group * SEQ, SEQ)
        keys_at, queries_at = pl.ds(base, SEQ), pl.ds(base, queries)
        own = slice(sub * HD, sub * HD + HD)
        s_ref[sub % 2, :, :queries] = score_tile(
            k_ref[place, keys_at, :], bias_ref[group], qt_ref[place, own, queries_at], sub
        )
        dp_ref[sub % 2, :, :queries] = mm_nn(
            v_ref[place, keys_at, :], widen_plain(dot_ref[place, own, queries_at], sub)
        )

    def heads(place, group, queries, out, out_base, following, between):
        block = block_at(place)
        base = pl.multiple_of(group * SEQ, SEQ)
        keys_at, queries_at = pl.ds(base, SEQ), pl.ds(base, queries)
        out_keys = pl.ds(out_base, SEQ)
        out_queries = pl.ds(out_base, queries)
        for sub in range(4):
            if sub < 3:
                tiles(place, group, queries, sub + 1)
            else:
                tiles(*following, queries, 0)
            own = slice(sub * HD, sub * HD + HD)
            q_rows, do_rows = qt_ref[place, own, queries_at], dot_ref[place, own, queries_at]
            delta = jnp.sum(
                do_rows.astype(F32) * ot_ref[place, own, queries_at].astype(F32), axis=0, keepdims=True
            )
            probs = jnp.exp2(
                s_ref[sub % 2, :, :queries] - lse_ref[group, block, sub : sub + 1, :queries]
            )
            draw = (probs * (dp_ref[sub % 2, :, :queries] - delta)).astype(BF)
            dq = mm_nn(kt_ref[place, own, keys_at], draw) * (HD ** (-0.5))
            out[own, out_queries] = dq.astype(BF)
            dk = mm_nt(q_rows, draw) * (1.0 / LOG2E)
            out[128 + sub * HD : 160 + sub * HD, out_keys] = dk.astype(BF)
            dv = mm_nt(do_rows, probs.astype(BF))
            out[256 + sub * HD : 288 + sub * HD, out_keys] = dv.astype(BF)
            if sub == 1:
                between()

    def weights_of(place):
        block = block_at(place)
        side, part = lax.div(block, 2), lax.rem(block, 2)
        return wt_ref[side, :, pl.ds(pl.multiple_of(part * 128, 128), 128), :].reshape(384, 512)

    for place in range(4):
        shared_ref[place, 0:128, HALF:SEQ] = jnp.zeros((128, HALF), BF)

    loaded(0)
    load_block(1)
    loads.wait("wt")

    def shared_step(place, carry):
        for turn in range(3):

            @pl.when(place == turn)
            def _():
                loaded(turn + 1)
                if turn < 2:
                    load_block(turn + 2)
                else:
                    loads.start("nt")
                    loads.start("x")
                    loads.start("dres")

        heads(place, 0, HALF, shared_ref.at[place], 0, (jnp.minimum(place + 1, 3), 0), lambda: None)
        for turn in range(4):

            @pl.when(place == turn)
            def _():
                run(SCHEDULE[1 + turn])
                if turn == 0:
                    spread("early", 0)
                elif turn == 3:
                    spread("early", 1)

        return carry

    tiles(0, 0, HALF, 0)
    lax.fori_loop(0, 4, shared_step, 0)
    tiles(0, 1, SEQ, 0)
    def rows_grad(grads, columns):
        total = mm_tn(grads[0, :, columns], weights_of(0))
        for place in range(1, 4):
            total += mm_tn(grads[place, :, columns], weights_of(place))
        return total

    far_send[...] = rows_grad(shared_ref, slice(HALF, SEQ)).astype(BF)
    spread("early", 2)
    sent.start("far", lambda: far_send, lambda: far_recv, to_peer)
    loads.wait("nt")

    def main_step(step, carry):
        place, group = lax.div(step, 2), 1 + lax.rem(step, 2)

        def pump(first):
            for turn in range(8):

                @pl.when(step == turn)
                def _():
                    run(SCHEDULE[first + 2 * turn])

        out_base = pl.multiple_of((group - 1) * SEQ, SEQ)
        after = jnp.minimum(step + 1, 7)
        following = (lax.div(after, 2), 1 + lax.rem(after, 2))
        heads(place, group, SEQ, grads_ref.at[place], out_base, following, lambda: pump(5))

        @pl.when(group == 2)
        def _():
            for part in range(3):
                rows = slice(part * 128, part * 128 + 128)
                total = mm_nt(nt_ref[:, 0:SEQ], shared_ref[place, rows, :])
                total += mm_nt(nt_ref[:, SEQ:], grads_ref[place, rows, :])
                g_ref[place, part] = total.astype(BF)
            ones = jnp.ones((8, 2 * SEQ), BF)
            bsum_ref[place] = mm_nt(ones[:, :SEQ], shared_ref[place]) + mm_nt(ones, grads_ref[place])

        pump(6)
        return carry

    lax.fori_loop(0, 8, main_step, 0)

    gain, shift = vec_ref[0:1, :], vec_ref[1:2, :]
    loads.wait("x")
    loads.wait("dres")
    run(SCHEDULE[21])

    for index in range(5):
        where = pl.ds(row_block(index, mp), HALF)
        loads.plan(
            ("grad", index), lambda where=where: grad_ref.at[where, :],
            lambda where=where: grad_out.at[where, :],
        )

    def finish_rows(index, dn, sums):
        at = pl.ds(pl.multiple_of(index * HALF, HALF), HALF)
        place = pl.ds(row_block(index, mp), HALF)
        _, unit, inverse = layer_norm_rows(x_ref[place, :].astype(F32), gain, shift)
        grad_ref[place, :] = dres_ref[at, :] + layer_norm_back(dn, unit, inverse, gain)
        folded = [jnp.sum(value.reshape(HALF // 8, 8, 512), axis=0) for value in (dn * unit, dn)]
        return sums[0] + folded[0], sums[1] + folded[1]

    def finish_step(index, sums):
        columns = pl.ds(pl.multiple_of(HALF * index - HALF, HALF), HALF)
        sums = finish_rows(index, rows_grad(grads_ref, columns), sums)
        for turn in range(1, 5):

            @pl.when(index == turn)
            def _():
                loads.start(("grad", turn))
                run(SCHEDULE[21 + turn])

        return sums

    zero = jnp.zeros((8, 512), F32)
    sums = lax.fori_loop(1, 5, finish_step, (zero, zero))
    sent.arrive("far")
    sums = finish_rows(0, rows_grad(shared_ref, slice(0, HALF)) + far_recv[...].astype(F32), sums)
    loads.start(("grad", 0))

    for place in range(4):
        lanes = slice(place * 128, place * 128 + 128)
        for row, value in enumerate((sums[0], sums[1])):
            late_core[0, 8 + 4 * row + place : 9 + 4 * row + place, :] = jnp.sum(
                value[:, lanes], axis=0, keepdims=True
            )
        for row, columns in enumerate((slice(0, 128), slice(256, 384))):
            late_core[0, 4 * row + place : 4 * row + place + 1, :] = jnp.where(
                mp == 0, bsum_ref[(place + 2) % 4, 0:1, columns], bsum_ref[place, 0:1, columns]
            )

    def square_stage(stage):
        if stage == 0:
            sent.start("square core")
        elif stage == 1:
            sent.arrive("square core")
            square_all[me] = square_sum[...] + square_core[...]
            everywhere("square", sent.start)
        else:
            everywhere("square", sent.arrive)
            for row in range(4):
                at = (0, 1, 6, 7)[row]
                for lane in range(4):
                    small_out[at : at + 1, lane * 128 : lane * 128 + 128] = late_part[
                        4 * row + lane : 4 * row + lane + 1, :
                    ]
            for row in range(8):
                at = 2 + row if row < 4 else 4 + row
                small_out[at : at + 1, 0:256] = early_part[row : row + 1, :]
                small_out[at : at + 1, 256:512] = early_part[8 + row : 9 + row, :]
            small_out[12:16, :] = jnp.zeros((4, 512), F32)
            small = small_out[...]
            total = jnp.sum(small * small) + jnp.sum(jnp.sum(square_all[...], axis=0))
            norm_out[...] = jnp.sqrt(jnp.full((8, 128), total, F32))

    sent.start(("late", "core"))
    for item in SCHEDULE[26]:
        if item[0] == "small":
            spread("late", item[1])
        elif item[0] == "square":
            square_stage(item[1])
        else:
            event(*item)
    sent.finish()
    for index in range(7):
        loads.wait(("out", index))
    for index in range(5):
        loads.wait(("grad", index))


def backward(key_count, qt, kt, dot, ot, k, v, lse, nt, wt, owns, fores, gp, patches, dres, vec_params, two, ups):
    ext, rows = 3 * SEQ, patches.shape[0]
    vmem, hbm = pl.BlockSpec(memory_space=pltpu.VMEM), pl.BlockSpec(memory_space=pl.ANY)
    buffers = []
    for index in range(7):
        for size in (2, 2, 2, 2, 2, 4):
            buffers.append(pltpu.VMEM(piece_rows(index, size), BF))
        members = 7 if index in WIDE else 3
        buffers.append(pltpu.VMEM((members, *piece_rows(index, 16)), BF))
        buffers.append(pltpu.VMEM(piece_rows(index, 1), BF))
    return pl.pallas_call(
        backward_kernel,
        out_shape=[
            sds((rows, 512), F32), sds((1024, 512), BF), sds((512, 1024), BF), sds((256, 512), BF),
            sds((3, 512, 256), BF), sds((16, 512), F32), sds((8, 128), F32),
        ],
        in_specs=[pl.BlockSpec(memory_space=pltpu.SMEM)] + [hbm] * 6 + [vmem] + [hbm] * 7 + [vmem] * 3,
        out_specs=[hbm] * 5 + [vmem] * 2,
        scratch_shapes=[
            *[pltpu.VMEM((4, 128, ext), BF)] * 4, *[pltpu.VMEM((4, ext, 128), BF)] * 2,
            pltpu.VMEM((512, ext), BF), pltpu.VMEM((2, 3, 256, 512), BF), pltpu.VMEM((rows, 512), BF),
            pltpu.VMEM((rows, 512), F32), pltpu.VMEM((rows, 512), F32), pltpu.VMEM((4, 384, SEQ), BF), pltpu.VMEM((4, 384, 2 * SEQ), BF),
            pltpu.VMEM((3, SEQ, 128), BF), pltpu.VMEM((2, SEQ, SEQ), F32),
            pltpu.VMEM((2, SEQ, SEQ), F32), pltpu.VMEM((4, 3, 512, 128), BF), pltpu.VMEM((4, 8, 384), F32),
            pltpu.VMEM((HALF, 512), BF), pltpu.VMEM((HALF, 512), BF), pltpu.VMEM((2, 16, 256), F32),
            pltpu.VMEM((16, 256), F32), pltpu.VMEM((16, 8, 256), F32), pltpu.VMEM((2, 16, 128), F32),
            pltpu.VMEM((16, 128), F32), pltpu.VMEM((16, 8, 128), F32), pltpu.VMEM((8, 128), F32),
            pltpu.VMEM((8, 128), F32), pltpu.VMEM((16, 8, 128), F32), *buffers,
            pltpu.SemaphoreType.DMA((137,)), pltpu.SemaphoreType.DMA((137,)), pltpu.SemaphoreType.DMA((48,)),
        ],
        compiler_params=pltpu.CompilerParams(
            collective_id=1, has_side_effects=True, vmem_limit_bytes=VMEM_LIMIT
        ),
        name="backward",
    )(key_count, qt, kt, dot, ot, k, v, lse, nt, wt, owns, fores, gp, patches, dres, vec_params, two, ups)


ADAM_STEPS = 4


def adam_step(weight, gradient, moment_one, moment_two, step_rate, decay_rate):
    first_new = BETA_FIRST * moment_one + (1.0 - BETA_FIRST) * gradient
    second_new = BETA_SECOND * moment_two + (1.0 - BETA_SECOND) * gradient * gradient
    root = jnp.sqrt(second_new * (1.0 / (1.0 - BETA_SECOND**ADAM_STEP))) + ADAM_EPS
    change = first_new * (step_rate / (1.0 - BETA_FIRST**ADAM_STEP)) / root
    return weight * (1.0 - step_rate * decay_rate) - change, first_new, second_new


def adam_kernel(norm_ref, small_ref, *refs):
    mp = lax.axis_index("mp")
    factor = jnp.minimum(1.0, CLIP_NORM / (norm_ref[0:1, 0:1] + 1e-06))
    vectors, refs = refs[:9], refs[9:]
    matrices, refs = refs[:16], refs[16:]
    results, vector_results, norm_out = refs[:12], refs[12:21], refs[21]
    for index in range(4):
        weight_ref, one_ref, two_ref, grad_ref = matrices[4 * index : 4 * index + 4]
        values = adam_step(
            weight_ref[...], grad_ref[...].astype(F32) * factor, one_ref[...], two_ref[...],
            MATRIX_RATE, DECAY_RATE,
        )
        for out, value in zip(results[3 * index : 3 * index + 3], values):
            out[...] = value

    @pl.when(pl.program_id(0) == 0)
    def _():
        norm_out[...] = norm_ref[0:1, 0:1]
        first = mp == 0
        qv = jnp.where(first, small_ref[0:2, 0:256], small_ref[0:2, 256:512])
        up = jnp.where(first, small_ref[2:4, :], small_ref[4:6, :])
        up = jnp.concatenate(
            [up[row : row + 1, lane * 128 : lane * 128 + 128] for row in range(2) for lane in range(4)], axis=0
        )
        for index, total in enumerate((qv, up, small_ref[6:12, :])):
            weight_ref, one_ref, two_ref = vectors[3 * index : 3 * index + 3]
            values = adam_step(
                weight_ref[...], total * factor, one_ref[...], two_ref[...], VECTOR_RATE, 0.0
            )
            for out, value in zip(vector_results[3 * index : 3 * index + 3], values):
                out[...] = value


def adam_all(norm, small, vectors, groups):
    steps = ADAM_STEPS
    in_specs, out_specs, out_shape = [full_spec((8, 128)), full_spec(small.shape)], [], []
    args = [norm, small]
    for vector in vectors:
        in_specs += [full_spec(array.shape) for array in vector]
        args += list(vector)
    for group in groups:
        rows, width = group[0].shape
        spec = pl.BlockSpec((rows // steps, width), lambda i: (i, 0))
        in_specs += [spec] * 4
        out_specs += [spec] * 3
        out_shape += [sds((rows, width), F32)] * 3
        args += list(group)
    for vector in vectors:
        out_specs += [full_spec(array.shape) for array in vector]
        out_shape += [sds(array.shape, F32) for array in vector]
    return pl.pallas_call(
        adam_kernel,
        grid=(steps,),
        out_shape=out_shape + [sds((1, 1), F32)],
        in_specs=in_specs,
        out_specs=out_specs + [full_spec((1, 1))],
        compiler_params=pltpu.CompilerParams(vmem_limit_bytes=VMEM_LIMIT),
        name="adam_all",
    )(*args)


IN_SPECS = (
            P(("dp", "mp"), None),
            P(("dp", "mp"), None),
            P("dp"),
            P(None, None, "mp"),
            P("mp", None),
            P(None, "mp"),
            P("mp", None),
            P(None, "mp"),
            P("mp"),
            P(),
            P(None, None, "mp"),
            P(None, None, "mp"),
            P("mp", None),
            P("mp", None),
            P(None, "mp"),
            P(None, "mp"),
            P("mp", None),
            P("mp", None),
            P(None, "mp"),
            P(None, "mp"),
            P("mp"),
            P("mp"),
            P(),
            P(),
        )
OUT_SPECS = (
            P(("dp", "mp"), None),
            P(("dp", "mp"), None),
            P(),
            P(None, None, "mp"),
            P(None, None, "mp"),
            P(None, None, "mp"),
            P("mp", None),
            P("mp", None),
            P("mp", None),
            P(None, "mp"),
            P(None, "mp"),
            P(None, "mp"),
            P("mp", None),
            P("mp", None),
            P("mp", None),
            P(None, "mp"),
            P(None, "mp"),
            P(None, "mp"),
            P("mp"),
            P("mp"),
            P("mp"),
            P(),
            P(),
            P(),
        )


def paired(
    patches, cotangent, key_count, w_qkv, w_proj, w_up, w_down, qv_bias, up_bias, vec_params,
    first_qkv, second_qkv, first_proj, second_proj, first_up, second_up, first_down, second_down,
    first_qv_bias, second_qv_bias, first_up_bias, second_up_bias, first_vec, second_vec,
):
    wt, wp, wu, wd, small_all, nt, qt, kt, k, v, ot, lse = forward(
        key_count, w_qkv, w_proj, w_up, w_down, qv_bias, up_bias.reshape(1, 1024), patches, vec_params
    )
    activations, dres, dot, owns, fores, g_proj, vsum_two, up_sums = mlp(
        patches, cotangent, ot, wp, wu, wd, vec_params, small_all
    )
    input_grad, down, up, proj, qkv, small_total, norm = backward(
        key_count, qt, kt, dot, ot, k, v, lse, nt, wt, owns, fores, g_proj, patches, dres, vec_params,
        vsum_two, up_sums,
    )
    qkv = qkv.reshape(1536, 256)
    flat = lambda array: array.reshape(-1, array.shape[-1])
    groups = [
        (flat(w_qkv), flat(first_qkv), flat(second_qkv), qkv),
        (w_proj, first_proj, second_proj, proj),
        (w_up, first_up, second_up, up),
        (w_down, first_down, second_down, down),
    ]
    square = lambda array: array.reshape(8, 128)
    vectors = [
        (qv_bias, first_qv_bias, second_qv_bias),
        (square(up_bias), square(first_up_bias), square(second_up_bias)),
        (vec_params, first_vec, second_vec),
    ]
    outs = adam_all(norm, small_total, vectors, groups)
    return (
        activations, input_grad, outs[21].reshape(()), *[array.reshape(w_qkv.shape) for array in outs[0:3]],
        *outs[3:12], *outs[12:15], *[array.reshape(up_bias.shape) for array in outs[15:18]], *outs[18:21],
    )


def fits_pairs(mesh, args):
    if dict(mesh.shape) != {"dp": 16, "mp": 2}:
        return False
    return args[0].shape == (40960, 512) and args[2].shape == (80,)


def solution(mesh):
    def run(*args):
        body = paired if fits_pairs(mesh, args) else local
        return jax.shard_map(body, mesh=mesh, in_specs=IN_SPECS, out_specs=OUT_SPECS, check_vma=False)(*args)

    return run
```

```python
import jax
import jax.numpy as jnp
from jax import lax
from jax.experimental import pallas as pl
from jax.experimental.pallas import tpu as pltpu
from jax.sharding import PartitionSpec as P

HD = 32
ADAM_STEP = 10


NORM_EPS = 1e-06
BETA_FIRST = 0.9
BETA_SECOND = 0.95
ADAM_EPS = 1e-08
DECAY_RATE = 0.05
MATRIX_RATE = 0.1
VECTOR_RATE = 0.8
CLIP_NORM = 1.0
MASK_FILL = -1e30
LOG2E = 1.4426950408889634
BF = jnp.bfloat16
F32 = jnp.float32
MESH = pl.DeviceIdType.MESH
SEQ = 512
HALF = 256
VMEM_LIMIT = 58 * 1024 * 1024


def mm_nn(left, right):
    return lax.dot_general(left, right, (((1,), (0,)), ((), ())), preferred_element_type=F32)


def mm_nt(left, right):
    return lax.dot_general(left, right, (((1,), (1,)), ((), ())), preferred_element_type=F32)


def mm_tn(left, right):
    return lax.dot_general(left, right, (((0,), (0,)), ((), ())), preferred_element_type=F32)


def partners(dp):
    core = dp + 1 - 2 * lax.rem(dp, 2)
    x_side = dp + 2 - 4 * lax.rem(lax.div(dp, 2), 2)
    z_near = dp + 4 - 8 * lax.rem(lax.div(dp, 4), 2)
    z_far = dp + 8 - 16 * lax.rem(lax.div(dp, 8), 2)
    return core, x_side, z_near, z_far


def greet(targets):
    barrier = pltpu.get_barrier_semaphore()
    for target in targets:
        pl.semaphore_signal(barrier, inc=1, device_id=target, device_id_type=MESH)
    pl.semaphore_wait(barrier, len(targets))


def full_spec(shape):
    return pl.BlockSpec(shape, lambda *_: (0,) * len(shape))


def sds(shape, dtype):
    return jax.ShapeDtypeStruct(shape, dtype)


def row_block(index, mp):
    return pl.multiple_of(lax.rem(index + 4 * (1 - mp), 5) * HALF, HALF)


def ext_cols(index):
    return pl.multiple_of(jnp.where(index == 0, 0, HALF + HALF * index), HALF)


def norm_forward(values, norm_gain, norm_shift):
    row_mean = jnp.mean(values, axis=-1, keepdims=True)
    centred = values - row_mean
    inverse = lax.rsqrt(jnp.mean(centred * centred, axis=-1, keepdims=True) + NORM_EPS)
    normed = centred * inverse
    return (normed * norm_gain + norm_shift, normed, inverse)


def norm_backward(grad_rows, normed, inverse, norm_gain):
    scaled = grad_rows * norm_gain
    centre_term = jnp.mean(scaled, axis=-1, keepdims=True)
    slope_term = jnp.mean(scaled * normed, axis=-1, keepdims=True)
    return inverse * (scaled - centre_term - normed * slope_term)


def exact_gelu(values):
    return jax.nn.gelu(values, approximate=False)


def key_mask(key_count, length):
    position = lax.broadcasted_iota(jnp.int32, (1, 1, 1, length), 3)
    return position < key_count[:, None, None, None]


def masked_scores(queries, key_rows, key_count):
    raw_scores = jnp.einsum(
        "sqhe,skhe->shqk", queries, key_rows, preferred_element_type=jnp.float32
    )
    scaled = raw_scores * queries.shape[-1] ** (-0.5)
    return jnp.where(key_mask(key_count, key_rows.shape[1]), scaled, MASK_FILL)


def attend_backward(queries, key_rows, value_rows, key_count, log_total, attended_grad):
    scores = masked_scores(queries, key_rows, key_count)
    probs = jnp.exp(scores - log_total)
    probs_low = probs.astype(jnp.bfloat16)
    probs_grad = jnp.einsum(
        "sqhe,skhe->shqk", attended_grad, value_rows, preferred_element_type=jnp.float32
    )
    score_grad = probs * (probs_grad - jnp.sum(probs_grad * probs, axis=-1, keepdims=True))
    visible = key_mask(key_count, key_rows.shape[1])
    raw_grad = jnp.where(visible, score_grad * queries.shape[-1] ** (-0.5), 0.0).astype(
        jnp.bfloat16
    )
    query_grad = jnp.einsum(
        "shqk,skhe->sqhe", raw_grad, key_rows, preferred_element_type=jnp.float32
    )
    key_grad = jnp.einsum("shqk,sqhe->skhe", raw_grad, queries, preferred_element_type=jnp.float32)
    value_grad = jnp.einsum(
        "shqk,sqhe->skhe", probs_low, attended_grad, preferred_element_type=jnp.float32
    )
    return jnp.stack([query_grad, key_grad, value_grad])


def own_slice(values, own_start, own_rows):
    return lax.dynamic_slice_in_dim(values, own_start, own_rows, 0)


def contract_rows(left, right):
    return lax.dot_general(
        left, right, (((0,), (0,)), ((), ())), preferred_element_type=jnp.float32
    )


def contract_cols(left, right):
    return lax.dot_general(
        left, right, (((1,), (1,)), ((), ())), preferred_element_type=jnp.float32
    )


def adam_update(weight, gradient, moment_one, moment_two, step_rate, decay_rate):
    first_new = BETA_FIRST * moment_one + (1.0 - BETA_FIRST) * gradient
    second_new = BETA_SECOND * moment_two + (1.0 - BETA_SECOND) * gradient * gradient
    first_hat = first_new / (1.0 - BETA_FIRST**ADAM_STEP)
    second_hat = second_new / (1.0 - BETA_SECOND**ADAM_STEP)
    weight_new = weight - step_rate * (
        first_hat / (jnp.sqrt(second_hat) + ADAM_EPS) + decay_rate * weight
    )
    return (weight_new, first_new, second_new)


def local(
    patches,
    cotangent,
    key_count,
    w_qkv,
    w_proj,
    w_up,
    w_down,
    qv_bias,
    up_bias,
    vec_params,
    first_qkv,
    second_qkv,
    first_proj,
    second_proj,
    first_up,
    second_up,
    first_down,
    second_down,
    first_qv_bias,
    second_qv_bias,
    first_up_bias,
    second_up_bias,
    first_vec,
    second_vec,
):
    own_rows = patches.shape[0]
    seq_count = key_count.shape[0]
    own_start = lax.axis_index("mp") * own_rows
    local_width = w_proj.shape[0]
    local_heads = local_width // HD
    own_grad = cotangent.astype(jnp.float32)
    qkv_low = w_qkv.astype(jnp.bfloat16)
    proj_low = w_proj.astype(jnp.bfloat16)
    up_low = w_up.astype(jnp.bfloat16)
    down_low = w_down.astype(jnp.bfloat16)
    gain_one, shift_one = (vec_params[0], vec_params[1])
    gain_two, shift_two = (vec_params[2], vec_params[3])
    proj_shift, down_shift = (vec_params[4], vec_params[5])
    qkv_shift = jnp.stack([qv_bias[0], jnp.zeros_like(qv_bias[0]), qv_bias[1]])[:, None, :]
    gathered, grad_all = (
        lax.all_gather(patches, "mp", axis=0, tiled=True),
        lax.all_gather(cotangent, "mp", axis=0, tiled=True),
    )
    whole_rows = gathered.astype(jnp.float32)
    normed_all, unit_one, inverse_one = norm_forward(whole_rows, gain_one, shift_one)
    norm_one = normed_all.astype(jnp.bfloat16)
    projected = (
        jnp.einsum("td,cde->cte", norm_one, qkv_low, preferred_element_type=jnp.float32) + qkv_shift
    )
    shaped = projected.astype(jnp.bfloat16).reshape(3, seq_count, -1, local_heads, HD)
    queries, key_rows, value_rows = (shaped[0], shaped[1], shaped[2])
    scores = masked_scores(queries, key_rows, key_count)
    top_score = jnp.max(scores, axis=-1, keepdims=True)
    log_total = top_score + jnp.log(jnp.sum(jnp.exp(scores - top_score), axis=-1, keepdims=True))
    probs_low = jnp.exp(scores - log_total).astype(jnp.bfloat16)
    attended = jnp.einsum(
        "shqk,skhe->sqhe", probs_low, value_rows, preferred_element_type=jnp.float32
    )
    attended_low = attended.astype(jnp.bfloat16).reshape(-1, local_width)
    proj_part = jnp.dot(attended_low, proj_low, preferred_element_type=jnp.float32)
    resid_all = whole_rows + lax.psum(proj_part, "mp") + proj_shift
    mid_all, unit_two, inverse_two = norm_forward(resid_all, gain_two, shift_two)
    norm_two = mid_all.astype(jnp.bfloat16)
    up_pre = jnp.dot(norm_two, up_low, preferred_element_type=jnp.float32) + up_bias
    hidden_full, gelu_pull = jax.vjp(exact_gelu, up_pre)
    hidden_low = hidden_full.astype(jnp.bfloat16)
    down_part = jnp.dot(hidden_low, down_low, preferred_element_type=jnp.float32)
    out_all = (
        resid_all + lax.psum(down_part.astype(jnp.bfloat16), "mp").astype(jnp.float32) + down_shift
    )
    block_out = own_slice(out_all, own_start, own_rows)
    activations = block_out.astype(jnp.bfloat16)
    down_grad = contract_rows(hidden_low, grad_all)
    hidden_grad = contract_cols(grad_all, down_low)
    up_grad_rows = gelu_pull(hidden_grad)[0].astype(jnp.bfloat16)
    up_grad = contract_rows(norm_two, up_grad_rows)
    up_bias_grad = jnp.sum(up_grad_rows.astype(jnp.float32), axis=0)
    mid_part = contract_cols(up_grad_rows, up_low)
    mid_all_grad = lax.psum(mid_part.astype(jnp.bfloat16), "mp").astype(jnp.float32)
    resid_all_grad = grad_all.astype(jnp.float32) + norm_backward(
        mid_all_grad, unit_two, inverse_two, gain_two
    )
    branch_low = resid_all_grad.astype(jnp.bfloat16)
    own_branch = own_slice(branch_low, own_start, own_rows)
    mid_grad = own_slice(mid_all_grad, own_start, own_rows)
    mid_unit = own_slice(unit_two, own_start, own_rows)
    proj_grad = contract_rows(attended_low, branch_low)
    attended_grad = (
        contract_cols(branch_low, proj_low)
        .astype(jnp.bfloat16)
        .reshape(seq_count, -1, local_heads, HD)
    )
    qkv_grads = attend_backward(queries, key_rows, value_rows, key_count, log_total, attended_grad)
    qkv_grad_rows = qkv_grads.reshape(3, -1, local_width).astype(jnp.bfloat16)
    qkv_grad = jnp.einsum(
        "td,cte->cde", norm_one, qkv_grad_rows, preferred_element_type=jnp.float32
    )
    qkv_grad_sums = jnp.sum(qkv_grad_rows.astype(jnp.float32), axis=1)
    qv_bias_grad = jnp.stack([qkv_grad_sums[0], qkv_grad_sums[2]])
    first_part = jnp.einsum(
        "cte,cde->td", qkv_grad_rows, qkv_low, preferred_element_type=jnp.float32
    )
    first_all = lax.psum(first_part.astype(jnp.bfloat16), "mp").astype(jnp.float32)
    input_all = resid_all_grad + norm_backward(first_all, unit_one, inverse_one, gain_one)
    input_grad = own_slice(input_all, own_start, own_rows)
    own_first_grad = own_slice(first_all, own_start, own_rows)
    own_unit_one = own_slice(unit_one, own_start, own_rows)
    vec_grad = jnp.stack(
        [
            jnp.sum(own_first_grad * own_unit_one, axis=0),
            jnp.sum(own_first_grad, axis=0),
            jnp.sum(mid_grad * mid_unit, axis=0),
            jnp.sum(mid_grad, axis=0),
            jnp.sum(own_branch.astype(jnp.float32), axis=0),
            jnp.sum(own_grad, axis=0),
        ]
    )
    summed = (
        lax.psum(qkv_grad.astype(jnp.bfloat16), "dp").astype(jnp.float32),
        lax.psum(proj_grad.astype(jnp.bfloat16), "dp").astype(jnp.float32),
        lax.psum(up_grad.astype(jnp.bfloat16), "dp").astype(jnp.float32),
        lax.psum(down_grad.astype(jnp.bfloat16), "dp").astype(jnp.float32),
        lax.psum(qv_bias_grad.astype(jnp.bfloat16), "dp").astype(jnp.float32),
        lax.psum(up_bias_grad.astype(jnp.bfloat16), "dp").astype(jnp.float32),
        lax.psum(vec_grad.astype(jnp.bfloat16), "dp").astype(jnp.float32),
    )
    split_square = jnp.float32(0.0)
    for gradient in summed[:6]:
        split_square = split_square + jnp.sum(gradient * gradient)
    vec_total, split_total = lax.psum((summed[6], split_square), "mp")
    grad_norm = jnp.sqrt(split_total + jnp.sum(vec_total * vec_total))
    factor = jnp.minimum(1.0, CLIP_NORM / (grad_norm + 1e-06))
    qkv_new, qkv_first, qkv_second = adam_update(
        w_qkv, summed[0] * factor, first_qkv, second_qkv, MATRIX_RATE, DECAY_RATE
    )
    proj_new, proj_first, proj_second = adam_update(
        w_proj, summed[1] * factor, first_proj, second_proj, MATRIX_RATE, DECAY_RATE
    )
    up_new, up_first, up_second = adam_update(
        w_up, summed[2] * factor, first_up, second_up, MATRIX_RATE, DECAY_RATE
    )
    down_new, down_first, down_second = adam_update(
        w_down, summed[3] * factor, first_down, second_down, MATRIX_RATE, DECAY_RATE
    )
    qvb_new, qvb_first, qvb_second = adam_update(
        qv_bias, summed[4] * factor, first_qv_bias, second_qv_bias, VECTOR_RATE, 0.0
    )
    upb_new, upb_first, upb_second = adam_update(
        up_bias, summed[5] * factor, first_up_bias, second_up_bias, VECTOR_RATE, 0.0
    )
    vec_new, vec_first, vec_second = adam_update(
        vec_params, vec_total * factor, first_vec, second_vec, VECTOR_RATE, 0.0
    )
    return (
        activations,
        input_grad,
        grad_norm,
        qkv_new,
        qkv_first,
        qkv_second,
        proj_new,
        proj_first,
        proj_second,
        up_new,
        up_first,
        up_second,
        down_new,
        down_first,
        down_second,
        qvb_new,
        qvb_first,
        qvb_second,
        upb_new,
        upb_first,
        upb_second,
        vec_new,
        vec_first,
        vec_second,
    )


class Transfers:
    def __init__(self, send_sem, recv_sem):
        self.sems = (send_sem, recv_sem)
        self.all = {}

    def make(self, key):
        index, src, dst, target = self.all[key]
        return pltpu.make_async_remote_copy(
            src_ref=src(), dst_ref=dst(), send_sem=self.sems[0].at[index], recv_sem=self.sems[1].at[index],
            device_id=target, device_id_type=MESH,
        )

    def plan(self, key, src, dst, target):
        self.all[key] = (len(self.all), src, dst, target)

    def start(self, key, *views):
        if views:
            self.plan(key, *views)
        self.make(key).start()

    def arrive(self, key):
        self.make(key).wait_recv()

    def finish(self):
        for key in self.all:
            self.make(key).wait_send()


class Loads:
    def __init__(self, sem):
        self.sem = sem
        self.all = {}

    def make(self, key):
        index, src, dst = self.all[key]
        return pltpu.make_async_copy(src(), dst(), self.sem.at[index])

    def plan(self, key, src, dst):
        self.all[key] = (len(self.all), src, dst)

    def start(self, key, *views):
        if views:
            self.plan(key, *views)
        self.make(key).start()

    def wait(self, key):
        self.make(key).wait()


def layer_norm_rows(rows, gain, shift):
    centred = rows - jnp.mean(rows, axis=-1, keepdims=True)
    inverse = lax.rsqrt(jnp.mean(centred * centred, axis=-1, keepdims=True) + NORM_EPS)
    unit = centred * inverse
    return unit * gain + shift, unit, inverse


def layer_norm_back(grad, unit, inverse, gain):
    scaled = grad * gain
    centre = jnp.mean(scaled, axis=-1, keepdims=True)
    slope = jnp.mean(scaled * unit, axis=-1, keepdims=True)
    return inverse * (scaled - centre - unit * slope)


def head_rows(block, sub):
    return pl.ds(pl.multiple_of(block * 128 + sub * HD, HD), HD)


def head_cols(block):
    return pl.ds(pl.multiple_of(block * 128, 128), 128)


def key_bias(shape, mp, count, shared):
    slot = lax.broadcasted_iota(jnp.int32, shape, 0)
    if shared:
        slot = lax.rem(slot + HALF * mp, SEQ)
    return jnp.where(slot < count, 0.0, MASK_FILL).astype(BF)


def widen(rows, sub):
    zeros = jnp.zeros_like(rows)
    row = lax.broadcasted_iota(jnp.int32, rows.shape, 0)
    ones = jnp.where(row == 0, 1.0, 0.0).astype(BF)
    parts = [zeros] * 4
    parts[sub] = rows
    parts[(sub + 1) % 4] = ones
    return jnp.concatenate(parts, axis=0)


def widen_plain(rows, sub):
    parts = [jnp.zeros_like(rows)] * 4
    parts[sub] = rows
    return jnp.concatenate(parts, axis=0)


def score_tile(key_block, bias, query_rows, sub):
    lane = lax.broadcasted_iota(jnp.int32, key_block.shape, 1)
    keys = jnp.where(lane // HD == (sub + 1) % 4, bias, key_block)
    return mm_nn(keys, widen(query_rows, sub))


def forward_kernel(
    count_ref, qkv_ref, proj_in, up_in, down_in, qv_ref, up_bias_ref, x_in, vec_ref,
    wt_out, wp_out, wu_out, wd_out, sm_out,
    nt_out, qt_out, kt_out, k_out, v_out, ot_out, lse_out,
    wt_ref, own_proj, own_up, own_down, sm_ref, other_ref,
    norm_ref, nt_ref, qt_ref, kt_ref, vt_ref, k_ref, v_ref, ot_ref, lse_ref, bias_ref, s_ref,
    proj_ref, up_ref, down_ref, x_ref, send_sem, recv_sem, local_sem, input_sem,
):
    dp, mp = lax.axis_index("dp"), lax.axis_index("mp")
    inputs = Loads(input_sem)
    for name, src, dst in (
        ("x", x_in, x_ref), ("proj", proj_in, proj_ref), ("up", up_in, up_ref), ("down", down_in, down_ref)
    ):
        inputs.start(name, lambda src=src: src, lambda dst=dst: dst)
    peer = 1 - mp
    core, x_side, _, _ = partners(dp)
    quarter = lax.rem(dp, 4)
    x_quarter = lax.rem(quarter + 2, 4)
    gain, shift = vec_ref[0:1, :], vec_ref[1:2, :]
    greet([{"mp": peer}, {"dp": core}, {"dp": x_side}])

    remote, local = [], []

    class Transfer:
        def __init__(self, src, dst, target):
            self.index = len(remote)
            self.views = (src, dst, target)
            remote.append(self)
            self.make().start()

        def make(self):
            src, dst, target = self.views
            return pltpu.make_async_remote_copy(
                src_ref=src(), dst_ref=dst(), send_sem=send_sem.at[self.index],
                recv_sem=recv_sem.at[self.index], device_id=target, device_id_type=MESH,
            )

        def wait_recv(self):
            self.make().wait_recv()

        def wait_send(self):
            self.make().wait_send()

    def send(src, dst, target):
        return Transfer(src, dst, target)

    def keep(src, dst):
        copy = pltpu.make_async_copy(src, dst, local_sem.at[len(local)])
        copy.start()
        local.append(copy)

    def span(start, size):
        return pl.ds(pl.multiple_of(start, 16), size)

    pieces = []
    for part in range(3):
        pieces.append((wt_ref.at[mp, part], lambda side, part=part: wt_ref.at[side, part], 64, 0))
    pieces.append((own_proj, lambda side: wp_out.at[side], 64, 0))
    for shard, out, rows in ((own_up, wu_out, 128), (own_down, wd_out, 256)):
        for part in range(2):
            pieces.append((shard, lambda side, out=out: out.at[side], rows // 2, part * rows * 2))

    def place(ref, index, part):
        rows, base = pieces[index][2], pieces[index][3]
        return ref.at[span(base + part * rows, rows), :]

    first, second, third = {}, {}, {}

    def to_peer(index):
        first[index] = send(
            lambda: place(pieces[index][0], index, quarter),
            lambda: place(pieces[index][1](mp), index, quarter), {"mp": peer},
        )

    def to_sides(index):
        first[index].wait_recv()
        at = lambda: place(pieces[index][1](peer), index, quarter)
        second[index] = send(at, at, {"dp": x_side})
        third[index] = [send(at, at, {"dp": core})]

    def to_core(index):
        second[index].wait_recv()
        at = lambda: place(pieces[index][1](peer), index, x_quarter)
        third[index].append(send(at, at, {"dp": core}))

    def arrive(index):
        for copy in third[index]:
            copy.wait_recv()

    own_half = pl.multiple_of((1 - mp) * 4 * HALF, HALF)
    for part in range(3):
        wt_ref[mp, part] = qkv_ref[part].T.astype(BF)
        to_peer(part)
    sm_ref[mp] = jnp.zeros((8, 1024), F32)
    sm_ref[mp, 0:1, :] = up_bias_ref[...]
    sm_ref[mp, 1:3, 0:256] = qv_ref[...]
    small_copy = send(lambda: sm_ref.at[mp], lambda: sm_ref.at[mp], {"mp": peer})
    inputs.wait("proj")
    own_proj[...] = proj_ref[...].astype(BF)
    inputs.wait("up")
    own_up[...] = up_ref[...].astype(BF)
    inputs.wait("down")
    own_down[...] = down_ref[...].astype(BF)
    inputs.wait("x")
    keep(wt_ref.at[mp], wt_out.at[mp])
    keep(own_proj, wp_out.at[mp])
    keep(own_up, wu_out.at[mp])
    keep(own_down, wd_out.at[mp])

    def as_column(row):
        return jnp.broadcast_to(row, (8, row.shape[1])).T[:, 0:1]

    def normalise(group, part, rows):
        base = group * SEQ + part * HALF
        norm = layer_norm_rows(rows.astype(F32), gain, shift)[0].astype(BF)
        norm_ref[span(base, HALF), :] = norm
        nt_ref[:, pl.ds(pl.multiple_of(base, HALF), HALF)] = norm.T

    def project(side, group):
        base = pl.multiple_of(group * SEQ, SEQ)
        at = pl.ds(base, SEQ)
        own = pl.ds(pl.multiple_of(side * 256, 256), 256)
        norm = norm_ref[at, :]
        q_bias, v_bias = sm_ref[side, 1:2, 0:256], sm_ref[side, 2:3, 0:256]
        scale = LOG2E * HD ** (-0.5)
        qt_ref[own, at] = ((mm_nt(wt_ref[side, 0], norm) + as_column(q_bias)) * scale).astype(BF)
        kt_ref[own, at] = mm_nt(wt_ref[side, 1], norm).astype(BF)
        vt_ref[own, :] = (mm_nt(wt_ref[side, 2], norm) + as_column(v_bias)).astype(BF)
        k_ref[at, own] = mm_nt(norm, wt_ref[side, 1]).astype(BF)
        v_ref[at, own] = (mm_nt(norm, wt_ref[side, 2]) + v_bias).astype(BF)

    def attend(side, group, queries, between):
        base = pl.multiple_of(group * SEQ, SEQ)
        keys_at, queries_at = pl.ds(base, SEQ), pl.ds(base, queries)
        bias = bias_ref[group]

        def scores(block, sub):
            return score_tile(
                k_ref[keys_at, head_cols(block)], bias, qt_ref[head_rows(block, sub), queries_at], sub
            )

        s_ref[0, :, :queries] = scores(2 * side, 0)

        def body(step, carry):
            block = 2 * side + step
            for sub in range(4):
                following = (block, sub + 1) if sub < 3 else (2 * side + 1, 0)
                s_ref[(sub + 1) % 2, :, :queries] = scores(*following)
                tile = s_ref[sub % 2, :, :queries]
                top = jnp.max(tile, axis=0, keepdims=True)
                weights = jnp.exp2(tile - top)
                rows = head_rows(block, sub)
                values = jnp.concatenate([vt_ref[rows, :], jnp.ones((16, SEQ), BF)], axis=0)
                mixed = mm_nn(values, weights.astype(BF))
                total = mixed[HD : HD + 1]
                ot_ref[rows, queries_at] = (mixed[:HD] * (1.0 / total)).astype(BF)
                lse_ref[group, block, sub : sub + 1, :queries] = top + jnp.log2(total)

            @pl.when(step == 0)
            def _():
                between()

            return carry

        lax.fori_loop(0, 2, body, 0)

    def nothing():
        pass

    def unit(side, group, queries, early=nothing, between=nothing):
        project(side, group)
        early()
        attend(side, group, queries, between)
        at = pl.ds(pl.multiple_of(group * SEQ, SEQ), SEQ)
        own = pl.ds(pl.multiple_of(side * 256, 256), 256)
        keep(qt_ref.at[own, at], qt_out.at[own, at])
        keep(kt_ref.at[own, at], kt_out.at[own, at])
        keep(ot_ref.at[own, at], ot_out.at[own, at])
        keep(k_ref.at[at, own], k_out.at[at, own])
        keep(v_ref.at[at, own], v_out.at[at, own])

    def in_turn(*calls):
        def run():
            for call, *indices in calls:
                for index in indices:
                    call(index)

        return run

    for group in (1, 2):
        bias_ref[group] = key_bias((SEQ, 128), mp, count_ref[3 * mp + group - 1], False)
        for part in range(2):
            normalise(group, part, x_ref[pl.ds(row_block(2 * group - 1 + part, mp), HALF), :])
        if group == 1:
            to_peer(3)
            to_peer(4)
    bias_ref[0] = key_bias((SEQ, 128), mp, count_ref[2], True)
    normalise(0, 0, x_ref[pl.ds(row_block(0, mp), HALF), :])
    for index in range(3):
        to_sides(index)
    to_peer(5)
    unit(mp, 1, SEQ)
    in_turn((to_sides, 3, 4), (to_peer, 6))()
    unit(mp, 2, SEQ, between=in_turn((to_core, 0, 1, 2), (to_sides, 5), (to_peer, 7)))
    small_copy.wait_recv()
    keep(sm_ref, sm_out)
    for index in range(3):
        arrive(index)
    keep(wt_ref.at[peer], wt_out.at[peer])
    rows_copy = send(lambda: x_ref.at[pl.ds(own_half, HALF), :], lambda: other_ref, {"mp": peer})
    unit(peer, 1, SEQ, early=in_turn((to_sides, 6)), between=in_turn((to_core, 3, 4)))
    in_turn((to_sides, 7))()
    unit(peer, 2, SEQ, early=in_turn((to_core, 5)), between=in_turn((to_core, 6)))
    rows_copy.wait_recv()
    normalise(0, 1, other_ref[...])
    keep(nt_ref, nt_out)
    unit(mp, 0, HALF, between=in_turn((to_core, 7)))
    unit(peer, 0, HALF)
    keep(lse_ref, lse_out)
    for index in range(3, 8):
        arrive(index)
    for copy in remote:
        copy.wait_send()
    for copy in local:
        copy.wait()


def forward(key_count, w_qkv, w_proj, w_up, w_down, qv_bias, up_bias, patches, vec_params):
    ext = 3 * SEQ
    vmem, hbm = pl.BlockSpec(memory_space=pltpu.VMEM), pl.BlockSpec(memory_space=pl.ANY)
    return pl.pallas_call(
        forward_kernel,
        out_shape=[
            sds((2, 3, 256, 512), BF), sds((2, 256, 512), BF), sds((2, 512, 1024), BF),
            sds((2, 1024, 512), BF), sds((2, 8, 1024), F32),
            sds((512, ext), BF), sds((512, ext), BF), sds((512, ext), BF), sds((ext, 512), BF),
            sds((ext, 512), BF), sds((512, ext), BF), sds((3, 4, 8, SEQ), F32),
        ],
        in_specs=[pl.BlockSpec(memory_space=pltpu.SMEM), vmem, hbm, hbm, hbm, vmem, vmem, hbm, vmem],
        out_specs=[hbm] * 12,
        scratch_shapes=[
            pltpu.VMEM((2, 3, 256, 512), BF), pltpu.VMEM((256, 512), BF), pltpu.VMEM((512, 1024), BF),
            pltpu.VMEM((1024, 512), BF), pltpu.VMEM((2, 8, 1024), F32), pltpu.VMEM((HALF, 512), BF),
            pltpu.VMEM((ext, 512), BF), pltpu.VMEM((512, ext), BF), pltpu.VMEM((512, ext), BF),
            pltpu.VMEM((512, ext), BF), pltpu.VMEM((512, SEQ), BF), pltpu.VMEM((ext, 512), BF),
            pltpu.VMEM((ext, 512), BF), pltpu.VMEM((512, ext), BF), pltpu.VMEM((3, 4, 8, SEQ), F32),
            pltpu.VMEM((3, SEQ, 128), BF), pltpu.VMEM((2, SEQ, SEQ), F32),
            pltpu.VMEM((256, 512), F32), pltpu.VMEM((512, 1024), F32), pltpu.VMEM((1024, 512), F32),
            pltpu.VMEM(patches.shape, BF), pltpu.SemaphoreType.DMA((34,)), pltpu.SemaphoreType.DMA((34,)),
            pltpu.SemaphoreType.DMA((40,)), pltpu.SemaphoreType.DMA((4,)),
        ],
        compiler_params=pltpu.CompilerParams(
            collective_id=0, has_side_effects=True, vmem_limit_bytes=VMEM_LIMIT
        ),
        name="forward",
    )(key_count, w_qkv, w_proj, w_up, w_down, qv_bias, up_bias, patches, vec_params)


def mlp_kernel(
    x_ref, dy_ref, ot_ref, wp_ref, wu_in, wd_in, vec_ref, small_ref,
    act_ref, dres_ref, dot_ref, own_out, fore_out, gp_ref, vsum_ref, bsum_ref,
    res_ref, n2_ref, out_ref, dn_ref, hid_ref, dup_ref, dyc_ref, br_ref,
    g_ref, fore_ref, fore_core, own_core, own_peer, wu_ref, wd_ref, send_sem, recv_sem, input_sem,
):
    step = pl.program_id(0)
    dp, mp = lax.axis_index("dp"), lax.axis_index("mp")
    peer, core, core_bit = 1 - mp, partners(dp)[0], lax.rem(dp, 2)
    side, part = jnp.where(step < 2, peer, mp), lax.rem(step, 2)
    sent = Transfers(send_sem, recv_sem)
    kept = pl.ds(pl.multiple_of(core_bit * HALF, HALF), HALF)
    away = pl.ds(pl.multiple_of(HALF - core_bit * HALF, HALF), HALF)
    for turn in range(2):
        sent.plan(
            ("F", turn), lambda turn=turn: g_ref.at[turn, :, away, :], lambda turn=turn: fore_core.at[turn],
            {"dp": core},
        )
        sent.plan(
            ("O", turn), lambda turn=turn: g_ref.at[2 + turn, :, away, :],
            lambda turn=turn: own_core.at[turn], {"dp": core},
        )
    sent.plan("peer", lambda: fore_ref, lambda: own_peer, {"mp": peer})
    gain, shift = vec_ref[2:3, :], vec_ref[3:4, :]
    w_proj = wp_ref[...].reshape(512, 512)

    def rows(index):
        return pl.ds(pl.multiple_of(index * HALF, HALF), HALF)

    inputs = Loads(input_sem)
    for turn in range(4):
        at, columns = (peer, mp)[turn // 2], slice(turn % 2 * 512, turn % 2 * 512 + 512)
        inputs.plan(
            ("up", turn), lambda at=at, columns=columns: wu_in.at[at, :, columns],
            lambda at=at, columns=columns: wu_ref.at[at, :, columns],
        )
        inputs.plan(
            ("down", turn), lambda at=at, columns=columns: wd_in.at[at, columns, :],
            lambda at=at, columns=columns: wd_ref.at[at, columns, :],
        )

    @pl.when(step == 0)
    def _():
        for turn in range(4):
            inputs.start(("up", turn))
            inputs.start(("down", turn))
        greet([{"dp": core}, {"mp": peer}])

        def body(index, carry):
            x_rows = x_ref[pl.ds(row_block(index, mp), HALF), :].astype(F32)
            mixed = ot_ref[:, pl.ds(ext_cols(index), HALF)]
            resid = x_rows + mm_tn(mixed, w_proj) + vec_ref[4:5, :]
            res_ref[rows(index), :] = resid
            n2_ref[rows(index), :] = layer_norm_rows(resid, gain, shift)[0].astype(BF)
            out_ref[rows(index), :] = resid + vec_ref[5:6, :]
            dn_ref[rows(index), :] = jnp.zeros((HALF, 512), F32)
            dyc_ref[rows(index), :] = dy_ref[pl.ds(row_block(index, mp), HALF), :]
            return carry

        lax.fori_loop(0, 5, body, 0, unroll=True)

    for turn in range(4):

        @pl.when(step == turn)
        def _():
            inputs.wait(("up", turn))
            inputs.wait(("down", turn))

    lanes = pl.ds(pl.multiple_of(part * 512, 512), 512)
    w_up, w_down = wu_ref[side, :, lanes], wd_ref[side, lanes, :]
    up_bias = small_ref[side, 0:1, lanes]

    def up_of(index):
        return mm_nn(n2_ref[index * HALF : index * HALF + HALF, :], w_up) + up_bias

    total = jnp.zeros((8, 512), F32)
    pre = up_of(0)
    for index in range(5):
        at = slice(index * HALF, index * HALF + HALF)
        up_pre = pre
        if index < 4:
            pre = up_of(index + 1)
        dhid = mm_nt(dyc_ref[at, :], w_down)
        cumulative = 0.5 * (1.0 + lax.erf(up_pre * (0.5**0.5)))
        density = jnp.exp(-0.5 * up_pre * up_pre) * 0.3989422804014327
        hidden = (up_pre * cumulative).astype(BF)
        hid_ref[at, :] = hidden
        slope = cumulative + up_pre * density
        dup = (dhid * slope).astype(BF)
        dup_ref[at, :] = dup
        total = total + jnp.sum(dup.astype(F32).reshape(HALF // 8, 8, 512), axis=0)
        out_ref[at, :] += mm_nn(hidden, w_down)
        dn_ref[at, :] += mm_nt(dup, w_up)
        if index == 1:

            @pl.when(step == 1)
            def _():
                sent.arrive(("F", 0))
                fore_ref[...] = g_ref[0, :, kept, :] + fore_core[0]
                sent.start("peer")

            @pl.when(step == 2)
            def _():
                sent.arrive(("F", 1))
                fore_out[...] = g_ref[1, :, kept, :] + fore_core[1]

    bsum_ref[2 * side + part] = total
    g_ref[step, 0] = mm_tn(hid_ref[...], dyc_ref[...]).astype(BF)
    g_ref[step, 1] = mm_tn(n2_ref[...], dup_ref[...]).astype(BF)
    for turn, key in enumerate((("F", 0), ("F", 1), ("O", 0), ("O", 1))):

        @pl.when(step == turn)
        def _():
            sent.start(key)

    @pl.when(step == 3)
    def _():
        vsum_ref[...] = jnp.zeros_like(vsum_ref)

        def body(index, carry):
            at = rows(index)
            act_ref[pl.ds(row_block(index, mp), HALF), :] = out_ref[at, :].astype(BF)
            _, unit, inverse = layer_norm_rows(res_ref[at, :], gain, shift)
            dn = dn_ref[at, :]
            dy = dyc_ref[at, :].astype(F32)
            dres = dy + layer_norm_back(dn, unit, inverse, gain)
            dres_ref[at, :] = dres
            branch = dres.astype(BF)
            br_ref[at, :] = branch
            dot_ref[:, pl.ds(ext_cols(index), HALF)] = mm_nt(w_proj, branch).astype(BF)
            sums = [dn * unit, dn, branch.astype(F32), dy]
            for place, value in enumerate(sums):
                vsum_ref[place] += jnp.sum(value.reshape(HALF // 8, 8, 512), axis=0)
            return carry

        lax.fori_loop(0, 5, body, 0, unroll=True)
        mixed = jnp.concatenate([ot_ref[:, 0:HALF], ot_ref[:, SEQ:]], axis=1)
        gp_ref[...] = mm_nn(mixed, br_ref[...]).astype(BF).reshape(2, 256, 512)
        sent.arrive(("O", 0))
        sent.arrive(("O", 1))
        sent.arrive("peer")
        near = g_ref[2, :, kept, :].astype(F32) + own_core[0].astype(F32)
        own_out[0] = (near + own_peer[...].astype(F32)).astype(BF)
        own_out[1] = g_ref[3, :, kept, :] + own_core[1]
        sent.finish()


def mlp(patches, cotangent, ot, wp, wu, wd, vec_params, small):
    rows = patches.shape[0]
    ext = 3 * SEQ
    hbm = pl.BlockSpec(memory_space=pl.ANY)
    return pl.pallas_call(
        mlp_kernel,
        grid=(4,),
        out_shape=[
            sds((rows, 512), BF), sds((rows, 512), F32), sds((512, ext), BF), sds((2, 2, HALF, 512), BF),
            sds((2, HALF, 512), BF), sds((2, 256, 512), BF), sds((4, 8, 512), F32), sds((4, 8, 512), F32),
        ],
        in_specs=[
            full_spec((rows, 512)), full_spec((rows, 512)), full_spec((512, ext)), full_spec(wp.shape),
            hbm, hbm, full_spec(vec_params.shape), full_spec(small.shape),
        ],
        out_specs=[
            full_spec((rows, 512)), full_spec((rows, 512)), full_spec((512, ext)),
            full_spec((2, 2, HALF, 512)), full_spec((2, HALF, 512)),
            full_spec((2, 256, 512)), full_spec((4, 8, 512)), full_spec((4, 8, 512)),
        ],
        scratch_shapes=[
            pltpu.VMEM((rows, 512), F32), pltpu.VMEM((rows, 512), BF), pltpu.VMEM((rows, 512), F32),
            pltpu.VMEM((rows, 512), F32), pltpu.VMEM((rows, 512), BF), pltpu.VMEM((rows, 512), BF),
            pltpu.VMEM((rows, 512), BF), pltpu.VMEM((rows, 512), BF), pltpu.VMEM((4, 2, 512, 512), BF),
            pltpu.VMEM((2, HALF, 512), BF), pltpu.VMEM((2, 2, HALF, 512), BF),
            pltpu.VMEM((2, 2, HALF, 512), BF), pltpu.VMEM((2, HALF, 512), BF),
            pltpu.VMEM(wu.shape, BF), pltpu.VMEM(wd.shape, BF), pltpu.SemaphoreType.DMA((5,)),
            pltpu.SemaphoreType.DMA((5,)), pltpu.SemaphoreType.DMA((8,)),
        ],
        compiler_params=pltpu.CompilerParams(
            collective_id=2, has_side_effects=True, vmem_limit_bytes=VMEM_LIMIT
        ),
        name="mlp",
    )(patches, cotangent, ot, wp, wu, wd, vec_params, small)


SCHEDULE = (
    (
        ("F", 2, 1), ("F", 4, 0), ("O", 0, 1), ("O", 1, 1), ("O", 4, 0),
    ),
    (
    ),
    (
        ("F", 3, 1),
    ),
    (
        ("O", 0, 2),
    ),
    (
        ("O", 1, 2), ("O", 2, 1),
    ),
    (
        ("F", 4, 1),
    ),
    (
    ),
    (
        ("O", 0, 3),
    ),
    (
        ("F", 5, 0), ("O", 1, 3), ("O", 3, 1),
    ),
    (
        ("F", 5, 1), ("O", 4, 1),
    ),
    (
        ("O", 2, 2),
    ),
    (
        ("O", 0, 4),
    ),
    (
        ("F", 6, 0), ("O", 1, 4), ("O", 3, 2),
    ),
    (
        ("F", 6, 1), ("O", 4, 2),
    ),
    (
        ("O", 0, 5), ("O", 2, 3),
    ),
    (
        ("O", 0, 6),
    ),
    (
        ("O", 1, 5), ("O", 3, 3), ("O", 5, 0),
    ),
    (
        ("O", 1, 6),
    ),
    (
        ("O", 4, 3),
    ),
    (
        ("O", 2, 4), ("O", 5, 1),
    ),
    (
        ("O", 6, 0),
    ),
    (
        ("O", 3, 4),
    ),
    (
        ("O", 6, 1),
    ),
    (
        ("O", 2, 5), ("O", 4, 4),
    ),
    (
        ("O", 2, 6),
    ),
    (
        ("O", 3, 5), ("O", 5, 3),
    ),
    (
        ("O", 4, 5), ("O", 3, 6), ("small", 0), ("O", 4, 6), ("O", 6, 3), ("square", 0), ("square", 1),
        ("small", 1), ("small", 2), ("O", 5, 5), ("square", 2), ("O", 5, 6), ("O", 6, 5), ("O", 6, 6),
    ),
)


def cut(ref, start, size):
    rows = pl.ds(pl.multiple_of(start, 16), size)
    return ref.at[:, rows, :] if len(ref.shape) == 3 else ref.at[rows, :]


WIDE = (5, 6)
PIECES = ((512, 512), (512, 512), (512, 512), (512, 512), (256, 512), (3, 512, 128), (3, 512, 128))


def piece_rows(index, size):
    return (*PIECES[index][:-2], PIECES[index][-2] // size, PIECES[index][-1])


def backward_kernel(
    count_ref, qt_in, kt_in, dot_in, ot_in, k_in, v_in, lse_ref, nt_in, wt_in,
    own_in, fore_in, gp_in, x_in, dres_in, vec_ref, two_ref, up_sum_ref,
    grad_out, down_out, up_out, proj_out, qkv_out, small_out, norm_out,
    qt_ref, kt_ref, dot_ref, ot_ref, k_ref, v_ref, nt_ref, wt_ref, x_ref, dres_ref, grad_ref,
    shared_ref, grads_ref, bias_ref, s_ref, dp_ref, g_ref, bsum_ref,
    far_send, far_recv, early_core, early_part, early_all, late_core, late_part, late_all, square_sum, square_core, square_all, *rest,
):
    buffers, (send_sem, recv_sem, local_sem) = rest[:-3], rest[-3:]
    dp, mp = lax.axis_index("dp"), lax.axis_index("mp")
    peer = 1 - mp
    core, x_side, _, _ = partners(dp)
    to_core, to_peer, to_x = {"dp": core}, {"mp": peer}, {"dp": x_side}
    core_bit, x_bit = lax.rem(dp, 2), lax.rem(lax.div(dp, 2), 2)
    chip, floor = lax.div(dp, 2), lax.div(dp, 4)

    def ring(index):
        return (chip, 8, 2) if index in WIDE else (floor, 4, 4)
    sent, loads = Transfers(send_sem, recv_sem), Loads(local_sem)

    def block_at(place):
        return 2 * jnp.where(place < 2, peer, mp) + lax.rem(place, 2)

    def source(index, side):
        if index == 4:
            return gp_in.at[side]
        return g_ref.at[index - 5 + (0 if side is peer else 2)]

    def result(index):
        if index < 4:
            lanes = slice(index // 2 * 512, index // 2 * 512 + 512)
            return up_out.at[:, lanes] if index % 2 else down_out.at[lanes, :]
        if index == 4:
            return proj_out
        return qkv_out.at[:, :, slice((index - 5) * 128, (index - 5) * 128 + 128)]

    def piece_buffers(index):
        return buffers[8 * index : 8 * index + 8]

    def region(index):
        half = PIECES[index][-2] // 2
        if index in WIDE:
            return core_bit * half, half
        return core_bit * half + x_bit * (half // 2), half // 2

    names = ("qt", "kt", "dot", "ot", "k", "v")
    sources = (qt_in, kt_in, dot_in, ot_in, k_in, v_in)
    homes = (qt_ref, kt_ref, dot_ref, ot_ref, k_ref, v_ref)
    for place in range(4):
        rows = pl.ds(pl.multiple_of(block_at(place) * 128, 128), 128)
        for name, src, dst in zip(names, sources, homes):
            loads.plan(
                (name, place),
                lambda src=src, rows=rows: src.at[rows, :] if src.shape[0] == 512 else src.at[:, rows],
                lambda dst=dst, place=place: dst.at[place],
            )

    def load_block(place):
        for name in names:
            loads.start((name, place))

    def loaded(place):
        for name in names:
            loads.wait((name, place))

    load_block(0)
    loads.start("wt", lambda: wt_in, lambda: wt_ref)
    for index in range(4):
        loads.plan(
            ("kept", index, 2), lambda index=index: own_in.at[index // 2, index % 2],
            lambda index=index: piece_buffers(index)[2],
        )
        if index > 1:
            loads.plan(
                ("kept", index, 0), lambda index=index: fore_in.at[index % 2],
                lambda index=index: piece_buffers(index)[0],
            )
    half = PIECES[4][-2] // 2
    for side, slot in ((peer, 0), (mp, 2)):
        loads.plan(
            ("kept", 4, slot), lambda side=side: cut(source(4, side), core_bit * half, half),
            lambda slot=slot: piece_buffers(4)[slot],
        )
    for key in ((2, 0), (0, 2), (1, 2), (3, 0), (2, 2), (3, 2), (4, 0), (4, 2)):
        loads.start(("kept", *key))
    loads.plan("nt", lambda: nt_in, lambda: nt_ref)
    loads.plan("x", lambda: x_in, lambda: x_ref)
    loads.plan("dres", lambda: dres_in, lambda: dres_ref)
    chips = [
        {"dp": lax.rem(dp + 2 * step, 16), "mp": side} for side in (mp, peer) for step in range(8)
    ][1:]
    greet([to_core] + chips)

    def plan_piece(index):
        total = PIECES[index][-2]
        half = total // 2
        kept = core_bit * half
        fore, fore_core, own, own_core, own_peer, own_x, landing, out = piece_buffers(index)
        away = (1 - core_bit) * half
        if index > 1:
            sent.plan(("F", index, 1), lambda: fore, lambda: own_peer, to_peer)
        if index > 3:
            sent.plan(("F", index, 0), lambda: cut(source(index, peer), away, half), lambda: fore_core, to_core)
            sent.plan(("O", index, 0), lambda: cut(source(index, mp), away, half), lambda: own_core, to_core)
        if index not in WIDE:
            other_x = (1 - x_bit) * (half // 2)
            sent.plan(("O", index, 1), lambda: cut(own, other_x, half // 2), lambda: own_x, to_x)
        first, size = region(index)
        me, members, stride = ring(index)
        size //= members
        for step in range(1, members):
            target = {"dp": lax.rem(dp + stride * step, 16)}
            their = lax.rem(me + step, members) * size + first
            mine = me * size + first
            sent.plan(
                ("O", index, 2, step), lambda their=their: cut(own, their - kept, size),
                lambda step=step: landing.at[step - 1], target,
            )
            place = lambda mine=mine: cut(out, mine, size)
            sent.plan(("O", index, 3, step), place, place, target)
        if index not in WIDE:
            across = lambda: cut(out, region(index)[0], half // 2)
            sent.plan(("O", index, 4), across, across, to_x)
        whole = lambda: cut(out, kept, half)
        sent.plan(("O", index, 5), whole, whole, to_core)
        loads.plan(("out", index), lambda: out, lambda: result(index))

    def event(kind, index, stage):
        total = PIECES[index][-2]
        half = total // 2
        kept = core_bit * half
        wide = index in WIDE
        fore, fore_core, own, own_core, own_peer, own_x, landing, out = piece_buffers(index)
        first, size = region(index)
        me, members, _ = ring(index)
        size //= members

        def each(stage, call):
            for step in range(1, members):
                call(("O", index, stage, step))

        if stage == 0:
            sent.start((kind, index, 0))
        elif kind == "F":
            if index > 3:
                sent.arrive((kind, index, 0))
            if index < 4:
                loads.wait(("kept", index, 0))
            elif index < 5:
                loads.wait(("kept", index, 0))
                fore[...] += fore_core[...]
            else:
                fore[...] = cut(source(index, peer), kept, half)[...] + fore_core[...]
            sent.start((kind, index, 1))
        elif stage == 1:
            if index > 3:
                sent.arrive((kind, index, 0))
            if index > 1:
                sent.arrive(("F", index, 1))
            if index < 5:
                loads.wait(("kept", index, 2))
            if index > 1:
                base = (own if index < 5 else cut(source(index, mp), kept, half))[...].astype(F32)
                if index > 3:
                    base = base + own_core[...].astype(F32)
                own[...] = (base + own_peer[...].astype(F32)).astype(BF)
            if wide:
                each(2, sent.start)
            else:
                sent.start((kind, index, 1))
        elif stage == 2:
            sent.arrive((kind, index, 1))
            at = x_bit * (half // 2)
            cut(own, at, half // 2)[...] += own_x[...]
            each(2, sent.start)
        elif stage == 3:
            each(2, sent.arrive)
            value = cut(own, first - kept + me * size, size)[...].astype(F32)
            for step in range(members - 1):
                value = value + landing[step].astype(F32)
            value = value.astype(BF)
            cut(out, first + me * size, size)[...] = value
            each(3, sent.start)
            squared = value.astype(F32)
            square = jnp.sum((squared * squared).reshape(-1, 8, squared.shape[-1]), axis=0)
            folded = square[:, 0:128]
            for lane in range(1, square.shape[1] // 128):
                folded = folded + square[:, lane * 128 : lane * 128 + 128]
            square_sum[...] += folded
        elif stage == 4:
            each(3, sent.arrive)
            sent.start((kind, index, 4))
        elif stage == 5:
            if wide:
                each(3, sent.arrive)
            else:
                sent.arrive((kind, index, 4))
            sent.start((kind, index, 5))
        else:
            sent.arrive((kind, index, 5))
            loads.start(("out", index))

    for index in range(7):
        plan_piece(index)

    me = mp * 8 + chip
    rows_mine = pl.ds(pl.multiple_of(core_bit * 8, 8), 8)
    rows_other = pl.ds(pl.multiple_of(8 - core_bit * 8, 8), 8)
    sums_of = {"early": (early_core, early_part, early_all), "late": (late_core, late_part, late_all)}
    sent.plan("square core", lambda: square_sum, lambda: square_core, to_core)
    for name, (both, part, everyone) in sums_of.items():
        sent.plan(
            (name, "core"), lambda both=both: both.at[0, rows_other],
            lambda both=both: both.at[1, rows_other], to_core,
        )
        back = lambda part=part: part.at[rows_mine]
        sent.plan((name, "back"), back, back, to_core)
        for place, target in enumerate(chips):
            slot = lambda everyone=everyone: everyone.at[me]
            sent.plan((name, place), slot, slot, target)
    for place, target in enumerate(chips):
        sent.plan(("square", place), lambda: square_all.at[me], lambda: square_all.at[me], target)

    def everywhere(name, call):
        for place in range(len(chips)):
            call((name, place))

    def spread(name, stage):
        both, part, everyone = sums_of[name]
        if stage == 0:
            sent.arrive((name, "core"))
            everyone[me] = both[0, rows_mine] + both[1, rows_mine]
            everywhere(name, sent.start)
        elif stage == 1:
            everywhere(name, sent.arrive)
            part[rows_mine] = jnp.sum(everyone[...], axis=0)
            sent.start((name, "back"))
        else:
            sent.arrive((name, "back"))

    for row in range(8):
        value = jnp.sum(up_sum_ref[row] if row < 4 else two_ref[row - 4], axis=0, keepdims=True)
        early_core[0, row : row + 1, :] = value[:, 0:256]
        early_core[0, 8 + row : 9 + row, :] = value[:, 256:512]

    def run(events):
        for item in events:
            event(*item)

    square_sum[...] = jnp.zeros((8, 128), F32)
    bias_ref[0] = key_bias((SEQ, 128), mp, count_ref[2], True)
    for group in (1, 2):
        bias_ref[group] = key_bias((SEQ, 128), mp, count_ref[3 * mp + group - 1], False)
    sent.start(("early", "core"))
    run(SCHEDULE[0])

    def tiles(place, group, queries, sub):
        base = pl.multiple_of(group * SEQ, SEQ)
        keys_at, queries_at = pl.ds(base, SEQ), pl.ds(base, queries)
        own = slice(sub * HD, sub * HD + HD)
        s_ref[sub % 2, :, :queries] = score_tile(
            k_ref[place, keys_at, :], bias_ref[group], qt_ref[place, own, queries_at], sub
        )
        dp_ref[sub % 2, :, :queries] = mm_nn(
            v_ref[place, keys_at, :], widen_plain(dot_ref[place, own, queries_at], sub)
        )

    def heads(place, group, queries, out, out_base, following, between):
        block = block_at(place)
        base = pl.multiple_of(group * SEQ, SEQ)
        keys_at, queries_at = pl.ds(base, SEQ), pl.ds(base, queries)
        out_keys = pl.ds(out_base, SEQ)
        out_queries = pl.ds(out_base, queries)
        for sub in range(4):
            if sub < 3:
                tiles(place, group, queries, sub + 1)
            else:
                tiles(*following, queries, 0)
            own = slice(sub * HD, sub * HD + HD)
            q_rows, do_rows = qt_ref[place, own, queries_at], dot_ref[place, own, queries_at]
            delta = jnp.sum(
                do_rows.astype(F32) * ot_ref[place, own, queries_at].astype(F32), axis=0, keepdims=True
            )
            probs = jnp.exp2(
                s_ref[sub % 2, :, :queries] - lse_ref[group, block, sub : sub + 1, :queries]
            )
            draw = (probs * (dp_ref[sub % 2, :, :queries] - delta)).astype(BF)
            dq = mm_nn(kt_ref[place, own, keys_at], draw) * (HD ** (-0.5))
            out[own, out_queries] = dq.astype(BF)
            dk = mm_nt(q_rows, draw) * (1.0 / LOG2E)
            out[128 + sub * HD : 160 + sub * HD, out_keys] = dk.astype(BF)
            dv = mm_nt(do_rows, probs.astype(BF))
            out[256 + sub * HD : 288 + sub * HD, out_keys] = dv.astype(BF)
            if sub == 1:
                between()

    def weights_of(place):
        block = block_at(place)
        side, part = lax.div(block, 2), lax.rem(block, 2)
        return wt_ref[side, :, pl.ds(pl.multiple_of(part * 128, 128), 128), :].reshape(384, 512)

    for place in range(4):
        shared_ref[place, 0:128, HALF:SEQ] = jnp.zeros((128, HALF), BF)

    loaded(0)
    load_block(1)
    loads.wait("wt")

    def shared_step(place, carry):
        for turn in range(3):

            @pl.when(place == turn)
            def _():
                loaded(turn + 1)
                if turn < 2:
                    load_block(turn + 2)
                else:
                    loads.start("nt")
                    loads.start("x")
                    loads.start("dres")

        heads(place, 0, HALF, shared_ref.at[place], 0, (jnp.minimum(place + 1, 3), 0), lambda: None)
        for turn in range(4):

            @pl.when(place == turn)
            def _():
                run(SCHEDULE[1 + turn])
                if turn == 0:
                    spread("early", 0)
                elif turn == 3:
                    spread("early", 1)

        return carry

    tiles(0, 0, HALF, 0)
    lax.fori_loop(0, 4, shared_step, 0)
    tiles(0, 1, SEQ, 0)
    def rows_grad(grads, columns):
        total = mm_tn(grads[0, :, columns], weights_of(0))
        for place in range(1, 4):
            total += mm_tn(grads[place, :, columns], weights_of(place))
        return total

    far_send[...] = rows_grad(shared_ref, slice(HALF, SEQ)).astype(BF)
    spread("early", 2)
    sent.start("far", lambda: far_send, lambda: far_recv, to_peer)
    loads.wait("nt")

    def main_step(step, carry):
        place, group = lax.div(step, 2), 1 + lax.rem(step, 2)

        def pump(first):
            for turn in range(8):

                @pl.when(step == turn)
                def _():
                    run(SCHEDULE[first + 2 * turn])

        out_base = pl.multiple_of((group - 1) * SEQ, SEQ)
        after = jnp.minimum(step + 1, 7)
        following = (lax.div(after, 2), 1 + lax.rem(after, 2))
        heads(place, group, SEQ, grads_ref.at[place], out_base, following, lambda: pump(5))

        @pl.when(group == 2)
        def _():
            for part in range(3):
                rows = slice(part * 128, part * 128 + 128)
                total = mm_nt(nt_ref[:, 0:SEQ], shared_ref[place, rows, :])
                total += mm_nt(nt_ref[:, SEQ:], grads_ref[place, rows, :])
                g_ref[place, part] = total.astype(BF)
            ones = jnp.ones((8, 2 * SEQ), BF)
            bsum_ref[place] = mm_nt(ones[:, :SEQ], shared_ref[place]) + mm_nt(ones, grads_ref[place])

        pump(6)
        return carry

    lax.fori_loop(0, 8, main_step, 0)

    gain, shift = vec_ref[0:1, :], vec_ref[1:2, :]
    loads.wait("x")
    loads.wait("dres")
    run(SCHEDULE[21])

    for index in range(5):
        where = pl.ds(row_block(index, mp), HALF)
        loads.plan(
            ("grad", index), lambda where=where: grad_ref.at[where, :],
            lambda where=where: grad_out.at[where, :],
        )

    def finish_rows(index, dn, sums):
        at = pl.ds(pl.multiple_of(index * HALF, HALF), HALF)
        place = pl.ds(row_block(index, mp), HALF)
        _, unit, inverse = layer_norm_rows(x_ref[place, :].astype(F32), gain, shift)
        grad_ref[place, :] = dres_ref[at, :] + layer_norm_back(dn, unit, inverse, gain)
        folded = [jnp.sum(value.reshape(HALF // 8, 8, 512), axis=0) for value in (dn * unit, dn)]
        return sums[0] + folded[0], sums[1] + folded[1]

    def finish_step(index, sums):
        columns = pl.ds(pl.multiple_of(HALF * index - HALF, HALF), HALF)
        sums = finish_rows(index, rows_grad(grads_ref, columns), sums)
        for turn in range(1, 5):

            @pl.when(index == turn)
            def _():
                loads.start(("grad", turn))
                run(SCHEDULE[21 + turn])

        return sums

    zero = jnp.zeros((8, 512), F32)
    sums = lax.fori_loop(1, 5, finish_step, (zero, zero))
    sent.arrive("far")
    sums = finish_rows(0, rows_grad(shared_ref, slice(0, HALF)) + far_recv[...].astype(F32), sums)
    loads.start(("grad", 0))

    for place in range(4):
        lanes = slice(place * 128, place * 128 + 128)
        for row, value in enumerate((sums[0], sums[1])):
            late_core[0, 8 + 4 * row + place : 9 + 4 * row + place, :] = jnp.sum(
                value[:, lanes], axis=0, keepdims=True
            )
        for row, columns in enumerate((slice(0, 128), slice(256, 384))):
            late_core[0, 4 * row + place : 4 * row + place + 1, :] = jnp.where(
                mp == 0, bsum_ref[(place + 2) % 4, 0:1, columns], bsum_ref[place, 0:1, columns]
            )

    def square_stage(stage):
        if stage == 0:
            sent.start("square core")
        elif stage == 1:
            sent.arrive("square core")
            square_all[me] = square_sum[...] + square_core[...]
            everywhere("square", sent.start)
        else:
            everywhere("square", sent.arrive)
            for row in range(4):
                at = (0, 1, 6, 7)[row]
                for lane in range(4):
                    small_out[at : at + 1, lane * 128 : lane * 128 + 128] = late_part[
                        4 * row + lane : 4 * row + lane + 1, :
                    ]
            for row in range(8):
                at = 2 + row if row < 4 else 4 + row
                small_out[at : at + 1, 0:256] = early_part[row : row + 1, :]
                small_out[at : at + 1, 256:512] = early_part[8 + row : 9 + row, :]
            small_out[12:16, :] = jnp.zeros((4, 512), F32)
            small = small_out[...]
            total = jnp.sum(small * small) + jnp.sum(jnp.sum(square_all[...], axis=0))
            norm_out[...] = jnp.sqrt(jnp.full((8, 128), total, F32))

    sent.start(("late", "core"))
    for item in SCHEDULE[26]:
        if item[0] == "small":
            spread("late", item[1])
        elif item[0] == "square":
            square_stage(item[1])
        else:
            event(*item)
    sent.finish()
    for index in range(7):
        loads.wait(("out", index))
    for index in range(5):
        loads.wait(("grad", index))


def backward(key_count, qt, kt, dot, ot, k, v, lse, nt, wt, owns, fores, gp, patches, dres, vec_params, two, ups):
    ext, rows = 3 * SEQ, patches.shape[0]
    vmem, hbm = pl.BlockSpec(memory_space=pltpu.VMEM), pl.BlockSpec(memory_space=pl.ANY)
    buffers = []
    for index in range(7):
        for size in (2, 2, 2, 2, 2, 4):
            buffers.append(pltpu.VMEM(piece_rows(index, size), BF))
        members = 7 if index in WIDE else 3
        buffers.append(pltpu.VMEM((members, *piece_rows(index, 16)), BF))
        buffers.append(pltpu.VMEM(piece_rows(index, 1), BF))
    return pl.pallas_call(
        backward_kernel,
        out_shape=[
            sds((rows, 512), F32), sds((1024, 512), BF), sds((512, 1024), BF), sds((256, 512), BF),
            sds((3, 512, 256), BF), sds((16, 512), F32), sds((8, 128), F32),
        ],
        in_specs=[pl.BlockSpec(memory_space=pltpu.SMEM)] + [hbm] * 6 + [vmem] + [hbm] * 7 + [vmem] * 3,
        out_specs=[hbm] * 5 + [vmem] * 2,
        scratch_shapes=[
            *[pltpu.VMEM((4, 128, ext), BF)] * 4, *[pltpu.VMEM((4, ext, 128), BF)] * 2,
            pltpu.VMEM((512, ext), BF), pltpu.VMEM((2, 3, 256, 512), BF), pltpu.VMEM((rows, 512), BF),
            pltpu.VMEM((rows, 512), F32), pltpu.VMEM((rows, 512), F32), pltpu.VMEM((4, 384, SEQ), BF), pltpu.VMEM((4, 384, 2 * SEQ), BF),
            pltpu.VMEM((3, SEQ, 128), BF), pltpu.VMEM((2, SEQ, SEQ), F32),
            pltpu.VMEM((2, SEQ, SEQ), F32), pltpu.VMEM((4, 3, 512, 128), BF), pltpu.VMEM((4, 8, 384), F32),
            pltpu.VMEM((HALF, 512), BF), pltpu.VMEM((HALF, 512), BF), pltpu.VMEM((2, 16, 256), F32),
            pltpu.VMEM((16, 256), F32), pltpu.VMEM((16, 8, 256), F32), pltpu.VMEM((2, 16, 128), F32),
            pltpu.VMEM((16, 128), F32), pltpu.VMEM((16, 8, 128), F32), pltpu.VMEM((8, 128), F32),
            pltpu.VMEM((8, 128), F32), pltpu.VMEM((16, 8, 128), F32), *buffers,
            pltpu.SemaphoreType.DMA((137,)), pltpu.SemaphoreType.DMA((137,)), pltpu.SemaphoreType.DMA((48,)),
        ],
        compiler_params=pltpu.CompilerParams(
            collective_id=1, has_side_effects=True, vmem_limit_bytes=VMEM_LIMIT
        ),
        name="backward",
    )(key_count, qt, kt, dot, ot, k, v, lse, nt, wt, owns, fores, gp, patches, dres, vec_params, two, ups)


ADAM_STEPS = 4


def adam_step(weight, gradient, moment_one, moment_two, step_rate, decay_rate):
    first_new = BETA_FIRST * moment_one + (1.0 - BETA_FIRST) * gradient
    second_new = BETA_SECOND * moment_two + (1.0 - BETA_SECOND) * gradient * gradient
    root = jnp.sqrt(second_new * (1.0 / (1.0 - BETA_SECOND**ADAM_STEP))) + ADAM_EPS
    change = first_new * (step_rate / (1.0 - BETA_FIRST**ADAM_STEP)) / root
    return weight * (1.0 - step_rate * decay_rate) - change, first_new, second_new


def adam_kernel(norm_ref, small_ref, *refs):
    mp = lax.axis_index("mp")
    factor = jnp.minimum(1.0, CLIP_NORM / (norm_ref[0:1, 0:1] + 1e-06))
    vectors, refs = refs[:9], refs[9:]
    matrices, refs = refs[:16], refs[16:]
    results, vector_results, norm_out = refs[:12], refs[12:21], refs[21]
    for index in range(4):
        weight_ref, one_ref, two_ref, grad_ref = matrices[4 * index : 4 * index + 4]
        values = adam_step(
            weight_ref[...], grad_ref[...].astype(F32) * factor, one_ref[...], two_ref[...],
            MATRIX_RATE, DECAY_RATE,
        )
        for out, value in zip(results[3 * index : 3 * index + 3], values):
            out[...] = value

    @pl.when(pl.program_id(0) == 0)
    def _():
        norm_out[...] = norm_ref[0:1, 0:1]
        first = mp == 0
        qv = jnp.where(first, small_ref[0:2, 0:256], small_ref[0:2, 256:512])
        up = jnp.where(first, small_ref[2:4, :], small_ref[4:6, :])
        up = jnp.concatenate(
            [up[row : row + 1, lane * 128 : lane * 128 + 128] for row in range(2) for lane in range(4)], axis=0
        )
        for index, total in enumerate((qv, up, small_ref[6:12, :])):
            weight_ref, one_ref, two_ref = vectors[3 * index : 3 * index + 3]
            values = adam_step(
                weight_ref[...], total * factor, one_ref[...], two_ref[...], VECTOR_RATE, 0.0
            )
            for out, value in zip(vector_results[3 * index : 3 * index + 3], values):
                out[...] = value


def adam_all(norm, small, vectors, groups):
    steps = ADAM_STEPS
    in_specs, out_specs, out_shape = [full_spec((8, 128)), full_spec(small.shape)], [], []
    args = [norm, small]
    for vector in vectors:
        in_specs += [full_spec(array.shape) for array in vector]
        args += list(vector)
    for group in groups:
        rows, width = group[0].shape
        spec = pl.BlockSpec((rows // steps, width), lambda i: (i, 0))
        in_specs += [spec] * 4
        out_specs += [spec] * 3
        out_shape += [sds((rows, width), F32)] * 3
        args += list(group)
    for vector in vectors:
        out_specs += [full_spec(array.shape) for array in vector]
        out_shape += [sds(array.shape, F32) for array in vector]
    return pl.pallas_call(
        adam_kernel,
        grid=(steps,),
        out_shape=out_shape + [sds((1, 1), F32)],
        in_specs=in_specs,
        out_specs=out_specs + [full_spec((1, 1))],
        compiler_params=pltpu.CompilerParams(vmem_limit_bytes=VMEM_LIMIT),
        name="adam_all",
    )(*args)


IN_SPECS = (
            P(("dp", "mp"), None),
            P(("dp", "mp"), None),
            P("dp"),
            P(None, None, "mp"),
            P("mp", None),
            P(None, "mp"),
            P("mp", None),
            P(None, "mp"),
            P("mp"),
            P(),
            P(None, None, "mp"),
            P(None, None, "mp"),
            P("mp", None),
            P("mp", None),
            P(None, "mp"),
            P(None, "mp"),
            P("mp", None),
            P("mp", None),
            P(None, "mp"),
            P(None, "mp"),
            P("mp"),
            P("mp"),
            P(),
            P(),
        )
OUT_SPECS = (
            P(("dp", "mp"), None),
            P(("dp", "mp"), None),
            P(),
            P(None, None, "mp"),
            P(None, None, "mp"),
            P(None, None, "mp"),
            P("mp", None),
            P("mp", None),
            P("mp", None),
            P(None, "mp"),
            P(None, "mp"),
            P(None, "mp"),
            P("mp", None),
            P("mp", None),
            P("mp", None),
            P(None, "mp"),
            P(None, "mp"),
            P(None, "mp"),
            P("mp"),
            P("mp"),
            P("mp"),
            P(),
            P(),
            P(),
        )


def paired(
    patches, cotangent, key_count, w_qkv, w_proj, w_up, w_down, qv_bias, up_bias, vec_params,
    first_qkv, second_qkv, first_proj, second_proj, first_up, second_up, first_down, second_down,
    first_qv_bias, second_qv_bias, first_up_bias, second_up_bias, first_vec, second_vec,
):
    wt, wp, wu, wd, small_all, nt, qt, kt, k, v, ot, lse = forward(
        key_count, w_qkv, w_proj, w_up, w_down, qv_bias, up_bias.reshape(1, 1024), patches, vec_params
    )
    activations, dres, dot, owns, fores, g_proj, vsum_two, up_sums = mlp(
        patches, cotangent, ot, wp, wu, wd, vec_params, small_all
    )
    input_grad, down, up, proj, qkv, small_total, norm = backward(
        key_count, qt, kt, dot, ot, k, v, lse, nt, wt, owns, fores, g_proj, patches, dres, vec_params,
        vsum_two, up_sums,
    )
    qkv = qkv.reshape(1536, 256)
    flat = lambda array: array.reshape(-1, array.shape[-1])
    groups = [
        (flat(w_qkv), flat(first_qkv), flat(second_qkv), qkv),
        (w_proj, first_proj, second_proj, proj),
        (w_up, first_up, second_up, up),
        (w_down, first_down, second_down, down),
    ]
    square = lambda array: array.reshape(8, 128)
    vectors = [
        (qv_bias, first_qv_bias, second_qv_bias),
        (square(up_bias), square(first_up_bias), square(second_up_bias)),
        (vec_params, first_vec, second_vec),
    ]
    outs = adam_all(norm, small_total, vectors, groups)
    return (
        activations, input_grad, outs[21].reshape(()), *[array.reshape(w_qkv.shape) for array in outs[0:3]],
        *outs[3:12], *outs[12:15], *[array.reshape(up_bias.shape) for array in outs[15:18]], *outs[18:21],
    )


def fits_pairs(mesh, args):
    if dict(mesh.shape) != {"dp": 16, "mp": 2}:
        return False
    return args[0].shape == (40960, 512) and args[2].shape == (80,)


def solution(mesh):
    def run(*args):
        body = paired if fits_pairs(mesh, args) else local
        return jax.shard_map(body, mesh=mesh, in_specs=IN_SPECS, out_specs=OUT_SPECS, check_vma=False)(*args)

    return run
```
